32 devices in a mesh: sp: 4 (over y, x), fsdp: 8 (over z, core).
Axes of the slice: x: 2, y: 2, z: 4, core: 2. Of those that a mesh axis runs over, the one named last changes fastest.
Arguments:
- tokens: bfloat16 [24576, 768], P(('fsdp', 'sp')), may hold values from -6 to 6
- segments: int32 [8, 3072], P('fsdp'), may hold values from 0 to 31, never falling along the last dimension, each value on 1 to 1536 neighbouring positions
- cotangent: bfloat16 [24576, 768], P(('fsdp', 'sp')), may hold values from -6 to 6
- w_qkv: bfloat16 [768, 2304], P(('sp', 'fsdp')), may hold values from -0.3125 to 0.3125
- b_query: bfloat16 [768], P(('sp', 'fsdp')), may hold values from -3 to 3
- b_value: bfloat16 [768], P(('sp', 'fsdp')), may hold values from -3 to 3
- w_out: bfloat16 [768, 768], P(('sp', 'fsdp')), may hold values from -0.625 to 0.625
- b_out: bfloat16 [768], P(('sp', 'fsdp')), may hold values from -2 to 2
- ln1_gain: bfloat16 [768], P(('sp', 'fsdp')), may hold values from 0.5 to 1.5
- ln1_bias: bfloat16 [768], P(('sp', 'fsdp')), may hold values from -2 to 2
- w_up: bfloat16 [768, 3072], P(('sp', 'fsdp')), may hold values from -0.21875 to 0.21875
- b_up: bfloat16 [3072], P(('sp', 'fsdp')), may hold values from -3 to 3
- w_down: bfloat16 [3072, 768], P(('sp', 'fsdp')), may hold values from -0.15625 to 0.15625
- b_down: bfloat16 [768], P(('sp', 'fsdp')), may hold values from -2 to 2
- ln2_gain: bfloat16 [768], P(('sp', 'fsdp')), may hold values from 0.5 to 1.5
- ln2_bias: bfloat16 [768], P(('sp', 'fsdp')), may hold values from -2 to 2
Outputs:
- output: bfloat16 [24576, 768], P(('fsdp', 'sp'))
- grad_input: float32 [24576, 768], P(('fsdp', 'sp'))
- grad_w_qkv: float32 [768, 2304], P(('sp', 'fsdp'))
- grad_b_query: float32 [768], P(('sp', 'fsdp'))
- grad_b_value: float32 [768], P(('sp', 'fsdp'))
- grad_w_out: float32 [768, 768], P(('sp', 'fsdp'))
- grad_b_out: float32 [768], P(('sp', 'fsdp'))
- grad_ln1_gain: float32 [768], P(('sp', 'fsdp'))
- grad_ln1_bias: float32 [768], P(('sp', 'fsdp'))
- grad_w_up: float32 [768, 3072], P(('sp', 'fsdp'))
- grad_b_up: float32 [3072], P(('sp', 'fsdp'))
- grad_w_down: float32 [3072, 768], P(('sp', 'fsdp'))
- grad_b_down: float32 [768], P(('sp', 'fsdp'))
- grad_ln2_gain: float32 [768], P(('sp', 'fsdp'))
- grad_ln2_bias: float32 [768], P(('sp', 'fsdp'))
The draws below stay inside these ranges and needn't reach their ends.
Inputs may be any that keep to these rules, and one draw needn't show every extreme that they name: `segments`: within a sequence the ids never fall; every document has at most 1536 tokens and one document of each sequence has exactly that many.
All inputs are finite; a program needn't handle non-finite values.
Results may differ from the reference program's by a relative error of at most 0.014.
The reference program's roundings to bfloat16 on the way count: a program that leaves them out, or rounds other values in their place, can miss the bound.
Values may be sent and summed in bfloat16 or wider, within the bound.
No kernel may reach another device: no remote copies, remote signals or barrier semaphores. Data moves between devices by JAX's collectives and lax.ppermute only.
A program may use at most 192 MiB of HBM per device.

```python
import math
import jax
import jax.numpy as jnp
import numpy as np
from jax import lax

D = 768
HEADS = 12
HEAD = 64
FF = 3072
SEQ = 3072
TOKENS = 24576
QBLOCK = 512
N_FSDP = 8


def steps_of(own_key, dims, cuts, smallest, top_value):
    def one(dim, shards_of):
        heights = jax.random.uniform(jax.random.fold_in(jax.random.fold_in(own_key, 6), dim), (shards_of,), jnp.float32, smallest / len(cuts), top_value / len(cuts))
        return jnp.repeat(jnp.exp(heights), dims[dim] // shards_of).reshape((-1,) + (1,) * (len(dims) - dim - 1))

    loudness = one(*cuts[0])
    for cut in cuts[1:]:
        loudness = loudness * one(*cut)
    return loudness


def profile(number_of, total, bound, lean):
    portions = [(1 << 20) // math.isqrt(grade ** lean) + 1 for grade in range(2, number_of + 1)]
    spare, holding = total - bound - (number_of - 1), [1] * (number_of - 1)
    while spare > 0:
        free = [i for i in range(number_of - 1) if holding[i] < bound]
        mass, left = sum([portions[i] for i in free]), spare
        for i in free:
            addition = min(bound - holding[i], max(1, left * portions[i] // mass), spare)
            holding[i] = holding[i] + addition
            spare = spare - addition
    return np.array([bound] + holding)


def uneven_parts(rng, number_of, total, limit, skew):
    if number_of == 2:
        one = jax.random.randint(rng, (), max(1, total - limit), min(limit, total - 1) + 1)
        return jnp.stack([one, total - one])
    lengths = jnp.asarray(profile(number_of, total, limit, skew), jnp.int32)
    twos = (number_of - 1) // 2
    giver, sink = lengths[1:1 + 2 * twos:2], lengths[2:2 + 2 * twos:2]
    room = jnp.minimum(giver - 1, limit - sink)
    shifted = jax.random.randint(jax.random.fold_in(rng, 1), (twos,), 0, 1 << 20) % (room + 1)
    lengths = lengths.at[1:1 + 2 * twos:2].set(giver - shifted).at[2:2 + 2 * twos:2].set(sink + shifted)
    return lengths[jax.random.permutation(jax.random.fold_in(rng, 2), number_of)]


def centred(own_key, shape, deviation, bound, pieces=(), held_as=jnp.bfloat16):
    level = steps_of(own_key, shape, pieces, -0.22, 0.18) if pieces else 1.0
    drawn = jax.random.normal(own_key, shape, jnp.float32) * deviation * level
    return jnp.minimum(jnp.maximum(drawn, -bound), bound).astype(held_as)


def setup_inputs(seed: int = 0) -> dict:
    key_of = jax.random.split(jax.random.key(seed), 17)
    return {
        "tokens": centred(key_of[0], (TOKENS, D), 1.0, 6.0, ((0, 32),)),
        "segments": jax.vmap(lambda own: jnp.searchsorted(jnp.cumsum(uneven_parts(own, max(4, SEQ // 96), SEQ, SEQ // 2, 2)), jnp.arange(SEQ), side="right"))(jax.random.split(key_of[1], N_FSDP)).reshape((N_FSDP, SEQ)).astype(jnp.int32),
        "cotangent": centred(key_of[2], (TOKENS, D), 1.0, 6.0, ((0, 32),)),
        "w_qkv": centred(key_of[3], (D, 3 * D), (D // 2) ** -0.5, 0.3125, ((0, 32),)),
        "b_query": centred(key_of[4], (D,), 0.5, 3.0, ((0, 32),)),
        "b_value": centred(key_of[5], (D,), 0.5, 3.0, ((0, 32),)),
        "w_out": centred(key_of[6], (D, D), (D // 8) ** -0.5, 0.625, ((0, 32),)),
        "b_out": centred(key_of[7], (D,), 0.3, 2.0, ((0, 32),)),
        "ln1_gain": jnp.clip(1.0 + 0.1 * jax.random.normal(key_of[8], (D,), jnp.float32), 0.5, 1.5).astype(jnp.bfloat16),
        "ln1_bias": centred(key_of[9], (D,), 0.3, 2.0, ((0, 32),)),
        "w_up": centred(key_of[10], (D, FF), D ** -0.5, 0.21875, ((0, 32),)),
        "b_up": centred(key_of[11], (FF,), 0.5, 3.0, ((0, 32),)),
        "w_down": centred(key_of[12], (FF, D), (FF // 2) ** -0.5, 0.15625, ((0, 32),)),
        "b_down": centred(key_of[13], (D,), 0.3, 2.0, ((0, 32),)),
        "ln2_gain": jnp.clip(1.0 + 0.1 * jax.random.normal(key_of[14], (D,), jnp.float32), 0.5, 1.5).astype(jnp.bfloat16),
        "ln2_bias": centred(key_of[15], (D,), 0.3, 2.0, ((0, 32),)),
    }


norm_eps = 1e-06
masked = -1e+30
highest = lax.Precision.HIGHEST

@jax.custom_vjp
def low(v):
    return lax.optimization_barrier(v.astype(jnp.bfloat16)).astype(jnp.float32)

@jax.custom_vjp
def low_back(v):
    return v

def low_keep(v):
    return (low(v), None)

def low_pass(kept, upstream_gradient):
    return (upstream_gradient,)

def back_keep(v):
    return (v, None)

def back_low(kept, upstream_gradient):
    return (low(upstream_gradient),)
low.defvjp(low_keep, low_pass)
low_back.defvjp(back_keep, back_low)

def matmul(left, right):
    return jnp.dot(left, right, precision=highest, preferred_element_type=jnp.float32)

def normalize(values, norm_gain, norm_shift):
    center = lax.optimization_barrier(jnp.mean(values, -1, keepdims=True))
    mean_removed = values - center
    spread = lax.optimization_barrier(jnp.mean(mean_removed * mean_removed, -1, keepdims=True))
    return mean_removed * lax.rsqrt(spread + norm_eps) * norm_gain + norm_shift

def layer(params, input_tokens, seg_row):
    w_qkv, b_query, b_value, w_out, b_out, ln1_gain, ln1_bias, w_up, b_up, w_down, b_down, ln2_gain, ln2_bias = params
    bias_qkv = jnp.concatenate([b_query, jnp.zeros_like(b_query), b_value])
    packed = low_back(low(matmul(input_tokens, w_qkv) + bias_qkv)).reshape(SEQ, 3, HEADS, HEAD)
    queries = packed[:, 0]
    keys = packed[:, 1]
    values = packed[:, 2]
    blocked_q = queries.reshape(SEQ // QBLOCK, QBLOCK, HEADS, HEAD)
    blocked_s = seg_row.reshape(SEQ // QBLOCK, QBLOCK)

    def attend(pair):
        query_block, seg_block = pair
        scores = jnp.einsum('qhe,khe->hqk', query_block, keys, precision=highest) * 0.125
        scores = low_back(scores)
        same = seg_block[:, None] == seg_row[None, :]
        scores = jnp.where(same[None], scores, masked)
        weights = jax.nn.softmax(scores, axis=-1)
        return jnp.einsum('hqk,khe->qhe', low(weights), values, precision=highest)
    mixed = lax.map(jax.checkpoint(attend), (blocked_q, blocked_s)).reshape(SEQ, D)
    mixed = low_back(low(mixed))
    residual_branch = low_back(matmul(mixed, w_out) + b_out)
    attention_output = normalize(input_tokens + residual_branch, ln1_gain, ln1_bias)
    pre = low_back(matmul(low(attention_output), w_up) + b_up)
    activ = low(jax.nn.gelu(pre, approximate=False))
    feedforward_net = low_back(matmul(activ, w_down) + b_down)
    return normalize(attention_output + feedforward_net, ln2_gain, ln2_bias)

def reference(tokens, segments, cotangent, w_qkv, b_query, b_value, w_out, b_out, ln1_gain, ln1_bias, w_up, b_up, w_down, b_down, ln2_gain, ln2_bias):
    params = tuple((item.astype(jnp.float32) for item in (w_qkv, b_query, b_value, w_out, b_out, ln1_gain, ln1_bias, w_up, b_up, w_down, b_down, ln2_gain, ln2_bias)))
    inputs_all = tokens.astype(jnp.float32).reshape(N_FSDP, SEQ, D)
    cots_all = cotangent.astype(jnp.float32).reshape(N_FSDP, SEQ, D)

    def step(total, item):
        input_tokens, seg_row, cots = item

        def forward(weights, values):
            return layer(weights, values, seg_row)
        layer_output, pullback = jax.vjp(forward, params, input_tokens)
        grad_params, incoming_gradient = pullback(cots)
        total = jax.tree.map(jnp.add, total, grad_params)
        return (total, (layer_output.astype(jnp.bfloat16), incoming_gradient))
    zeros = jax.tree.map(jnp.zeros_like, params)
    total, (results, grads_in) = lax.scan(step, zeros, (inputs_all, segments, cots_all))
    return (results.reshape(TOKENS, D), grads_in.reshape(TOKENS, D), total[0], total[1], total[2], total[3], total[4], total[5], total[6], total[7], total[8], total[9], total[10], total[11], total[12])
```

```python
from functools import partial

import jax
import jax.numpy as jnp
from jax import lax
from jax.experimental import pallas as pl
from jax.experimental.pallas import tpu as pltpu
from jax.sharding import PartitionSpec as P

HEADS = 12
HEAD = 64
IDS = 32
far = 1e30
QB = 256
KB = 256
f32 = jnp.float32
bf16 = jnp.bfloat16
norm_eps = 1e-06


def padded_width(width):
    return -(-(width + IDS) // 128) * 128


def spans(seg_row, block):
    seq = seg_row.shape[0]
    count = seq // block
    first = seg_row[::block]
    last = seg_row[block - 1 :: block]
    lo = jnp.sum((seg_row[None, :] < first[:, None]).astype(jnp.int32), 1)
    hi = jnp.sum((seg_row[None, :] <= last[:, None]).astype(jnp.int32), 1)
    return lo, hi


def windows(seg_row, block, step, grain):
    lo, hi = spans(seg_row, block)
    seq = seg_row.shape[0]
    start = lo // grain * grain
    number = -(-(hi - start) // step)
    start = jnp.minimum(start, seq - number * step)
    return start.astype(jnp.int32), number.astype(jnp.int32)


def lanes_of(head, shape):
    lane = lax.broadcasted_iota(jnp.int32, shape, len(shape) - 1)
    return (lane >= head * HEAD) & (lane < (head + 1) * HEAD)


def forward_kernel(heads, start_ref, number_ref, q_ref, k_ref, v_ref, o_ref, lse_ref, kh, vt, acc):
    step = pl.program_id(0)
    seq, wide = k_ref.shape
    width = heads * HEAD

    @pl.when(step == 0)
    def _():
        def part(i, carry):
            rows = pl.ds(i * KB, KB)
            k = k_ref[rows, :]
            lane = lax.broadcasted_iota(jnp.int32, k.shape, 1)
            for h in range(heads):
                keep = lanes_of(h, k.shape) | (lane >= width)
                kh[h, rows, :] = jnp.where(keep, k, jnp.zeros_like(k))
            vt[:, rows] = v_ref[rows, :].T
            return carry

        lax.fori_loop(0, seq // KB, part, 0)

    q = q_ref[...]
    start = start_ref[step]
    acc[...] = jnp.zeros_like(acc)

    def one(j, carry):
        at = pl.multiple_of(start + j * KB, 128)
        rows = pl.ds(at, KB)
        out = []
        for h in range(heads):
            top, total = carry[2 * h], carry[2 * h + 1]
            s = lax.dot_general(
                kh[h, rows, :], q, (((1,), (1,)), ((), ())), preferred_element_type=f32
            )
            new = jnp.maximum(top, jnp.max(s, 0, keepdims=True))
            p = jnp.exp(s - new)
            fade = jnp.exp(top - new)
            total = total * fade + jnp.sum(p, 0, keepdims=True)
            part = jnp.dot(
                vt[h * HEAD : (h + 1) * HEAD, rows], p.astype(bf16), preferred_element_type=f32
            )
            mine = slice(h * HEAD, (h + 1) * HEAD)
            acc[mine, :] = acc[mine, :] * fade + part
            out += [new, total]
        return tuple(out)

    first = (jnp.full((1, QB), -jnp.inf, f32), jnp.zeros((1, QB), f32)) * heads
    done = lax.fori_loop(0, number_ref[step], one, first)
    for h in range(heads):
        mine = slice(h * HEAD, (h + 1) * HEAD)
        acc[mine, :] = acc[mine, :] / done[2 * h + 1]
        lse_ref[h : h + 1, :] = done[2 * h] + jnp.log(done[2 * h + 1])
    o_ref[...] = acc[...].T.astype(bf16)


def attend_forward(q, k, v, starts, numbers, heads):
    seq, wide = q.shape
    width = heads * HEAD
    steps = seq // QB
    cost = pl.CostEstimate(
        flops=2 * heads * seq * seq * HEAD, bytes_accessed=8 * seq * wide, transcendentals=heads * seq * seq // 3
    )
    return pl.pallas_call(
        lambda *refs: forward_kernel(heads, *refs),
        grid_spec=pltpu.PrefetchScalarGridSpec(
            num_scalar_prefetch=2,
            grid=(steps,),
            in_specs=[
                pl.BlockSpec((QB, wide), lambda i, a, b: (i, 0)),
                pl.BlockSpec((seq, wide), lambda i, a, b: (0, 0)),
                pl.BlockSpec((seq, width), lambda i, a, b: (0, 0)),
            ],
            out_specs=[
                pl.BlockSpec((QB, width), lambda i, a, b: (i, 0)),
                pl.BlockSpec((8, QB), lambda i, a, b: (0, i)),
            ],
            scratch_shapes=[
                pltpu.VMEM((heads, seq, wide), bf16),
                pltpu.VMEM((width, seq), bf16),
                pltpu.VMEM((width, QB), f32),
            ],
        ),
        out_shape=[
            jax.ShapeDtypeStruct((seq, width), bf16),
            jax.ShapeDtypeStruct((8, seq), f32),
        ],
        cost_estimate=cost,
        compiler_params=pltpu.CompilerParams(vmem_limit_bytes=48 << 20),
        name="attend_forward",
    )(starts, numbers, q, k, v)


def backward_kernel(
    heads, start_ref, number_ref, q_ref, k_ref, v_ref, g_ref, o_ref, lse_ref,
    dq_ref, dk_ref, dv_ref, qh, gh, gq, dqt, delta, dk, dv,
):
    step = pl.program_id(0)
    seq, wide = q_ref.shape
    width = heads * HEAD

    @pl.when(step == 0)
    def _():
        def part(i, carry):
            rows = pl.ds(i * QB, QB)
            q = q_ref[rows, :]
            g = g_ref[rows, :]
            base = i * (heads * QB)
            gz = jnp.concatenate([g, jnp.zeros((QB, wide - width), bf16)], 1)
            gq[rows, :] = gz
            for h in range(heads):
                keep = lanes_of(h, q.shape)
                qh[pl.ds(base + h * QB, QB), :] = jnp.where(keep, q, jnp.zeros_like(q))
                gh[pl.ds(base + h * QB, QB), :] = jnp.where(keep, gz, jnp.zeros_like(gz))
            product = g.astype(f32) * o_ref[rows, :].astype(f32)
            lane = lax.broadcasted_iota(jnp.int32, (8, width), 1)
            row = lax.broadcasted_iota(jnp.int32, (8, width), 0)
            pick = ((lane >= row * HEAD) & (lane < (row + 1) * HEAD)).astype(f32)
            delta[:, rows] = lax.dot_general(
                pick, product, (((1,), (1,)), ((), ())),
                preferred_element_type=f32, precision=lax.Precision.HIGHEST,
            )
            dqt[:, rows] = jnp.zeros((width, QB), f32)
            return carry

        lax.fori_loop(0, seq // QB, part, 0)

    start = start_ref[step]
    k = k_ref[...]
    v = v_ref[...]
    lane = lax.broadcasted_iota(jnp.int32, k.shape, 1)
    vz = jnp.concatenate([v, jnp.zeros((KB, wide - width), bf16)], 1)
    kh = [jnp.where(lanes_of(h, k.shape) | (lane >= width), k, jnp.zeros_like(k)) for h in range(heads)]
    vh = [jnp.where(lanes_of(h, k.shape), vz, jnp.zeros_like(vz)) for h in range(heads)]
    kt = k[:, :].T
    dk[...] = jnp.zeros_like(dk)
    dv[...] = jnp.zeros_like(dv)

    def one(i, carry):
        block = start + i
        rows = pl.ds(pl.multiple_of(block * QB, QB), QB)
        tall = pl.ds(pl.multiple_of(block * (heads * QB), heads * QB), heads * QB)
        q = q_ref[rows, :]
        g = gq[rows, :]
        ps, dss = [], []
        for h in range(heads):
            s = lax.dot_general(kh[h], q, (((1,), (1,)), ((), ())), preferred_element_type=f32)
            p = jnp.exp(s - lse_ref[h : h + 1, rows])
            dp = lax.dot_general(vh[h], g, (((1,), (1,)), ((), ())), preferred_element_type=f32)
            ds = (p * (dp - delta[h : h + 1, rows])).astype(bf16)
            ps.append(p.astype(bf16))
            dss.append(ds)
            mine = slice(h * HEAD, (h + 1) * HEAD)
            dqt[mine, rows] += jnp.dot(kt[mine, :], ds, preferred_element_type=f32)
        dv[...] += jnp.dot(jnp.concatenate(ps, 1), gh[tall, :], preferred_element_type=f32)
        dk[...] += jnp.dot(jnp.concatenate(dss, 1), qh[tall, :], preferred_element_type=f32)
        return carry

    lax.fori_loop(0, number_ref[step], one, 0)
    dk_ref[...] = dk[:, :width].astype(bf16)
    dv_ref[...] = dv[:, :width].astype(bf16)

    @pl.when(step == pl.num_programs(0) - 1)
    def _():
        def part(i, carry):
            rows = pl.ds(i * QB, QB)
            dq_ref[rows, :] = (dqt[:, rows] * 0.125).T.astype(bf16)
            return carry

        lax.fori_loop(0, seq // QB, part, 0)


def attend_backward(q, k, v, g, o, lse, starts, numbers, heads):
    seq, wide = q.shape
    width = heads * HEAD
    steps = seq // KB
    whole = lambda shape: pl.BlockSpec(shape, lambda i, a, b: (0, 0))
    cost = pl.CostEstimate(
        flops=5 * heads * seq * seq * HEAD, bytes_accessed=16 * seq * wide, transcendentals=heads * seq * seq // 3
    )
    return pl.pallas_call(
        lambda *refs: backward_kernel(heads, *refs),
        grid_spec=pltpu.PrefetchScalarGridSpec(
            num_scalar_prefetch=2,
            grid=(steps,),
            in_specs=[
                whole((seq, wide)),
                pl.BlockSpec((KB, wide), lambda i, a, b: (i, 0)),
                pl.BlockSpec((KB, width), lambda i, a, b: (i, 0)),
                whole((seq, width)),
                whole((seq, width)),
                whole((8, seq)),
            ],
            out_specs=[
                whole((seq, width)),
                pl.BlockSpec((KB, width), lambda i, a, b: (i, 0)),
                pl.BlockSpec((KB, width), lambda i, a, b: (i, 0)),
            ],
            scratch_shapes=[
                pltpu.VMEM((heads * seq, wide), bf16),
                pltpu.VMEM((heads * seq, wide), bf16),
                pltpu.VMEM((seq, wide), bf16),
                pltpu.VMEM((width, seq), f32),
                pltpu.VMEM((8, seq), f32),
                pltpu.VMEM((KB, wide), f32),
                pltpu.VMEM((KB, wide), f32),
            ],
        ),
        out_shape=[jax.ShapeDtypeStruct((seq, width), bf16)] * 3,
        cost_estimate=cost,
        compiler_params=pltpu.CompilerParams(vmem_limit_bytes=56 << 20),
        name="attend_backward",
    )(starts, numbers, q, k, v, g, o, lse)


def augment(q, k, seg_row):
    seq, width = q.shape
    wide = padded_width(width)
    hot = (seg_row[:, None] == jnp.arange(IDS)[None, :])
    rest = jnp.zeros((seq, wide - width - IDS), bf16)
    qa = jnp.concatenate([q * jnp.asarray(0.125, bf16), hot.astype(bf16), rest], 1)
    ka = jnp.concatenate([k, jnp.where(hot, 0.0, -far).astype(bf16), rest], 1)
    return qa, ka


def layer_normalizer(values, norm_gain, norm_shift):
    center = jnp.mean(values, -1, keepdims=True)
    mean_removed = values - center
    spread = jnp.mean(mean_removed * mean_removed, -1, keepdims=True)
    inverse_deviation = lax.rsqrt(spread + norm_eps)
    normalized_rows = mean_removed * inverse_deviation
    return (normalized_rows * norm_gain + norm_shift, normalized_rows, inverse_deviation)


def norm_reverse_pass(upstream_gradient, normalized_rows, inverse_deviation, norm_gain):
    norm_gain_gradient = jnp.sum(upstream_gradient * normalized_rows, 0)
    grad_shift = jnp.sum(upstream_gradient, 0)
    scaled_rows = upstream_gradient * norm_gain
    inner_activation = jnp.mean(scaled_rows * normalized_rows, -1, keepdims=True)
    incoming_gradient = inverse_deviation * (
        scaled_rows - jnp.mean(scaled_rows, -1, keepdims=True) - normalized_rows * inner_activation
    )
    return (incoming_gradient, norm_gain_gradient, grad_shift)


def body(
    tokens,
    segments,
    cotangent,
    w_qkv,
    b_query,
    b_value,
    w_out,
    b_out,
    ln1_gain,
    ln1_bias,
    w_up,
    b_up,
    w_down,
    b_down,
    ln2_gain,
    ln2_bias,
):
    whole = (
        lax.all_gather(w_qkv, ("sp", "fsdp"), axis=0, tiled=True),
        lax.all_gather(b_query, ("sp", "fsdp"), axis=0, tiled=True),
        lax.all_gather(b_value, ("sp", "fsdp"), axis=0, tiled=True),
        lax.all_gather(w_out, ("sp", "fsdp"), axis=0, tiled=True),
        lax.all_gather(b_out, ("sp", "fsdp"), axis=0, tiled=True),
        lax.all_gather(ln1_gain, ("sp", "fsdp"), axis=0, tiled=True),
        lax.all_gather(ln1_bias, ("sp", "fsdp"), axis=0, tiled=True),
        lax.all_gather(w_up, ("sp", "fsdp"), axis=0, tiled=True),
        lax.all_gather(b_up, ("sp", "fsdp"), axis=0, tiled=True),
        lax.all_gather(w_down, ("sp", "fsdp"), axis=0, tiled=True),
        lax.all_gather(b_down, ("sp", "fsdp"), axis=0, tiled=True),
        lax.all_gather(ln2_gain, ("sp", "fsdp"), axis=0, tiled=True),
        lax.all_gather(ln2_bias, ("sp", "fsdp"), axis=0, tiled=True),
    )
    (
        full_qkv,
        bias_query,
        bias_value,
        full_out,
        bias_out,
        attention_norm_gain,
        attention_norm_shift,
        full_up,
        bias_up,
        full_down,
        bias_down,
        feedforward_norm_gain,
        feedforward_norm_shift,
    ) = whole
    bias_query = bias_query.astype(jnp.float32)
    bias_value = bias_value.astype(jnp.float32)
    bias_out = bias_out.astype(jnp.float32)
    attention_norm_gain = attention_norm_gain.astype(jnp.float32)
    attention_norm_shift = attention_norm_shift.astype(jnp.float32)
    bias_up = bias_up.astype(jnp.float32)
    bias_down = bias_down.astype(jnp.float32)
    feedforward_norm_gain = feedforward_norm_gain.astype(jnp.float32)
    feedforward_norm_shift = feedforward_norm_shift.astype(jnp.float32)
    groups = lax.axis_size("sp")
    rows = tokens.shape[0]
    width_all = tokens.shape[1]
    heads_local = HEADS // groups
    width = heads_local * HEAD
    seq_len = rows * groups
    input_tokens = tokens.astype(jnp.float32)
    bias_qkv = jnp.concatenate([bias_query, jnp.zeros_like(bias_query), bias_value])
    packed = (jnp.dot(tokens, full_qkv, preferred_element_type=jnp.float32) + bias_qkv).astype(
        jnp.bfloat16
    )
    heads_in = lax.all_to_all(
        packed.reshape(rows, 3, groups, width), "sp", split_axis=2, concat_axis=0, tiled=True
    )
    seg_row = segments[0]
    queries, keys = augment(heads_in[:, 0, 0], heads_in[:, 1, 0], seg_row)
    values = heads_in[:, 2, 0]
    forward_start, forward_number = windows(seg_row, QB, KB, 128)
    backward_start, backward_number = windows(seg_row, KB, QB, QB)
    attended, logsum = attend_forward(
        queries, keys, values, forward_start, forward_number, heads_local
    )
    back_tokens = lax.all_to_all(
        attended.reshape(seq_len, 1, width), "sp", split_axis=0, concat_axis=1, tiled=True
    )
    mixed = back_tokens.reshape(rows, width_all)
    residual_branch = jnp.dot(mixed, full_out, preferred_element_type=jnp.float32) + bias_out
    attention_output, attention_normalized, attention_inverse_deviation = layer_normalizer(
        input_tokens + residual_branch, attention_norm_gain, attention_norm_shift
    )
    first_low = attention_output.astype(jnp.bfloat16)
    pre = jnp.dot(first_low, full_up, preferred_element_type=jnp.float32) + bias_up
    activ = jax.nn.gelu(pre, approximate=False).astype(jnp.bfloat16)
    feedforward_net = jnp.dot(activ, full_down, preferred_element_type=jnp.float32) + bias_down
    layer_output, feedforward_normalized, feedforward_inverse_deviation = layer_normalizer(
        attention_output + feedforward_net, feedforward_norm_gain, feedforward_norm_shift
    )
    output = layer_output.astype(jnp.bfloat16)
    again = (
        lax.all_gather(w_qkv, ("sp", "fsdp"), axis=0, tiled=True),
        lax.all_gather(w_out, ("sp", "fsdp"), axis=0, tiled=True),
        lax.all_gather(ln1_gain, ("sp", "fsdp"), axis=0, tiled=True),
        lax.all_gather(w_up, ("sp", "fsdp"), axis=0, tiled=True),
        lax.all_gather(w_down, ("sp", "fsdp"), axis=0, tiled=True),
        lax.all_gather(ln2_gain, ("sp", "fsdp"), axis=0, tiled=True),
    )
    back_qkv, back_out, reverse_attention_gain, back_up, back_down, reverse_feedforward_gain = again
    reverse_attention_gain = reverse_attention_gain.astype(jnp.float32)
    reverse_feedforward_gain = reverse_feedforward_gain.astype(jnp.float32)
    outgoing_gradient = cotangent.astype(jnp.float32)
    hidden_two_gradient, feedforward_gain_gradient, feedforward_shift_gradient = norm_reverse_pass(
        outgoing_gradient,
        feedforward_normalized,
        feedforward_inverse_deviation,
        reverse_feedforward_gain,
    )
    grad_ffn = hidden_two_gradient.astype(jnp.bfloat16)
    grad_bias_down = jnp.sum(grad_ffn.astype(jnp.float32), 0)
    grad_full_down = jnp.einsum("tf,td->fd", activ, grad_ffn, preferred_element_type=jnp.float32)
    grad_activ = jnp.einsum("td,fd->tf", grad_ffn, back_down, preferred_element_type=jnp.float32)
    gelu_value, gelu_pull = jax.vjp(partial(jax.nn.gelu, approximate=False), pre)
    grad_pre = gelu_pull(grad_activ)[0].astype(jnp.bfloat16)
    grad_bias_up = jnp.sum(grad_pre.astype(jnp.float32), 0)
    grad_full_up = jnp.einsum("td,tf->df", first_low, grad_pre, preferred_element_type=jnp.float32)
    attention_output_gradient = hidden_two_gradient + jnp.einsum(
        "tf,df->td", grad_pre, back_up, preferred_element_type=jnp.float32
    )
    grad_h1, grad_gain_one, grad_shift_one = norm_reverse_pass(
        attention_output_gradient,
        attention_normalized,
        attention_inverse_deviation,
        reverse_attention_gain,
    )
    grad_branch = grad_h1.astype(jnp.bfloat16)
    grad_bias_out = jnp.sum(grad_branch.astype(jnp.float32), 0)
    grad_full_out = jnp.einsum("td,te->de", mixed, grad_branch, preferred_element_type=jnp.float32)
    grad_mixed = jnp.einsum(
        "te,de->td", grad_branch, back_out, preferred_element_type=jnp.float32
    ).astype(jnp.bfloat16)
    grad_heads = lax.all_to_all(
        grad_mixed.reshape(rows, groups, width), "sp", split_axis=1, concat_axis=0, tiled=True
    )
    grad_query, grad_keys, grad_values = attend_backward(
        queries,
        keys,
        values,
        grad_heads.reshape(seq_len, width),
        attended,
        logsum,
        backward_start // QB,
        backward_number,
        heads_local,
    )
    stacked = jnp.stack(
        [
            grad_query.reshape(seq_len, width),
            grad_keys.reshape(seq_len, width),
            grad_values.reshape(seq_len, width),
        ],
        1,
    )
    stacked = stacked[:, :, None, :]
    grad_back = lax.all_to_all(stacked, "sp", split_axis=0, concat_axis=2, tiled=True)
    grad_packed = grad_back.reshape(rows, 3 * width_all)
    grad_wide = grad_packed.astype(jnp.float32)
    grad_bias_query = jnp.sum(grad_wide[:, :width_all], 0)
    grad_bias_value = jnp.sum(grad_wide[:, 2 * width_all :], 0)
    grad_full_qkv = jnp.einsum("td,tc->dc", tokens, grad_packed, preferred_element_type=jnp.float32)
    grad_input = grad_h1 + jnp.einsum(
        "tc,dc->td", grad_packed, back_qkv, preferred_element_type=jnp.float32
    )
    grads = (
        grad_full_qkv,
        grad_bias_query,
        grad_bias_value,
        grad_full_out,
        grad_bias_out,
        grad_gain_one,
        grad_shift_one,
        grad_full_up,
        grad_bias_up,
        grad_full_down,
        grad_bias_down,
        feedforward_gain_gradient,
        feedforward_shift_gradient,
    )
    owned = (
        lax.psum_scatter(grads[0], ("sp", "fsdp"), scatter_dimension=0, tiled=True),
        lax.psum_scatter(grads[1], ("sp", "fsdp"), scatter_dimension=0, tiled=True),
        lax.psum_scatter(grads[2], ("sp", "fsdp"), scatter_dimension=0, tiled=True),
        lax.psum_scatter(grads[3], ("sp", "fsdp"), scatter_dimension=0, tiled=True),
        lax.psum_scatter(grads[4], ("sp", "fsdp"), scatter_dimension=0, tiled=True),
        lax.psum_scatter(grads[5], ("sp", "fsdp"), scatter_dimension=0, tiled=True),
        lax.psum_scatter(grads[6], ("sp", "fsdp"), scatter_dimension=0, tiled=True),
        lax.psum_scatter(grads[7], ("sp", "fsdp"), scatter_dimension=0, tiled=True),
        lax.psum_scatter(grads[8], ("sp", "fsdp"), scatter_dimension=0, tiled=True),
        lax.psum_scatter(grads[9], ("sp", "fsdp"), scatter_dimension=0, tiled=True),
        lax.psum_scatter(grads[10], ("sp", "fsdp"), scatter_dimension=0, tiled=True),
        lax.psum_scatter(grads[11], ("sp", "fsdp"), scatter_dimension=0, tiled=True),
        lax.psum_scatter(grads[12], ("sp", "fsdp"), scatter_dimension=0, tiled=True),
    )
    return (
        output,
        grad_input,
        owned[0],
        owned[1],
        owned[2],
        owned[3],
        owned[4],
        owned[5],
        owned[6],
        owned[7],
        owned[8],
        owned[9],
        owned[10],
        owned[11],
        owned[12],
    )


def solution(mesh):
    in_specs = (
        P(("fsdp", "sp"), None),
        P("fsdp", None),
        P(("fsdp", "sp"), None),
        P(("sp", "fsdp"), None),
        P(("sp", "fsdp")),
        P(("sp", "fsdp")),
        P(("sp", "fsdp"), None),
        P(("sp", "fsdp")),
        P(("sp", "fsdp")),
        P(("sp", "fsdp")),
        P(("sp", "fsdp"), None),
        P(("sp", "fsdp")),
        P(("sp", "fsdp"), None),
        P(("sp", "fsdp")),
        P(("sp", "fsdp")),
        P(("sp", "fsdp")),
    )
    out_specs = (
        P(("fsdp", "sp"), None),
        P(("fsdp", "sp"), None),
        P(("sp", "fsdp"), None),
        P(("sp", "fsdp")),
        P(("sp", "fsdp")),
        P(("sp", "fsdp"), None),
        P(("sp", "fsdp")),
        P(("sp", "fsdp")),
        P(("sp", "fsdp")),
        P(("sp", "fsdp"), None),
        P(("sp", "fsdp")),
        P(("sp", "fsdp"), None),
        P(("sp", "fsdp")),
        P(("sp", "fsdp")),
        P(("sp", "fsdp")),
    )
    return jax.shard_map(body, mesh=mesh, in_specs=in_specs, out_specs=out_specs, check_vma=False)
```

```python
from functools import partial

import jax
import jax.numpy as jnp
from jax import lax
from jax.experimental import pallas as pl
from jax.experimental.pallas import tpu as pltpu
from jax.sharding import PartitionSpec as P

HEADS = 12
HEAD = 64
IDS = 32
far = 1e30
QB = 256
KB = 256
f32 = jnp.float32
bf16 = jnp.bfloat16
norm_eps = 1e-06


def padded_width(width):
    return -(-(width + IDS) // 128) * 128


def spans(seg_row, block):
    seq = seg_row.shape[0]
    count = seq // block
    first = seg_row[::block]
    last = seg_row[block - 1 :: block]
    lo = jnp.sum((seg_row[None, :] < first[:, None]).astype(jnp.int32), 1)
    hi = jnp.sum((seg_row[None, :] <= last[:, None]).astype(jnp.int32), 1)
    return lo, hi


def windows(seg_row, block, step, grain):
    lo, hi = spans(seg_row, block)
    seq = seg_row.shape[0]
    start = lo // grain * grain
    number = -(-(hi - start) // step)
    start = jnp.minimum(start, seq - number * step)
    return start.astype(jnp.int32), number.astype(jnp.int32)


def lanes_of(head, shape):
    lane = lax.broadcasted_iota(jnp.int32, shape, len(shape) - 1)
    return (lane >= head * HEAD) & (lane < (head + 1) * HEAD)


def forward_kernel(heads, start_ref, number_ref, q_ref, k_ref, v_ref, o_ref, lse_ref, kh, vt, acc):
    step = pl.program_id(0)
    seq, wide = k_ref.shape
    width = heads * HEAD

    @pl.when(step == 0)
    def _():
        def part(i, carry):
            rows = pl.ds(i * KB, KB)
            k = k_ref[rows, :]
            lane = lax.broadcasted_iota(jnp.int32, k.shape, 1)
            for h in range(heads):
                keep = lanes_of(h, k.shape) | (lane >= width)
                kh[h, rows, :] = jnp.where(keep, k, jnp.zeros_like(k))
            vt[:, rows] = v_ref[rows, :].T
            return carry

        lax.fori_loop(0, seq // KB, part, 0)

    q = q_ref[...]
    start = start_ref[step]
    acc[...] = jnp.zeros_like(acc)

    def one(j, carry):
        at = pl.multiple_of(start + j * KB, 128)
        rows = pl.ds(at, KB)
        out = []
        for h in range(heads):
            top, total = carry[2 * h], carry[2 * h + 1]
            s = lax.dot_general(
                kh[h, rows, :], q, (((1,), (1,)), ((), ())), preferred_element_type=f32
            )
            new = jnp.maximum(top, jnp.max(s, 0, keepdims=True))
            p = jnp.exp(s - new)
            fade = jnp.exp(top - new)
            total = total * fade + jnp.sum(p, 0, keepdims=True)
            part = jnp.dot(
                vt[h * HEAD : (h + 1) * HEAD, rows], p.astype(bf16), preferred_element_type=f32
            )
            mine = slice(h * HEAD, (h + 1) * HEAD)
            acc[mine, :] = acc[mine, :] * fade + part
            out += [new, total]
        return tuple(out)

    first = (jnp.full((1, QB), -jnp.inf, f32), jnp.zeros((1, QB), f32)) * heads
    done = lax.fori_loop(0, number_ref[step], one, first)
    for h in range(heads):
        mine = slice(h * HEAD, (h + 1) * HEAD)
        acc[mine, :] = acc[mine, :] / done[2 * h + 1]
        lse_ref[h : h + 1, :] = done[2 * h] + jnp.log(done[2 * h + 1])
    o_ref[...] = acc[...].T.astype(bf16)


def attend_forward(q, k, v, starts, numbers, heads):
    seq, wide = q.shape
    width = heads * HEAD
    steps = seq // QB
    cost = pl.CostEstimate(
        flops=2 * heads * seq * seq * HEAD, bytes_accessed=8 * seq * wide, transcendentals=heads * seq * seq // 3
    )
    return pl.pallas_call(
        lambda *refs: forward_kernel(heads, *refs),
        grid_spec=pltpu.PrefetchScalarGridSpec(
            num_scalar_prefetch=2,
            grid=(steps,),
            in_specs=[
                pl.BlockSpec((QB, wide), lambda i, a, b: (i, 0)),
                pl.BlockSpec((seq, wide), lambda i, a, b: (0, 0)),
                pl.BlockSpec((seq, width), lambda i, a, b: (0, 0)),
            ],
            out_specs=[
                pl.BlockSpec((QB, width), lambda i, a, b: (i, 0)),
                pl.BlockSpec((8, QB), lambda i, a, b: (0, i)),
            ],
            scratch_shapes=[
                pltpu.VMEM((heads, seq, wide), bf16),
                pltpu.VMEM((width, seq), bf16),
                pltpu.VMEM((width, QB), f32),
            ],
        ),
        out_shape=[
            jax.ShapeDtypeStruct((seq, width), bf16),
            jax.ShapeDtypeStruct((8, seq), f32),
        ],
        cost_estimate=cost,
        compiler_params=pltpu.CompilerParams(vmem_limit_bytes=48 << 20),
        name="attend_forward",
    )(starts, numbers, q, k, v)


def backward_kernel(
    heads, start_ref, number_ref, q_ref, k_ref, v_ref, g_ref, o_ref, lse_ref,
    dq_ref, dk_ref, dv_ref, qh, gh, gq, dqt, delta, dk, dv,
):
    step = pl.program_id(0)
    seq, wide = q_ref.shape
    width = heads * HEAD

    @pl.when(step == 0)
    def _():
        def part(i, carry):
            rows = pl.ds(i * QB, QB)
            q = q_ref[rows, :]
            g = g_ref[rows, :]
            base = i * (heads * QB)
            gz = jnp.concatenate([g, jnp.zeros((QB, wide - width), bf16)], 1)
            gq[rows, :] = gz
            for h in range(heads):
                keep = lanes_of(h, q.shape)
                qh[pl.ds(base + h * QB, QB), :] = jnp.where(keep, q, jnp.zeros_like(q))
                gh[pl.ds(base + h * QB, QB), :] = jnp.where(keep, gz, jnp.zeros_like(gz))
            product = g.astype(f32) * o_ref[rows, :].astype(f32)
            lane = lax.broadcasted_iota(jnp.int32, (8, width), 1)
            row = lax.broadcasted_iota(jnp.int32, (8, width), 0)
            pick = ((lane >= row * HEAD) & (lane < (row + 1) * HEAD)).astype(f32)
            delta[:, rows] = lax.dot_general(
                pick, product, (((1,), (1,)), ((), ())),
                preferred_element_type=f32, precision=lax.Precision.HIGHEST,
            )
            dqt[:, rows] = jnp.zeros((width, QB), f32)
            return carry

        lax.fori_loop(0, seq // QB, part, 0)

    start = start_ref[step]
    k = k_ref[...]
    v = v_ref[...]
    lane = lax.broadcasted_iota(jnp.int32, k.shape, 1)
    vz = jnp.concatenate([v, jnp.zeros((KB, wide - width), bf16)], 1)
    kh = [jnp.where(lanes_of(h, k.shape) | (lane >= width), k, jnp.zeros_like(k)) for h in range(heads)]
    vh = [jnp.where(lanes_of(h, k.shape), vz, jnp.zeros_like(vz)) for h in range(heads)]
    kt = k[:, :].T
    dk[...] = jnp.zeros_like(dk)
    dv[...] = jnp.zeros_like(dv)

    def one(i, carry):
        block = start + i
        rows = pl.ds(pl.multiple_of(block * QB, QB), QB)
        tall = pl.ds(pl.multiple_of(block * (heads * QB), heads * QB), heads * QB)
        q = q_ref[rows, :]
        g = gq[rows, :]
        ps, dss = [], []
        for h in range(heads):
            s = lax.dot_general(kh[h], q, (((1,), (1,)), ((), ())), preferred_element_type=f32)
            p = jnp.exp(s - lse_ref[h : h + 1, rows])
            dp = lax.dot_general(vh[h], g, (((1,), (1,)), ((), ())), preferred_element_type=f32)
            ds = (p * (dp - delta[h : h + 1, rows])).astype(bf16)
            ps.append(p.astype(bf16))
            dss.append(ds)
            mine = slice(h * HEAD, (h + 1) * HEAD)
            dqt[mine, rows] += jnp.dot(kt[mine, :], ds, preferred_element_type=f32)
        dv[...] += jnp.dot(jnp.concatenate(ps, 1), gh[tall, :], preferred_element_type=f32)
        dk[...] += jnp.dot(jnp.concatenate(dss, 1), qh[tall, :], preferred_element_type=f32)
        return carry

    lax.fori_loop(0, number_ref[step], one, 0)
    dk_ref[...] = dk[:, :width].astype(bf16)
    dv_ref[...] = dv[:, :width].astype(bf16)

    @pl.when(step == pl.num_programs(0) - 1)
    def _():
        def part(i, carry):
            rows = pl.ds(i * QB, QB)
            dq_ref[rows, :] = (dqt[:, rows] * 0.125).T.astype(bf16)
            return carry

        lax.fori_loop(0, seq // QB, part, 0)


def attend_backward(q, k, v, g, o, lse, starts, numbers, heads):
    seq, wide = q.shape
    width = heads * HEAD
    steps = seq // KB
    whole = lambda shape: pl.BlockSpec(shape, lambda i, a, b: (0, 0))
    cost = pl.CostEstimate(
        flops=5 * heads * seq * seq * HEAD, bytes_accessed=16 * seq * wide, transcendentals=heads * seq * seq // 3
    )
    return pl.pallas_call(
        lambda *refs: backward_kernel(heads, *refs),
        grid_spec=pltpu.PrefetchScalarGridSpec(
            num_scalar_prefetch=2,
            grid=(steps,),
            in_specs=[
                whole((seq, wide)),
                pl.BlockSpec((KB, wide), lambda i, a, b: (i, 0)),
                pl.BlockSpec((KB, width), lambda i, a, b: (i, 0)),
                whole((seq, width)),
                whole((seq, width)),
                whole((8, seq)),
            ],
            out_specs=[
                whole((seq, width)),
                pl.BlockSpec((KB, width), lambda i, a, b: (i, 0)),
                pl.BlockSpec((KB, width), lambda i, a, b: (i, 0)),
            ],
            scratch_shapes=[
                pltpu.VMEM((heads * seq, wide), bf16),
                pltpu.VMEM((heads * seq, wide), bf16),
                pltpu.VMEM((seq, wide), bf16),
                pltpu.VMEM((width, seq), f32),
                pltpu.VMEM((8, seq), f32),
                pltpu.VMEM((KB, wide), f32),
                pltpu.VMEM((KB, wide), f32),
            ],
        ),
        out_shape=[jax.ShapeDtypeStruct((seq, width), bf16)] * 3,
        cost_estimate=cost,
        compiler_params=pltpu.CompilerParams(vmem_limit_bytes=56 << 20),
        name="attend_backward",
    )(starts, numbers, q, k, v, g, o, lse)


def augment(q, k, seg_row):
    seq, width = q.shape
    wide = padded_width(width)
    hot = (seg_row[:, None] == jnp.arange(IDS)[None, :])
    rest = jnp.zeros((seq, wide - width - IDS), bf16)
    qa = jnp.concatenate([q * jnp.asarray(0.125, bf16), hot.astype(bf16), rest], 1)
    ka = jnp.concatenate([k, jnp.where(hot, 0.0, -far).astype(bf16), rest], 1)
    return qa, ka


def layer_normalizer(values, norm_gain, norm_shift):
    center = jnp.mean(values, -1, keepdims=True)
    mean_removed = values - center
    spread = jnp.mean(mean_removed * mean_removed, -1, keepdims=True)
    inverse_deviation = lax.rsqrt(spread + norm_eps)
    normalized_rows = mean_removed * inverse_deviation
    return (normalized_rows * norm_gain + norm_shift, normalized_rows, inverse_deviation)


def norm_reverse_pass(upstream_gradient, normalized_rows, inverse_deviation, norm_gain):
    norm_gain_gradient = jnp.sum(upstream_gradient * normalized_rows, 0)
    grad_shift = jnp.sum(upstream_gradient, 0)
    scaled_rows = upstream_gradient * norm_gain
    inner_activation = jnp.mean(scaled_rows * normalized_rows, -1, keepdims=True)
    incoming_gradient = inverse_deviation * (
        scaled_rows - jnp.mean(scaled_rows, -1, keepdims=True) - normalized_rows * inner_activation
    )
    return (incoming_gradient, norm_gain_gradient, grad_shift)


def by_sp(value, flip):
    groups = lax.axis_size("sp")
    return lax.ppermute(value, "sp", [(i, i ^ flip) for i in range(groups)])


def gather_tokens(tokens):
    rows = tokens.shape[0]
    half = rows // 2
    along_x = by_sp(tokens, 1)
    along_y = by_sp(tokens, 2)
    upper = by_sp(along_y[:half], 1)
    lower = by_sp(along_x[half:], 2)
    me = lax.axis_index("sp")
    out = jnp.zeros((4 * rows, tokens.shape[1]), tokens.dtype)
    for flip, part in ((0, tokens), (1, along_x), (2, along_y)):
        out = lax.dynamic_update_slice(out, part, ((me ^ flip) * rows, 0))
    out = lax.dynamic_update_slice(out, upper, ((me ^ 3) * rows, 0))
    return lax.dynamic_update_slice(out, lower, ((me ^ 3) * rows + half, 0))


def scatter_rows(partial):
    rows = partial.shape[0] // 4
    half = rows // 2
    me = lax.axis_index("sp")

    def piece(flip, lower):
        at = (me ^ flip) * rows + (half if lower else 0)
        return lax.dynamic_slice(partial, (at, 0), (half, partial.shape[1]))

    sent_x = jnp.concatenate([piece(1, False), piece(3, False)], 0).astype(bf16)
    sent_y = jnp.concatenate([piece(2, True), piece(3, True)], 0).astype(bf16)
    got_x = by_sp(sent_x, 1).astype(f32)
    got_y = by_sp(sent_y, 2).astype(f32)
    next_y = by_sp((piece(2, False) + got_x[half:]).astype(bf16), 2).astype(f32)
    next_x = by_sp((piece(1, True) + got_y[half:]).astype(bf16), 1).astype(f32)
    upper = piece(0, False) + got_x[:half] + next_y
    lower = piece(0, True) + got_y[:half] + next_x
    return jnp.concatenate([upper, lower], 0)


def body(
    tokens,
    segments,
    cotangent,
    w_qkv,
    b_query,
    b_value,
    w_out,
    b_out,
    ln1_gain,
    ln1_bias,
    w_up,
    b_up,
    w_down,
    b_down,
    ln2_gain,
    ln2_bias,
):
    both = ("sp", "fsdp")
    groups = lax.axis_size("sp")
    shards = lax.axis_size("fsdp")
    devices = groups * shards
    rows, model = tokens.shape
    hidden = w_up.shape[1]
    ratio = hidden // model
    own = w_qkv.shape[0]
    heads_local = HEADS // groups
    width = heads_local * HEAD
    seq_len = rows * groups
    seg_row = segments[0]

    vectors = [b_out, ln1_gain, ln1_bias, b_down, ln2_gain, ln2_bias, b_up]
    sizes = [item.shape[0] for item in vectors]
    flat = jnp.concatenate(vectors)
    flat = jnp.concatenate([flat, jnp.zeros((8 * model - flat.shape[0],), bf16)]).reshape(8, model)
    up_blocks = [w_up[:, c * model : (c + 1) * model] for c in range(ratio)]
    pack = jnp.concatenate([w_down] + up_blocks + [w_out, flat], 0)
    packed_weights = lax.all_gather(pack, both, axis=0, tiled=False)
    at = ratio * own
    full_down = packed_weights[:, :at].reshape(hidden, model)
    full_up = (
        packed_weights[:, at : 2 * at]
        .reshape(devices, ratio, own, model)
        .transpose(0, 2, 1, 3)
        .reshape(model, hidden)
    )
    full_out = packed_weights[:, 2 * at : 2 * at + own].reshape(model, model)
    flat_all = packed_weights[:, 2 * at + own :].reshape(devices, 8 * model)
    full_vectors = []
    spot = 0
    for size in sizes:
        full_vectors.append(flat_all[:, spot : spot + size].reshape(-1).astype(f32))
        spot += size
    bias_out, gain_one, shift_one, bias_down, gain_two, shift_two, bias_up = full_vectors

    by_group = w_qkv.reshape(own, 3, groups, width).transpose(2, 0, 1, 3).reshape(groups, own, 3 * width)
    mine = lax.all_to_all(by_group, "sp", split_axis=0, concat_axis=0, tiled=True)
    biases = jnp.concatenate([b_query, b_value]).reshape(1, 2 * own)
    biases = jnp.pad(biases, ((0, 0), (0, 3 * width - 2 * own)))
    sent = jnp.concatenate([mine.reshape(groups * own, 3 * width), jnp.pad(biases, ((0, 7), (0, 0)))], 0)
    all_f = lax.all_gather(sent, "fsdp", axis=0, tiled=False)
    weights_qkv = (
        all_f[:, : groups * own]
        .reshape(shards, groups, own, 3 * width)
        .transpose(1, 0, 2, 3)
        .reshape(model, 3 * width)
    )
    bias_row = all_f[:, groups * own]
    bias_query = bias_row[:, :own].reshape(-1).astype(f32)
    bias_value = bias_row[:, own : 2 * own].reshape(-1).astype(f32)
    bias_qkv = jnp.concatenate([bias_query, jnp.zeros_like(bias_query), bias_value])

    tokens_all = gather_tokens(tokens)
    packed = (jnp.dot(tokens_all, weights_qkv, preferred_element_type=f32) + bias_qkv).astype(bf16)
    queries, keys = augment(packed[:, :width], packed[:, width : 2 * width], seg_row)
    values = packed[:, 2 * width :]
    forward_start, forward_number = windows(seg_row, QB, KB, 128)
    backward_start, backward_number = windows(seg_row, KB, QB, QB)
    attended, logsum = attend_forward(
        queries, keys, values, forward_start, forward_number, heads_local
    )
    back_tokens = lax.all_to_all(
        attended.reshape(groups, rows, width), "sp", split_axis=0, concat_axis=0, tiled=True
    )
    mixed = back_tokens.transpose(1, 0, 2).reshape(rows, model)

    input_tokens = tokens.astype(f32)
    residual_branch = jnp.dot(mixed, full_out, preferred_element_type=f32) + bias_out
    first, first_hat, first_rstd = layer_normalizer(
        input_tokens + residual_branch, gain_one, shift_one
    )
    first_low = first.astype(bf16)
    pre = jnp.dot(first_low, full_up, preferred_element_type=f32) + bias_up
    activ = jax.nn.gelu(pre, approximate=False).astype(bf16)
    feedforward_net = jnp.dot(activ, full_down, preferred_element_type=f32) + bias_down
    layer_output, second_hat, second_rstd = layer_normalizer(
        first + feedforward_net, gain_two, shift_two
    )
    output = layer_output.astype(bf16)
    outgoing_gradient = cotangent.astype(f32)
    hidden_two_gradient, grad_gain_two, grad_shift_two = norm_reverse_pass(
        outgoing_gradient, second_hat, second_rstd, gain_two
    )
    grad_ffn = hidden_two_gradient.astype(bf16)
    grad_bias_down = jnp.sum(grad_ffn.astype(f32), 0)
    grad_full_down = jnp.einsum("tf,td->fd", activ, grad_ffn, preferred_element_type=f32)
    grad_activ = jnp.einsum("td,fd->tf", grad_ffn, full_down, preferred_element_type=f32)
    gelu_value, gelu_pull = jax.vjp(partial(jax.nn.gelu, approximate=False), pre)
    grad_pre = gelu_pull(grad_activ)[0].astype(bf16)
    grad_bias_up = jnp.sum(grad_pre.astype(f32), 0)
    grad_full_up = jnp.einsum("td,tf->df", first_low, grad_pre, preferred_element_type=f32)
    attention_output_gradient = hidden_two_gradient + jnp.einsum(
        "tf,df->td", grad_pre, full_up, preferred_element_type=f32
    )
    grad_h1, grad_gain_one, grad_shift_one = norm_reverse_pass(
        attention_output_gradient, first_hat, first_rstd, gain_one
    )
    grad_branch = grad_h1.astype(bf16)
    grad_bias_out = jnp.sum(grad_branch.astype(f32), 0)
    grad_full_out = jnp.einsum("td,te->de", mixed, grad_branch, preferred_element_type=f32)
    grad_mixed = jnp.einsum("te,de->td", grad_branch, full_out, preferred_element_type=f32).astype(
        bf16
    )

    grad_vectors = [
        grad_bias_out,
        grad_gain_one,
        grad_shift_one,
        grad_bias_down,
        grad_gain_two,
        grad_shift_two,
        grad_bias_up,
    ]
    flat = jnp.concatenate([item.reshape(devices, -1) for item in grad_vectors], 1)
    flat = jnp.pad(flat, ((0, 0), (0, 8 * model - flat.shape[1]))).reshape(devices, 8, model)
    grad_up_blocks = (
        grad_full_up.reshape(devices, own, ratio, model)
        .transpose(0, 2, 1, 3)
        .reshape(devices, ratio * own, model)
    )
    grad_pack = jnp.concatenate(
        [
            grad_full_down.reshape(devices, ratio * own, model).astype(bf16),
            grad_up_blocks.astype(bf16),
            grad_full_out.reshape(devices, own, model).astype(bf16),
            flat.astype(bf16),
        ],
        1,
    )
    grad_pack = grad_pack.reshape(-1, model)
    reduced = lax.psum_scatter(grad_pack, both, scatter_dimension=0, tiled=True).astype(f32)

    grad_heads = lax.all_to_all(
        grad_mixed.reshape(rows, groups, width).transpose(1, 0, 2),
        "sp",
        split_axis=0,
        concat_axis=0,
        tiled=True,
    )
    grad_query, grad_keys, grad_values = attend_backward(
        queries,
        keys,
        values,
        grad_heads.reshape(seq_len, width),
        attended,
        logsum,
        backward_start // QB,
        backward_number,
        heads_local,
    )
    grad_packed = jnp.concatenate([grad_query, grad_keys, grad_values], 1)
    grad_qkv = jnp.einsum("td,tc->dc", tokens_all, grad_packed, preferred_element_type=f32)
    by_shard = (
        grad_qkv.reshape(groups, shards, own, 3 * width)
        .transpose(1, 0, 2, 3)
        .reshape(shards, groups * own, 3 * width)
        .astype(bf16)
    )
    by_shard = lax.all_to_all(by_shard, "fsdp", split_axis=0, concat_axis=0, tiled=True)
    small = jnp.sum(by_shard.astype(f32), 0)
    owned_qkv = lax.all_to_all(
        small.reshape(groups, own, 3 * width), "sp", split_axis=0, concat_axis=0, tiled=True
    )
    owned_qkv = (
        owned_qkv.reshape(groups, own, 3, width).transpose(1, 2, 0, 3).reshape(own, 3 * model)
    )
    ones = jnp.ones((8, seq_len), bf16)
    bias_sums = jnp.dot(ones, grad_packed, preferred_element_type=f32)[0].reshape(3, shards, own)
    bias_sums = jnp.concatenate([bias_sums[0], bias_sums[2]], 1)
    bias_sums = lax.all_to_all(bias_sums, "fsdp", split_axis=0, concat_axis=0, tiled=True)
    bias_sums = jnp.sum(bias_sums, 0)
    grad_query_bias = bias_sums[:own]
    grad_value_bias = bias_sums[own:]
    partial_in = jnp.einsum("tc,dc->td", grad_packed, weights_qkv, preferred_element_type=f32)
    grad_input = grad_h1 + scatter_rows(partial_in)

    owned_down = reduced[:at]
    owned_up = reduced[at : 2 * at].reshape(ratio, own, model).transpose(1, 0, 2).reshape(own, hidden)
    owned_out = reduced[2 * at : 2 * at + own]
    flat = reduced[2 * at + own :].reshape(-1)
    pieces = []
    spot = 0
    for size in sizes:
        pieces.append(flat[spot : spot + size])
        spot += size
    grad_b_out, grad_g1, grad_s1, grad_b_down, grad_g2, grad_s2, grad_b_up = pieces
    return (
        output,
        grad_input,
        owned_qkv,
        grad_query_bias,
        grad_value_bias,
        owned_out,
        grad_b_out,
        grad_g1,
        grad_s1,
        owned_up,
        grad_b_up,
        owned_down,
        grad_b_down,
        grad_g2,
        grad_s2,
    )


def solution(mesh):
    in_specs = (
        P(("fsdp", "sp"), None),
        P("fsdp", None),
        P(("fsdp", "sp"), None),
        P(("sp", "fsdp"), None),
        P(("sp", "fsdp")),
        P(("sp", "fsdp")),
        P(("sp", "fsdp"), None),
        P(("sp", "fsdp")),
        P(("sp", "fsdp")),
        P(("sp", "fsdp")),
        P(("sp", "fsdp"), None),
        P(("sp", "fsdp")),
        P(("sp", "fsdp"), None),
        P(("sp", "fsdp")),
        P(("sp", "fsdp")),
        P(("sp", "fsdp")),
    )
    out_specs = (
        P(("fsdp", "sp"), None),
        P(("fsdp", "sp"), None),
        P(("sp", "fsdp"), None),
        P(("sp", "fsdp")),
        P(("sp", "fsdp")),
        P(("sp", "fsdp"), None),
        P(("sp", "fsdp")),
        P(("sp", "fsdp")),
        P(("sp", "fsdp")),
        P(("sp", "fsdp"), None),
        P(("sp", "fsdp")),
        P(("sp", "fsdp"), None),
        P(("sp", "fsdp")),
        P(("sp", "fsdp")),
        P(("sp", "fsdp")),
    )
    return jax.shard_map(body, mesh=mesh, in_specs=in_specs, out_specs=out_specs, check_vma=False)
```

```python
import jax
import jax.numpy as jnp
from jax import lax
from jax.experimental import pallas as pl
from jax.experimental.pallas import tpu as pltpu
from jax.sharding import PartitionSpec as P

HEADS = 12
HEAD = 64
IDS = 32
far = 1e30
FQ, FK = 512, 512
BQ, BK = 512, 256
ROWS = 256
f32 = jnp.float32
bf16 = jnp.bfloat16
norm_eps = 1e-06


def padded_width(width):
    return -(-(width + IDS) // 128) * 128


def spans(seg_row, block):
    seq = seg_row.shape[0]
    count = seq // block
    first = seg_row[::block]
    last = seg_row[block - 1 :: block]
    lo = jnp.sum((seg_row[None, :] < first[:, None]).astype(jnp.int32), 1)
    hi = jnp.sum((seg_row[None, :] <= last[:, None]).astype(jnp.int32), 1)
    return lo, hi


def windows(seg_row, block, step, grain):
    lo, hi = spans(seg_row, block)
    seq = seg_row.shape[0]
    start = lo // grain * grain
    number = -(-(hi - start) // step)
    start = jnp.minimum(start, seq - number * step)
    return start.astype(jnp.int32), number.astype(jnp.int32)


def lanes_of(head, shape):
    lane = lax.broadcasted_iota(jnp.int32, shape, len(shape) - 1)
    return (lane >= head * HEAD) & (lane < (head + 1) * HEAD)


def mm(a, b):
    return jnp.dot(a, b, preferred_element_type=f32)


def mm_nt(a, b):
    return lax.dot_general(a, b, (((1,), (1,)), ((), ())), preferred_element_type=f32)


def forward_kernel(heads, start_ref, number_ref, q_ref, k_ref, v_ref, o_ref, lse_ref, kh, vt, scores, acc):
    step = pl.program_id(0)
    seq, wide = k_ref.shape
    width = heads * HEAD
    tall = HEAD + 16

    @pl.when(step == 0)
    def _():
        row = lax.broadcasted_iota(jnp.int32, (16, FK), 0)
        ones = jnp.where(row == 0, 1.0, 0.0).astype(bf16)

        def part(i, carry):
            rows = pl.ds(pl.multiple_of(i * FK, FK), FK)
            k = k_ref[rows, :]
            lane = lax.broadcasted_iota(jnp.int32, k.shape, 1)
            turned = v_ref[rows, :].T
            for h in range(heads):
                keep = lanes_of(h, k.shape) | (lane >= width)
                kept = jnp.where(keep, k, jnp.zeros_like(k))
                for c in range(FK // 128):
                    at = pl.multiple_of(i * (FK * heads) + (c * heads + h) * 128, 128)
                    kh[pl.ds(at, 128), :] = kept[c * 128 : (c + 1) * 128]
                vt[h * tall : h * tall + HEAD, rows] = turned[h * HEAD : (h + 1) * HEAD]
                vt[h * tall + HEAD : (h + 1) * tall, rows] = ones
            return carry

        lax.fori_loop(0, seq // FK, part, 0)

    q = q_ref[...]
    start = start_ref[step]
    number = number_ref[step]

    def score(j, tops):
        at = pl.multiple_of((start + j * FK) * heads, 128)
        every = mm_nt(kh[pl.ds(at, FK * heads), :], q)
        news = list(tops)
        for c in range(FK // 128):
            for h in range(heads):
                s = every[(c * heads + h) * 128 : (c * heads + h + 1) * 128]
                scores[h, pl.ds(pl.multiple_of(j * FK + c * 128, 128), 128), :] = s
                news[h] = jnp.maximum(news[h], jnp.max(s.reshape(16, 8, FQ), 0))
        return tuple(news)

    tops = lax.fori_loop(0, number, score, (jnp.full((8, FQ), -jnp.inf, f32),) * heads)
    tops = [jnp.max(top, 0, keepdims=True) for top in tops]
    acc[...] = jnp.zeros_like(acc)

    def mix(j, carry):
        rows = pl.ds(pl.multiple_of(start + j * FK, 128), FK)
        out = pl.ds(pl.multiple_of(j * FK, FK), FK)
        for h in range(heads):
            p = jnp.exp(scores[h, out, :] - tops[h]).astype(bf16)
            acc[h] += mm(vt[h * tall : (h + 1) * tall, rows], p)
        return carry

    lax.fori_loop(0, number, mix, 0)
    outs = []
    for h in range(heads):
        total = acc[h, HEAD : HEAD + 1, :]
        outs.append(acc[h, :HEAD, :] / total)
        lse_ref[h : h + 1, :] = tops[h] + jnp.log(total)
    o_ref[...] = jnp.concatenate(outs, 0).T.astype(bf16)


def attend_forward(q, k, v, starts, numbers, heads):
    seq, wide = q.shape
    width = heads * HEAD
    steps = seq // FQ
    cost = pl.CostEstimate(
        flops=2 * heads * seq * seq * HEAD, bytes_accessed=8 * seq * wide, transcendentals=heads * seq * seq // 3
    )
    return pl.pallas_call(
        lambda *refs: forward_kernel(heads, *refs),
        grid_spec=pltpu.PrefetchScalarGridSpec(
            num_scalar_prefetch=2,
            grid=(steps,),
            in_specs=[
                pl.BlockSpec((FQ, wide), lambda i, a, b: (i, 0)),
                pl.BlockSpec((seq, wide), lambda i, a, b: (0, 0)),
                pl.BlockSpec((seq, width), lambda i, a, b: (0, 0)),
            ],
            out_specs=[
                pl.BlockSpec((FQ, width), lambda i, a, b: (i, 0)),
                pl.BlockSpec((8, FQ), lambda i, a, b: (0, i)),
            ],
            scratch_shapes=[
                pltpu.VMEM((heads * seq, wide), bf16),
                pltpu.VMEM((heads * (HEAD + 16), seq), bf16),
                pltpu.VMEM((heads, seq, FQ), f32),
                pltpu.VMEM((heads, HEAD + 16, FQ), f32),
            ],
        ),
        out_shape=[
            jax.ShapeDtypeStruct((seq, width), bf16),
            jax.ShapeDtypeStruct((8, seq), f32),
        ],
        cost_estimate=cost,
        compiler_params=pltpu.CompilerParams(vmem_limit_bytes=48 << 20),
        name="attend_forward",
    )(starts, numbers, q, k, v)


def backward_kernel(
    heads, start_ref, number_ref, q_ref, k_ref, v_ref, g_ref, o_ref, lse_ref,
    dq_ref, dk_ref, dv_ref, gq, qt, gt, dqt, delta, dkt, dvt, kh, vh,
):
    step = pl.program_id(0)
    seq, wide = q_ref.shape
    width = heads * HEAD

    @pl.when(step == 0)
    def _():
        def part(i, carry):
            rows = pl.ds(pl.multiple_of(i * 256, 256), 256)
            g = g_ref[rows, :]
            gq[rows, :] = jnp.concatenate([g, jnp.zeros((256, wide - width), bf16)], 1)
            qt[:, rows] = q_ref[rows, :].T[:width]
            gt[:, rows] = g.T
            product = g.astype(f32) * o_ref[rows, :].astype(f32)
            lane = lax.broadcasted_iota(jnp.int32, (8, width), 1)
            row = lax.broadcasted_iota(jnp.int32, (8, width), 0)
            pick = ((lane >= row * HEAD) & (lane < (row + 1) * HEAD)).astype(f32)
            delta[:, rows] = lax.dot_general(
                pick, product, (((1,), (1,)), ((), ())),
                preferred_element_type=f32, precision=lax.Precision.HIGHEST,
            )
            dqt[:, rows] = jnp.zeros((width, 256), f32)
            return carry

        lax.fori_loop(0, seq // 256, part, 0)

    start = start_ref[step]
    k = k_ref[...]
    v = v_ref[...]
    lane = lax.broadcasted_iota(jnp.int32, k.shape, 1)
    vz = jnp.concatenate([v, jnp.zeros((BK, wide - width), bf16)], 1)
    for h in range(heads):
        part = slice(h * BK, (h + 1) * BK)
        keep = lanes_of(h, k.shape)
        kh[part, :] = jnp.where(keep | (lane >= width), k, jnp.zeros_like(k))
        vh[part, :] = jnp.where(keep, vz, jnp.zeros_like(vz))
    kt = k.T
    dkt[...] = jnp.zeros_like(dkt)
    dvt[...] = jnp.zeros_like(dvt)

    def one(i, carry):
        rows = pl.ds(pl.multiple_of(start + i * BQ, 128), BQ)
        q = q_ref[rows, :]
        g = gq[rows, :]
        ss = mm_nt(kh[...], q)
        dps = mm_nt(vh[...], g)
        for h in range(heads):
            mine = slice(h * HEAD, (h + 1) * HEAD)
            part = slice(h * BK, (h + 1) * BK)
            p = jnp.exp(ss[part] - lse_ref[h : h + 1, rows])
            dp = dps[part]
            ds = (p * (dp - delta[h : h + 1, rows])).astype(bf16)
            dvt[mine, :] += mm_nt(gt[mine, rows], p.astype(bf16))
            dkt[mine, :] += mm_nt(qt[mine, rows], ds)
            dqt[mine, rows] += mm(kt[mine, :], ds)
        return carry

    lax.fori_loop(0, number_ref[step], one, 0)
    dk_ref[...] = dkt[...].T.astype(bf16)
    dv_ref[...] = dvt[...].T.astype(bf16)

    @pl.when(step == pl.num_programs(0) - 1)
    def _():
        def part(i, carry):
            rows = pl.ds(pl.multiple_of(i * 256, 256), 256)
            dq_ref[rows, :] = (dqt[:, rows] * 0.125).T.astype(bf16)
            return carry

        lax.fori_loop(0, seq // 256, part, 0)


def attend_backward(q, k, v, g, o, lse, starts, numbers, heads):
    seq, wide = q.shape
    width = heads * HEAD
    steps = seq // BK
    whole = lambda shape: pl.BlockSpec(shape, lambda i, a, b: (0, 0))
    cost = pl.CostEstimate(
        flops=5 * heads * seq * seq * HEAD, bytes_accessed=16 * seq * wide, transcendentals=heads * seq * seq // 3
    )
    return pl.pallas_call(
        lambda *refs: backward_kernel(heads, *refs),
        grid_spec=pltpu.PrefetchScalarGridSpec(
            num_scalar_prefetch=2,
            grid=(steps,),
            in_specs=[
                whole((seq, wide)),
                pl.BlockSpec((BK, wide), lambda i, a, b: (i, 0)),
                pl.BlockSpec((BK, width), lambda i, a, b: (i, 0)),
                whole((seq, width)),
                whole((seq, width)),
                whole((8, seq)),
            ],
            out_specs=[
                whole((seq, width)),
                pl.BlockSpec((BK, width), lambda i, a, b: (i, 0)),
                pl.BlockSpec((BK, width), lambda i, a, b: (i, 0)),
            ],
            scratch_shapes=[
                pltpu.VMEM((seq, wide), bf16),
                pltpu.VMEM((width, seq), bf16),
                pltpu.VMEM((width, seq), bf16),
                pltpu.VMEM((width, seq), f32),
                pltpu.VMEM((8, seq), f32),
                pltpu.VMEM((width, BK), f32),
                pltpu.VMEM((width, BK), f32),
                pltpu.VMEM((heads * BK, wide), bf16),
                pltpu.VMEM((heads * BK, wide), bf16),
            ],
        ),
        out_shape=[jax.ShapeDtypeStruct((seq, width), bf16)] * 3,
        cost_estimate=cost,
        compiler_params=pltpu.CompilerParams(vmem_limit_bytes=56 << 20),
        name="attend_backward",
    )(starts, numbers, q, k, v, g, o, lse)


def pack_kernel(ratio, down_ref, up_ref, out_ref, *refs):
    vectors, (packed_ref, rows_ref) = refs[:-2], refs[-2:]
    own, model = out_ref.shape
    at = ratio * own
    packed_ref[:at] = down_ref[...]
    for c in range(ratio):
        packed_ref[at + c * own : at + (c + 1) * own] = up_ref[:, c * model : (c + 1) * model]
    packed_ref[2 * at : 2 * at + own] = out_ref[...]
    rows_ref[...] = jnp.zeros_like(rows_ref)
    for j, vector in enumerate(vectors):
        rows_ref[j : j + 1, : vector.shape[1]] = vector[...].astype(f32)
    packed_ref[2 * at + own :] = rows_ref[...].astype(bf16)


def pack_weights(w_down, w_up, w_out, vectors):
    own, model = w_out.shape
    ratio = w_down.shape[0] // own
    if own % 8 == 0:
        return pl.pallas_call(
            lambda *refs: pack_kernel(ratio, *refs),
            out_shape=jax.ShapeDtypeStruct((own * (2 * ratio + 1) + 8, model), bf16),
            scratch_shapes=[pltpu.VMEM((8, model), f32)],
            name="pack_weights",
        )(w_down, w_up, w_out, *[item[None] for item in vectors])
    up_blocks = [w_up[:, c * model : (c + 1) * model] for c in range(ratio)]
    rows = [jnp.pad(item, (0, model - item.shape[0]))[None] for item in vectors]
    rows.append(jnp.zeros((8 - len(rows), model), bf16))
    return jnp.concatenate([w_down] + up_blocks + [w_out] + rows, 0)


def spread_kernel(groups, width, w_ref, q_ref, v_ref, out_ref, rows_ref):
    own = w_ref.shape[0]
    model = groups * width
    rows_ref[...] = jnp.zeros_like(rows_ref)
    rows_ref[0:1, :own] = q_ref[...].astype(f32)
    rows_ref[1:2, :own] = v_ref[...].astype(f32)
    biases = rows_ref[...].astype(bf16)
    for g in range(groups):
        parts = [w_ref[:, c * model + g * width : c * model + (g + 1) * width] for c in range(3)]
        block = jnp.concatenate(parts, 1)
        for i in range(out_ref.shape[1]):
            out_ref[g, i, :own, :] = block
            out_ref[g, i, own:, :] = biases


def spread_qkv(w_qkv, b_query, b_value, groups, shards):
    own = w_qkv.shape[0]
    width = w_qkv.shape[1] // (3 * groups)
    shape = (groups, shards, own + 8, 3 * width)
    if own % 8 == 0:
        return pl.pallas_call(
            lambda *refs: spread_kernel(groups, width, *refs),
            out_shape=jax.ShapeDtypeStruct(shape, bf16),
            scratch_shapes=[pltpu.VMEM((8, 3 * width), f32)],
            name="spread_qkv",
        )(w_qkv, b_query[None], b_value[None])
    block = w_qkv.reshape(own, 3, groups, width).transpose(2, 0, 1, 3).reshape(groups, own, 3 * width)
    rows = jnp.pad(jnp.stack([b_query, b_value]), ((0, 6), (0, 3 * width - own)))
    block = jnp.concatenate([block, jnp.broadcast_to(rows, (groups, 8, 3 * width))], 1)
    return jnp.broadcast_to(block[:, None], shape)


def project_kernel(
    heads, me_ref, x0_ref, x1_ref, x2_ref, upper_ref, lower_ref, seg_ref, w_ref, bias_ref,
    q_ref, k_ref, v_ref, all_ref, wide_w,
):
    step = pl.program_id(0)
    rows = x0_ref.shape[0]
    half = rows // 2
    width = heads * HEAD
    wide = q_ref.shape[1]
    slot = lax.bitwise_xor(step, me_ref[0])

    @pl.when(step == 0)
    def _():
        whole = w_ref[...].reshape(x0_ref.shape[1], 3 * width)
        for c in range(3):
            wide_w[c] = whole[:, c * width : (c + 1) * width]

    for k, part in ((0, x0_ref), (1, x1_ref), (2, x2_ref)):

        @pl.when(slot == k)
        def _():
            all_ref[...] = part[...]

    @pl.when(slot == 3)
    def _():
        all_ref[:half] = upper_ref[...]
        all_ref[half:] = lower_ref[...]

    size = 256

    def part(i, carry):
        at = pl.ds(pl.multiple_of(i * size, size), size)
        x = all_ref[at, :]
        lane = lax.broadcasted_iota(jnp.int32, (size, wide - width), 1)
        same = lane == seg_ref[at, :]
        q = (mm(x, wide_w[0]) + bias_ref[0:1, :width]).astype(bf16)
        q_ref[at, :width] = q * jnp.asarray(0.125, bf16)
        q_ref[at, width:] = jnp.where(same, 1.0, 0.0).astype(bf16)
        k_ref[at, :width] = mm(x, wide_w[1]).astype(bf16)
        k_ref[at, width:] = jnp.where(same, 0.0, -far).astype(bf16)
        v_ref[at, :] = (mm(x, wide_w[2]) + bias_ref[1:2, :width]).astype(bf16)
        return carry

    lax.fori_loop(0, rows // size, part, 0)


def project(blocks, seg_row, weights, biases, heads):
    own_rows, model = blocks[0].shape
    width = heads * HEAD
    wide = padded_width(width)
    seq = 4 * own_rows
    pieces = weights.shape[0]
    once = dict(pipeline_mode=pl.Buffered(1))
    fixed = lambda a: pl.BlockSpec(a, lambda s, m: (0,) * len(a), **once)
    cost = pl.CostEstimate(
        flops=6 * seq * model * width, bytes_accessed=4 * seq * (model + wide), transcendentals=0
    )
    return pl.pallas_call(
        lambda *refs: project_kernel(heads, *refs),
        grid_spec=pltpu.PrefetchScalarGridSpec(
            num_scalar_prefetch=1,
            grid=(4,),
            in_specs=[
                fixed((own_rows, model)),
                fixed((own_rows, model)),
                fixed((own_rows, model)),
                fixed((own_rows // 2, model)),
                fixed((own_rows // 2, model)),
                pl.BlockSpec((own_rows, 1), lambda s, m: (s, 0)),
                fixed((pieces, model // pieces, 3 * width)),
                fixed((8, width)),
            ],
            out_specs=[
                pl.BlockSpec((own_rows, wide), lambda s, m: (s, 0)),
                pl.BlockSpec((own_rows, wide), lambda s, m: (s, 0)),
                pl.BlockSpec((own_rows, width), lambda s, m: (s, 0)),
                pl.BlockSpec((own_rows, model), lambda s, m: (s, 0)),
            ],
            scratch_shapes=[pltpu.VMEM((3, model, width), bf16)],
        ),
        out_shape=[
            jax.ShapeDtypeStruct((seq, wide), bf16),
            jax.ShapeDtypeStruct((seq, wide), bf16),
            jax.ShapeDtypeStruct((seq, width), bf16),
            jax.ShapeDtypeStruct((seq, model), bf16),
        ],
        cost_estimate=cost,
        compiler_params=pltpu.CompilerParams(vmem_limit_bytes=40 << 20),
        name="project",
    )(lax.axis_index("sp").reshape(1).astype(jnp.int32), *blocks, seg_row[:, None], weights, biases)


def normal_rows(z):
    center = jnp.mean(z, -1, keepdims=True)
    moved = z - center
    rstd = lax.rsqrt(jnp.mean(moved * moved, -1, keepdims=True) + norm_eps)
    return moved * rstd, rstd


def norm_pull(s, hat, rstd):
    inner = jnp.mean(s * hat, -1, keepdims=True)
    return rstd * (s - jnp.mean(s, -1, keepdims=True) - hat * inner)


def gelu_both(x):
    z = jnp.abs(x) * 0.7071067811865476
    t = 1.0 / (1.0 + 0.3275911 * z)
    e = jnp.exp(-(z * z))
    poly = t * (
        0.127414796 + t * (-0.142248368 + t * (0.7107068705 + t * (-0.7265760135 + t * 0.5307027145)))
    )
    tail = poly * e
    cdf = jnp.where(x >= 0.0, 1.0 - tail, tail)
    return x * cdf, cdf + x * (e * 0.3989422804014327)


def spread_vectors(chunks, small_ref, vec_ref):
    pieces, _, model = small_ref.shape

    def spread(block, size):
        count = block.shape[0]
        lane = lax.broadcasted_iota(jnp.int32, (128, model), 1)
        row = lax.broadcasted_iota(jnp.int32, (128, model), 0)
        tile = jnp.where(lax.rem(lane, size) == row, 1.0, 0.0).astype(bf16)
        wide = mm(block, tile)
        lane = lax.broadcasted_iota(jnp.int32, (count, model), 1)
        row = lax.broadcasted_iota(jnp.int32, (count, model), 0)
        keep = lane // size == row
        return jnp.sum(jnp.where(keep, wide, 0.0), 0, keepdims=True)

    vec_ref[...] = jnp.zeros_like(vec_ref)
    for j in range(6):
        vec_ref[j : j + 1, :] = spread(small_ref[:, j, :128], model // pieces)
    share = pieces // chunks
    for c in range(chunks):
        block = small_ref[c * share : (c + 1) * share, 6, :128]
        vec_ref[8 + c : 9 + c, :] = spread(block, model // share)


def gather_vectors(chunks, vec_ref, wide_ref, small_ref):
    pieces, _, model = small_ref.shape
    wide_ref[...] = jnp.zeros_like(wide_ref)

    def gather(vector, size, count):
        lane = lax.broadcasted_iota(jnp.int32, (128, model), 1)
        row = lax.broadcasted_iota(jnp.int32, (128, model), 0)
        tile = jnp.where(lax.rem(lane, size) == row, 1.0, 0.0).astype(bf16)
        lane = lax.broadcasted_iota(jnp.int32, (count, model), 1)
        row = lax.broadcasted_iota(jnp.int32, (count, model), 0)
        kept = jnp.where(lane // size == row, vector, 0.0).astype(bf16)
        return mm_nt(kept, tile)

    for j in range(6):
        wide_ref[:, j, :128] = gather(vec_ref[j : j + 1, :], model // pieces, pieces)
    share = pieces // chunks
    for c in range(chunks):
        block = gather(vec_ref[8 + c : 9 + c, :], model // share, share)
        wide_ref[c * share : (c + 1) * share, 6, :128] = block
    small_ref[...] = wide_ref[...].astype(bf16)


def middle_kernel(
    groups, chunks, x_ref, cot_ref, mixed_ref, out_w_ref, up_ref, down_ref, small_ref,
    y_ref, gh1_ref, gmix_ref, sent_ref,
    first_low, first_t, hat1, rstd1, activ_t, slope, total, gffn, gpre, vec_ref,
    gvec_ref, gdown, gup, gout, gwide, gsmall, down_sem, up_sem, out_sem, small_sem,
):
    step = pl.program_id(0)
    rows, model = x_ref.shape
    parts = rows // ROWS
    width = mixed_ref.shape[2]

    def out_w(g):
        share = out_w_ref.shape[0] // groups
        return out_w_ref[g * share : (g + 1) * share].reshape(width, model)

    def up_w():
        return up_ref[...].reshape(model, model)

    def down_w():
        return down_ref[...].reshape(model, model)

    pieces, own = out_w_ref.shape[:2]
    share = pieces // groups

    def down_copy(slot, chunk):
        return pltpu.make_async_copy(
            gdown.at[slot], sent_ref.at[:, chunk, : chunks * own, :], down_sem.at[slot]
        )

    def up_copies(slot, chunk):
        at = pl.multiple_of((chunks + chunk) * own, 8)
        return [
            pltpu.make_async_copy(
                gup.at[slot, g * share : (g + 1) * share],
                sent_ref.at[:, g, pl.ds(at, own), :],
                up_sem.at[slot, g],
            )
            for g in range(groups)
        ]

    def out_copies():
        at = 2 * chunks * own
        return [
            pltpu.make_async_copy(
                gout.at[g * share : (g + 1) * share], sent_ref.at[:, g, at : at + own, :], out_sem.at[g]
            )
            for g in range(groups)
        ]

    def small_copies():
        at = 2 * chunks * own + own
        return [
            pltpu.make_async_copy(
                gsmall.at[g * share : (g + 1) * share], sent_ref.at[:, g, at : at + 8, :], small_sem.at[g]
            )
            for g in range(groups)
        ]

    def vec(i):
        return vec_ref[i : i + 1, :]

    def sums(value):
        return jnp.sum(value, 0, keepdims=True)

    @pl.when(step == 0)
    def _():
        gvec_ref[...] = jnp.zeros_like(gvec_ref)
        spread_vectors(chunks, small_ref, vec_ref)

        def part(i, carry):
            at = pl.ds(pl.multiple_of(i * ROWS, ROWS), ROWS)
            branch = vec(0)
            for g in range(groups):
                branch = branch + mm(mixed_ref[g, at, :], out_w(g))
            hat, rstd = normal_rows(x_ref[at, :].astype(f32) + branch)
            value = hat * vec(1) + vec(2)
            hat1[at, :] = hat
            rstd1[at, :] = jnp.broadcast_to(rstd, (ROWS, 128))
            low = value.astype(bf16)
            first_low[at, :] = low
            first_t[:, at] = low.T
            total[at, :] = value + vec(3)
            return carry

        lax.fori_loop(0, parts, part, 0)

    @pl.when(step < chunks)
    def _():
        def part(i, carry):
            at = pl.ds(pl.multiple_of(i * ROWS, ROWS), ROWS)
            pre = mm(first_low[at, :], up_w()) + vec_ref[pl.ds(8 + step, 1), :]
            value, pull = gelu_both(pre)
            low = value.astype(bf16)
            slope[step, at, :] = pull
            activ_t[step, :, at] = low.T
            total[at, :] += mm(low, down_w())
            return carry

        lax.fori_loop(0, parts, part, 0)

    @pl.when(step == chunks - 1)
    def _():
        def part(i, carry):
            at = pl.ds(pl.multiple_of(i * ROWS, ROWS), ROWS)
            hat, rstd = normal_rows(total[at, :])
            y_ref[at, :] = (hat * vec(4) + vec(5)).astype(bf16)
            g = cot_ref[at, :].astype(f32)
            gh2 = norm_pull(g * vec(4), hat, rstd)
            total[at, :] = gh2
            low = gh2.astype(bf16)
            gffn[at, :] = low
            gvec_ref[3:4, :] += sums(low.astype(f32))
            gvec_ref[4:5, :] += sums(g * hat)
            gvec_ref[5:6, :] += sums(g)
            return carry

        lax.fori_loop(0, parts, part, 0)

    @pl.when(step >= chunks)
    def _():
        chunk = 2 * chunks - 1 - step
        slot = lax.rem(step, 2)

        @pl.when(step >= chunks + 2)
        def _():
            down_copy(slot, chunk).wait()
            for copy in up_copies(slot, chunk):
                copy.wait()

        def part(i, carry):
            at = pl.ds(pl.multiple_of(i * ROWS, ROWS), ROWS)
            low = (mm_nt(gffn[at, :], down_w()) * slope[chunk, at, :]).astype(bf16)
            gpre[at, :] = low
            gvec_ref[pl.ds(8 + chunk, 1), :] += sums(low.astype(f32))
            total[at, :] += mm_nt(low, up_w())
            return carry

        lax.fori_loop(0, parts, part, 0)
        tall = 4 * chunks * own

        def weights_down(i, carry):
            at = pl.ds(pl.multiple_of(i * tall, tall), tall)
            value = mm(activ_t[chunk, at, :], gffn[...]).astype(bf16)
            gdown[slot, pl.ds(i * 4, 4)] = value.reshape(4, chunks * own, model)
            return carry

        lax.fori_loop(0, model // tall, weights_down, 0)
        down_copy(slot, chunk).start()
        high = 16 * own

        def weights_up(i, carry):
            at = pl.ds(pl.multiple_of(i * high, high), high)
            value = mm(first_t[at, :], gpre[...]).astype(bf16)
            gup[slot, pl.ds(i * 16, 16)] = value.reshape(16, own, model)
            return carry

        lax.fori_loop(0, model // high, weights_up, 0)
        for copy in up_copies(slot, chunk):
            copy.start()

    @pl.when(step == 2 * chunks - 1)
    def _():
        def part(i, carry):
            at = pl.ds(pl.multiple_of(i * ROWS, ROWS), ROWS)
            g = total[at, :]
            hat = hat1[at, :]
            gh1 = norm_pull(g * vec(1), hat, rstd1[at, :1])
            gh1_ref[at, :] = gh1
            low = gh1.astype(bf16)
            gpre[at, :] = low
            gvec_ref[0:1, :] += sums(low.astype(f32))
            gvec_ref[1:2, :] += sums(g * hat)
            gvec_ref[2:3, :] += sums(g)
            for k in range(groups):
                gmix_ref[k, at, :] = mm_nt(low, out_w(k)).astype(bf16)
            return carry

        lax.fori_loop(0, parts, part, 0)
        for k in range(groups):
            value = lax.dot_general(
                mixed_ref[k], gpre[...], (((0,), (0,)), ((), ())), preferred_element_type=f32
            ).astype(bf16)
            gout[k * share : (k + 1) * share] = value.reshape(share, own, model)
        for copy in out_copies():
            copy.start()
        gather_vectors(chunks, gvec_ref, gwide, gsmall)
        for copy in small_copies():
            copy.start()
        for back in range(2):
            down_copy(back, 0).wait()
            for copy in up_copies(back, 0):
                copy.wait()
        for copy in out_copies() + small_copies():
            copy.wait()


def middle(x, cot, mixed, packed):
    rows, model = x.shape
    groups, _, width = mixed.shape
    pieces = packed.shape[0]
    own = model // pieces
    chunks = (packed.shape[1] - 8 - own) // (2 * own)
    last = 2 * chunks - 1
    back = lambda s: jnp.minimum(s, last - s)
    assert chunks == groups and pieces % (8 * groups) == 0
    once = dict(pipeline_mode=pl.Buffered(1))
    fixed2 = lambda a: pl.BlockSpec(a, lambda s: (0, 0), **once)
    fixed3 = lambda a: pl.BlockSpec(a, lambda s: (0, 0, 0), **once)
    vectors_at = own * (2 * chunks + 1) // 8
    cost = pl.CostEstimate(
        flops=2 * rows * model * model * (3 + 6 * chunks),
        bytes_accessed=2 * model * model * (4 * chunks + 8),
        transcendentals=rows * model * chunks,
    )
    return pl.pallas_call(
        lambda *refs: middle_kernel(groups, chunks, *refs),
        grid=(2 * chunks,),
        in_specs=[
            fixed2((rows, model)),
            fixed2((rows, model)),
            fixed3((groups, rows, width)),
            pl.BlockSpec((pieces, own, model), lambda s: (0, 2 * chunks, 0), **once),
            pl.BlockSpec((pieces, own, model), lambda s: (0, chunks + back(s), 0)),
            pl.BlockSpec((pieces // chunks, chunks * own, model), lambda s: (back(s), 0, 0)),
            pl.BlockSpec((pieces, 8, model), lambda s: (0, vectors_at, 0), **once),
        ],
        out_specs=[
            fixed2((rows, model)),
            fixed2((rows, model)),
            fixed3((groups, rows, width)),
            pl.BlockSpec(memory_space=pl.ANY),
        ],
        out_shape=[
            jax.ShapeDtypeStruct((rows, model), bf16),
            jax.ShapeDtypeStruct((rows, model), f32),
            jax.ShapeDtypeStruct((groups, rows, width), bf16),
            jax.ShapeDtypeStruct((pieces // groups, groups, packed.shape[1], model), bf16),
        ],
        scratch_shapes=[
            pltpu.VMEM((rows, model), bf16),
            pltpu.VMEM((model, rows), bf16),
            pltpu.VMEM((rows, model), f32),
            pltpu.VMEM((rows, 128), f32),
            pltpu.VMEM((chunks, model, rows), bf16),
            pltpu.VMEM((chunks, rows, model), f32),
            pltpu.VMEM((rows, model), f32),
            pltpu.VMEM((rows, model), bf16),
            pltpu.VMEM((rows, model), bf16),
            pltpu.VMEM((16, model), f32),
            pltpu.VMEM((16, model), f32),
            pltpu.VMEM((2, pieces // chunks, chunks * own, model), bf16),
            pltpu.VMEM((2, pieces, own, model), bf16),
            pltpu.VMEM((pieces, own, model), bf16),
            pltpu.VMEM((pieces, 8, model), f32),
            pltpu.VMEM((pieces, 8, model), bf16),
            pltpu.SemaphoreType.DMA((2,)),
            pltpu.SemaphoreType.DMA((2, groups)),
            pltpu.SemaphoreType.DMA((groups,)),
            pltpu.SemaphoreType.DMA((groups,)),
        ],
        cost_estimate=cost,
        compiler_params=pltpu.CompilerParams(vmem_limit_bytes=60 << 20),
        name="middle",
    )(x, cot, mixed, packed, packed, packed, packed)


def by_sp(value, flip):
    groups = lax.axis_size("sp")
    return lax.ppermute(value, "sp", [(i, i ^ flip) for i in range(groups)])


def gather_tokens(tokens):
    half = tokens.shape[0] // 2
    along_x = by_sp(tokens, 1)
    along_y = by_sp(tokens, 2)
    upper = by_sp(along_y[:half], 1)
    lower = by_sp(along_x[half:], 2)
    return tokens, along_x, along_y, upper, lower


def scatter_rows(partial):
    rows = partial.shape[0] // 4
    half = rows // 2
    me = lax.axis_index("sp")

    def piece(flip, lower):
        at = (me ^ flip) * rows + (half if lower else 0)
        return lax.dynamic_slice(partial, (at, 0), (half, partial.shape[1]))

    sent_x = jnp.concatenate([piece(1, False), piece(3, False)], 0).astype(bf16)
    sent_y = jnp.concatenate([piece(2, True), piece(3, True)], 0).astype(bf16)
    got_x = by_sp(sent_x, 1).astype(f32)
    got_y = by_sp(sent_y, 2).astype(f32)
    next_y = by_sp((piece(2, False) + got_x[half:]).astype(bf16), 2).astype(f32)
    next_x = by_sp((piece(1, True) + got_y[half:]).astype(bf16), 1).astype(f32)
    upper = piece(0, False) + got_x[:half] + next_y
    lower = piece(0, True) + got_y[:half] + next_x
    return jnp.concatenate([upper, lower], 0)


def unpack(packed, ratio):
    pieces, _, model = packed.shape
    own = model // pieces
    at = ratio * own
    down = packed[:, :at].reshape(ratio * model, model)
    up = packed[:, at : 2 * at].reshape(pieces, ratio, own, model).transpose(1, 0, 2, 3)
    out = packed[:, 2 * at : 2 * at + own].reshape(model, model)
    vectors = [packed[:, 2 * at + own + j, :own].reshape(-1) for j in range(6)]
    vectors.append(packed[:, 2 * at + own + 6, :at].reshape(-1))
    return down, up.reshape(ratio, model, model), out, vectors


def repack(packed, ratio, pieces):
    if packed.shape[0] == pieces:
        return packed
    down, up, out, vectors = unpack(packed, ratio)
    model = out.shape[0]
    own = model // pieces
    up = up.reshape(ratio, pieces, own, model).transpose(1, 0, 2, 3)
    rows = [jnp.pad(v.reshape(pieces, -1), ((0, 0), (0, model - v.shape[0] // pieces))) for v in vectors]
    rows.append(jnp.zeros_like(rows[0]))
    return jnp.concatenate(
        [
            down.reshape(pieces, ratio * own, model),
            up.reshape(pieces, ratio * own, model),
            out.reshape(pieces, own, model),
            jnp.stack(rows, 1),
        ],
        1,
    )


def body(
    tokens,
    segments,
    cotangent,
    w_qkv,
    b_query,
    b_value,
    w_out,
    b_out,
    ln1_gain,
    ln1_bias,
    w_up,
    b_up,
    w_down,
    b_down,
    ln2_gain,
    ln2_bias,
):
    both = ("sp", "fsdp")
    groups = lax.axis_size("sp")
    shards = lax.axis_size("fsdp")
    devices = groups * shards
    rows, model = tokens.shape
    hidden = w_up.shape[1]
    ratio = hidden // model
    own = w_qkv.shape[0]
    pieces = devices if own % 8 == 0 else 8 * groups
    heads_local = HEADS // groups
    width = heads_local * HEAD
    seq_len = rows * groups
    seg_row = segments[0]

    blocks = gather_tokens(tokens)
    pack = pack_weights(
        w_down, w_up, w_out, [b_out, ln1_gain, ln1_bias, b_down, ln2_gain, ln2_bias, b_up]
    )
    packed_weights = repack(lax.all_gather(pack, both, axis=0, tiled=False), ratio, pieces)

    by_device = spread_qkv(w_qkv, b_query, b_value, groups, shards)
    arrived = lax.all_to_all(
        by_device.reshape(devices, own + 8, 3 * width), both, split_axis=0, concat_axis=0, tiled=True
    )
    bias_rows = lax.dynamic_slice(
        arrived, (lax.axis_index("sp") * shards, own, 0), (shards, 2, own)
    )
    bias_rows = bias_rows.transpose(1, 0, 2).reshape(2, width).astype(f32)
    bias_rows = jnp.pad(bias_rows, ((0, 6), (0, 0)))
    weights = arrived if own % 8 == 0 else arrived[:, :own].reshape(pieces, model // pieces, 3 * width)
    queries, keys, values, tokens_all = project(blocks, seg_row, weights, bias_rows, heads_local)
    forward_start, forward_number = windows(seg_row, FQ, FK, 128)
    backward_start, backward_number = windows(seg_row, BK, BQ, 128)
    attended, logsum = attend_forward(
        queries, keys, values, forward_start, forward_number, heads_local
    )
    mixed = lax.all_to_all(
        attended.reshape(groups, rows, width), "sp", split_axis=0, concat_axis=0, tiled=True
    )
    output, grad_h1, grad_mixed, sent = middle(tokens, cotangent, mixed, packed_weights)

    lines = sent.shape[2]
    if pieces != devices:
        sent = sent.transpose(1, 0, 2, 3).reshape(pieces, lines, model)
        sent = repack(sent, ratio, devices)
        lines = sent.shape[1]
        sent = sent.reshape(groups, shards, lines, model).transpose(1, 0, 2, 3)
    reduced = lax.psum_scatter(
        sent.reshape(devices * lines, model), "fsdp", scatter_dimension=0, tiled=True
    )
    reduced = lax.all_to_all(
        reduced.reshape(groups, lines, model), "sp", split_axis=0, concat_axis=0, tiled=True
    )
    reduced = jnp.sum(reduced.astype(f32), 0)

    grad_heads = lax.all_to_all(grad_mixed, "sp", split_axis=0, concat_axis=0, tiled=True)
    grad_query, grad_keys, grad_values = attend_backward(
        queries,
        keys,
        values,
        grad_heads.reshape(seq_len, width),
        attended,
        logsum,
        backward_start,
        backward_number,
        heads_local,
    )
    grad_packed = jnp.concatenate([grad_query, grad_keys, grad_values], 1)
    weights_qkv = arrived[:, :own].reshape(model, 3 * width)
    extra = 8
    partial_in = jnp.einsum("tc,dc->td", grad_packed, weights_qkv, preferred_element_type=f32)
    grad_input = grad_h1 + scatter_rows(partial_in)

    grad_qkv = jnp.einsum("td,tc->dc", tokens_all, grad_packed, preferred_element_type=f32)
    ones = jnp.ones((8, seq_len), bf16)
    bias_sums = jnp.dot(ones, grad_packed, preferred_element_type=f32)[0].reshape(3, shards, own)
    bias_sums = jnp.concatenate([bias_sums[0], bias_sums[2]], 1).astype(bf16)
    bias_sums = jnp.pad(bias_sums[:, None], ((0, 0), (0, extra - 1), (0, 3 * width - 2 * own)))
    bias_sums = jnp.broadcast_to(bias_sums[None], (groups, shards, extra, 3 * width))
    by_owner = jnp.concatenate(
        [
            grad_qkv.astype(bf16).reshape(devices, own, 3 * width),
            bias_sums.reshape(devices, extra, 3 * width),
        ],
        1,
    )
    by_owner = lax.all_to_all(by_owner, both, split_axis=0, concat_axis=0, tiled=True)
    by_owner = by_owner.reshape(groups, shards, own + extra, 3 * width).astype(f32)
    by_owner = jnp.sum(by_owner, 1)
    owned_qkv = by_owner[:, :own].reshape(groups, own, 3, width).transpose(1, 2, 0, 3)
    owned_qkv = owned_qkv.reshape(own, 3 * model)
    bias_sums = lax.dynamic_slice(
        by_owner, (lax.axis_index("sp"), own, 0), (1, 1, 3 * width)
    ).reshape(-1)
    grad_query_bias = bias_sums[:own]
    grad_value_bias = bias_sums[own : 2 * own]

    at = ratio * own
    owned_up = reduced[at : 2 * at].reshape(ratio, own, model).transpose(1, 0, 2).reshape(own, hidden)
    tail = reduced[2 * at + own :]
    return (
        output,
        grad_input,
        owned_qkv,
        grad_query_bias,
        grad_value_bias,
        reduced[2 * at : 2 * at + own],
        tail[0, :own],
        tail[1, :own],
        tail[2, :own],
        owned_up,
        tail[6, :at],
        reduced[:at],
        tail[3, :own],
        tail[4, :own],
        tail[5, :own],
    )


def solution(mesh):
    in_specs = (
        P(("fsdp", "sp"), None),
        P("fsdp", None),
        P(("fsdp", "sp"), None),
        P(("sp", "fsdp"), None),
        P(("sp", "fsdp")),
        P(("sp", "fsdp")),
        P(("sp", "fsdp"), None),
        P(("sp", "fsdp")),
        P(("sp", "fsdp")),
        P(("sp", "fsdp")),
        P(("sp", "fsdp"), None),
        P(("sp", "fsdp")),
        P(("sp", "fsdp"), None),
        P(("sp", "fsdp")),
        P(("sp", "fsdp")),
        P(("sp", "fsdp")),
    )
    out_specs = (
        P(("fsdp", "sp"), None),
        P(("fsdp", "sp"), None),
        P(("sp", "fsdp"), None),
        P(("sp", "fsdp")),
        P(("sp", "fsdp")),
        P(("sp", "fsdp"), None),
        P(("sp", "fsdp")),
        P(("sp", "fsdp")),
        P(("sp", "fsdp")),
        P(("sp", "fsdp"), None),
        P(("sp", "fsdp")),
        P(("sp", "fsdp"), None),
        P(("sp", "fsdp")),
        P(("sp", "fsdp")),
        P(("sp", "fsdp")),
    )
    return jax.shard_map(body, mesh=mesh, in_specs=in_specs, out_specs=out_specs, check_vma=False)
```

```python
import jax
import jax.numpy as jnp
from jax import lax
from jax.experimental import pallas as pl
from jax.experimental.pallas import tpu as pltpu
from jax.sharding import PartitionSpec as P

HEADS = 12
HEAD = 64
IDS = 32
far = 1e30
FQ, FK = 512, 512
BQ, BK = 512, 256
ROWS = 384
f32 = jnp.float32
bf16 = jnp.bfloat16
norm_eps = 1e-06


def padded_width(width):
    return -(-(width + IDS) // 128) * 128


def spans(seg_row, block):
    seq = seg_row.shape[0]
    count = seq // block
    first = seg_row[::block]
    last = seg_row[block - 1 :: block]
    lo = jnp.sum((seg_row[None, :] < first[:, None]).astype(jnp.int32), 1)
    hi = jnp.sum((seg_row[None, :] <= last[:, None]).astype(jnp.int32), 1)
    return lo, hi


def windows(seg_row, block, step, grain):
    lo, hi = spans(seg_row, block)
    seq = seg_row.shape[0]
    start = lo // grain * grain
    number = -(-(hi - start) // step)
    start = jnp.minimum(start, seq - number * step)
    return start.astype(jnp.int32), number.astype(jnp.int32)


def lanes_of(head, shape):
    lane = lax.broadcasted_iota(jnp.int32, shape, len(shape) - 1)
    return (lane >= head * HEAD) & (lane < (head + 1) * HEAD)


def mm(a, b):
    return jnp.dot(a, b, preferred_element_type=f32)


def mm_nt(a, b):
    return lax.dot_general(a, b, (((1,), (1,)), ((), ())), preferred_element_type=f32)


def mm_tn(a, b):
    return lax.dot_general(a, b, (((0,), (0,)), ((), ())), preferred_element_type=f32)


def forward_kernel(
    heads, start_ref, number_ref, me_ref, q_ref, k_ref, v_ref,
    o0_ref, o1_ref, o2_ref, o3_ref, lse_ref, kh, vt, scores, acc,
):
    step = pl.program_id(0)
    seq, wide = k_ref.shape
    width = heads * HEAD
    tall = HEAD + 16

    @pl.when(step == 0)
    def _():
        row = lax.broadcasted_iota(jnp.int32, (16, FK), 0)
        ones = jnp.where(row == 0, 1.0, 0.0).astype(bf16)

        def part(i, carry):
            rows = pl.ds(pl.multiple_of(i * FK, FK), FK)
            k = k_ref[rows, :]
            lane = lax.broadcasted_iota(jnp.int32, k.shape, 1)
            turned = v_ref[rows, :].T
            for h in range(heads):
                keep = lanes_of(h, k.shape) | (lane >= width)
                kept = jnp.where(keep, k, jnp.zeros_like(k))
                for c in range(FK // 128):
                    at = pl.multiple_of(i * (FK * heads) + (c * heads + h) * 128, 128)
                    kh[pl.ds(at, 128), :] = kept[c * 128 : (c + 1) * 128]
                vt[h * tall : h * tall + HEAD, rows] = turned[h * HEAD : (h + 1) * HEAD]
                vt[h * tall + HEAD : (h + 1) * tall, rows] = ones
            return carry

        lax.fori_loop(0, seq // FK, part, 0)

    q = q_ref[...]
    start = start_ref[step]
    number = number_ref[step]

    def score(j, tops):
        at = pl.multiple_of((start + j * FK) * heads, 128)
        every = mm_nt(kh[pl.ds(at, FK * heads), :], q)
        news = list(tops)
        for c in range(FK // 128):
            for h in range(heads):
                s = every[(c * heads + h) * 128 : (c * heads + h + 1) * 128]
                scores[h, pl.ds(pl.multiple_of(j * FK + c * 128, 128), 128), :] = s
                news[h] = jnp.maximum(news[h], jnp.max(s.reshape(16, 8, FQ), 0))
        return tuple(news)

    tops = lax.fori_loop(0, number, score, (jnp.full((8, FQ), -jnp.inf, f32),) * heads)
    tops = [jnp.max(top, 0, keepdims=True) for top in tops]
    acc[...] = jnp.zeros_like(acc)

    def mix(j, carry):
        rows = pl.ds(pl.multiple_of(start + j * FK, 128), FK)
        out = pl.ds(pl.multiple_of(j * FK, FK), FK)
        for h in range(heads):
            p = jnp.exp(scores[h, out, :] - tops[h]).astype(bf16)
            acc[h] += mm(vt[h * tall : (h + 1) * tall, rows], p)
        return carry

    lax.fori_loop(0, number, mix, 0)
    outs = []
    for h in range(heads):
        total = acc[h, HEAD : HEAD + 1, :]
        outs.append(acc[h, :HEAD, :] / total)
        lse_ref[h : h + 1, :] = tops[h] + jnp.log(total)
    mixed = jnp.concatenate(outs, 0).astype(bf16)
    per = o0_ref.shape[1] // 256
    for u in range(FQ // 256):
        block = step * (FQ // 256) + u
        at = pl.ds(pl.multiple_of(lax.rem(block, per) * 256, 256), 256)
        slot = lax.bitwise_xor(block // per, me_ref[0])
        for r, out_ref in enumerate((o0_ref, o1_ref, o2_ref, o3_ref)):

            @pl.when(slot == r)
            def _():
                out_ref[:, at] = mixed[:, u * 256 : (u + 1) * 256]


def attend_forward(q, k, v, starts, numbers, me, heads):
    seq, wide = q.shape
    width = heads * HEAD
    steps = seq // FQ
    cost = pl.CostEstimate(
        flops=2 * heads * seq * seq * HEAD, bytes_accessed=8 * seq * wide, transcendentals=heads * seq * seq // 3
    )
    return pl.pallas_call(
        lambda *refs: forward_kernel(heads, *refs),
        grid_spec=pltpu.PrefetchScalarGridSpec(
            num_scalar_prefetch=3,
            grid=(steps,),
            in_specs=[
                pl.BlockSpec((FQ, wide), lambda i, a, b, m: (i, 0)),
                pl.BlockSpec((seq, wide), lambda i, a, b, m: (0, 0)),
                pl.BlockSpec((seq, width), lambda i, a, b, m: (0, 0)),
            ],
            out_specs=[
                pl.BlockSpec((width, seq // 4), lambda i, a, b, m: (0, 0)),
                pl.BlockSpec((width, seq // 4), lambda i, a, b, m: (0, 0)),
                pl.BlockSpec((width, seq // 4), lambda i, a, b, m: (0, 0)),
                pl.BlockSpec((width, seq // 4), lambda i, a, b, m: (0, 0)),
                pl.BlockSpec((8, FQ), lambda i, a, b, m: (0, i)),
            ],
            scratch_shapes=[
                pltpu.VMEM((heads * seq, wide), bf16),
                pltpu.VMEM((heads * (HEAD + 16), seq), bf16),
                pltpu.VMEM((heads, seq, FQ), f32),
                pltpu.VMEM((heads, HEAD + 16, FQ), f32),
            ],
        ),
        out_shape=[
            jax.ShapeDtypeStruct((width, seq // 4), bf16),
            jax.ShapeDtypeStruct((width, seq // 4), bf16),
            jax.ShapeDtypeStruct((width, seq // 4), bf16),
            jax.ShapeDtypeStruct((width, seq // 4), bf16),
            jax.ShapeDtypeStruct((8, seq), f32),
        ],
        cost_estimate=cost,
        compiler_params=pltpu.CompilerParams(vmem_limit_bytes=48 << 20),
        name="attend_forward",
    )(starts, numbers, me, q, k, v)


def backward_kernel(
    heads, start_ref, number_ref, me_ref, q_ref, k_ref, v_ref,
    g0_ref, g1_ref, g2_ref, g3_ref, o0_ref, o1_ref, o2_ref, o3_ref, lse_ref, x_ref, w_ref, gh1_ref,
    sx_ref, sy_ref, mine_ref, low_ref, up_ref, kept_ref, sent_ref,
    qt, gt, dqt, delta, dkt, dvt, kh, vh, turned, grads, rows_ref,
):
    step = pl.program_id(0)
    seq, wide = q_ref.shape
    width = heads * HEAD
    own_rows = seq // 4
    per = own_rows // 256
    me = me_ref[0]

    @pl.when(step == 0)
    def _():
        def part(i, carry):
            rows = pl.ds(pl.multiple_of(i * 256, 256), 256)
            at = pl.ds(pl.multiple_of(lax.rem(i, per) * 256, 256), 256)
            slot = lax.bitwise_xor(i // per, me)
            qt[:, rows] = q_ref[rows, :].T[:width]
            dqt[:, rows] = jnp.zeros((width, 256), f32)
            pairs = ((g0_ref, o0_ref), (g1_ref, o1_ref), (g2_ref, o2_ref), (g3_ref, o3_ref))
            for r, (g_ref, o_ref) in enumerate(pairs):

                @pl.when(slot == r)
                def _():
                    g = g_ref[:, at]
                    gt[:, rows] = g
                    product = g.astype(f32) * o_ref[:, at].astype(f32)
                    for h in range(heads):
                        mine = slice(h * HEAD, (h + 1) * HEAD)
                        delta[h : h + 1, rows] = jnp.sum(product[mine], 0, keepdims=True)

            return carry

        lax.fori_loop(0, seq // 256, part, 0)

    start = start_ref[step]
    k = k_ref[...]
    v = v_ref[...]
    lane = lax.broadcasted_iota(jnp.int32, k.shape, 1)
    for h in range(heads):
        part = slice(h * BK, (h + 1) * BK)
        kh[part, :] = jnp.where(lanes_of(h, k.shape) | (lane >= width), k, jnp.zeros_like(k))
        vh[part, :] = jnp.where(lanes_of(h, v.shape), v, jnp.zeros_like(v))
    kt = k.T
    dkt[...] = jnp.zeros_like(dkt)
    dvt[...] = jnp.zeros_like(dvt)

    def one(i, carry):
        rows = pl.ds(pl.multiple_of(start + i * BQ, 128), BQ)
        q = q_ref[rows, :]
        ss = mm_nt(kh[...], q)
        dps = mm(vh[...], gt[:, rows])
        for h in range(heads):
            mine = slice(h * HEAD, (h + 1) * HEAD)
            part = slice(h * BK, (h + 1) * BK)
            p = jnp.exp(ss[part] - lse_ref[h : h + 1, rows])
            dp = dps[part]
            ds = (p * (dp - delta[h : h + 1, rows])).astype(bf16)
            dvt[mine, :] += mm_nt(gt[mine, rows], p.astype(bf16))
            dkt[mine, :] += mm_nt(qt[mine, rows], ds)
            dqt[mine, rows] += mm(kt[mine, :], ds)
        return carry

    lax.fori_loop(0, number_ref[step], one, 0)
    here = pl.ds(pl.multiple_of(step * BK, BK), BK)
    for c, total in ((1, dkt), (2, dvt)):
        low = total[...].astype(bf16)
        turned[c * width : (c + 1) * width, here] = low
        grads[c, here, :] = low.T

    @pl.when(step == pl.num_programs(0) - 1)
    def _():
        def part(i, carry):
            rows = pl.ds(pl.multiple_of(i * 256, 256), 256)
            low = (dqt[:, rows] * 0.125).astype(bf16)
            turned[:width, rows] = low
            grads[0, rows, :] = low.T
            return carry

        lax.fori_loop(0, seq // 256, part, 0)
        half = own_rows // 2

        def back(i, carry):
            def rows_of(lower):
                at = pl.ds(pl.multiple_of(i * own_rows + lower * half, 128), half)
                value = mm_nt(grads[0, at, :], w_ref[0])
                value = value + mm_nt(grads[1, at, :], w_ref[1])
                return value + mm_nt(grads[2, at, :], w_ref[2])

            slot = lax.bitwise_xor(i, me)
            for lower in range(2):
                value = rows_of(lower)
                here = slice(lower * half, (lower + 1) * half)

                @pl.when(slot == 0)
                def _():
                    mine_ref[here, :] = value + gh1_ref[here, :]

                @pl.when(slot == 1)
                def _():
                    if lower:
                        low_ref[...] = value
                    else:
                        sx_ref[:half] = value.astype(bf16)

                @pl.when(slot == 2)
                def _():
                    if lower:
                        sy_ref[:half] = value.astype(bf16)
                    else:
                        up_ref[...] = value

                @pl.when(slot == 3)
                def _():
                    if lower:
                        sy_ref[half:] = value.astype(bf16)
                    else:
                        sx_ref[half:] = value.astype(bf16)

            return carry

        lax.fori_loop(0, 4, back, 0)
        model = x_ref.shape[1]
        columns, _, own = kept_ref.shape[:3]
        shards = 2 * columns
        lane = lax.broadcasted_iota(jnp.int32, (128, width), 1)
        row = lax.broadcasted_iota(jnp.int32, (128, width), 0)
        tile = jnp.where(lax.rem(lane, own) == row, 1.0, 0.0).astype(bf16)
        lane = lax.broadcasted_iota(jnp.int32, (shards, width), 1)
        row = lax.broadcasted_iota(jnp.int32, (shards, width), 0)
        ones = jnp.ones((8, seq), bf16)
        rows_ref[...] = jnp.zeros_like(rows_ref)
        for j, c in enumerate((0, 2)):
            sums = mm(ones, grads[c])[:1]
            rows_ref[:, j, :] = mm_nt(jnp.where(lane // own == row, sums, 0.0).astype(bf16), tile)
        value = mm(turned[...], x_ref[...]).T.astype(bf16).reshape(4 * shards, own, 3 * width)
        for core in range(2):

            @pl.when(me_ref[3] == core)
            def _():
                for piece in range(4 * shards):
                    group, shard = piece // shards, piece % shards
                    target = kept_ref if shard % 2 == core else sent_ref
                    z = lax.bitwise_xor(me_ref[2], shard // 2)
                    r = lax.bitwise_xor(me_ref[1], group)
                    target[z, r, :, : 3 * width] = value[piece]
                    target[z, r, :, 3 * width :] = jnp.zeros((own, model - 3 * width), bf16)
                    target[z, r, :8, model - 128 :] = rows_ref[shard].astype(bf16)


def attend_backward(q, k, v, g, o, lse, starts, numbers, place, x, w, gh1, pieces, heads):
    seq, wide = q.shape
    width = heads * HEAD
    steps = seq // BK
    own_rows, model = gh1.shape
    own = model // pieces
    once = dict(pipeline_mode=pl.Buffered(1))
    whole = lambda a: pl.BlockSpec(a, lambda i, a_, b_, m_: (0,) * len(a), **once)
    cost = pl.CostEstimate(
        flops=5 * heads * seq * seq * HEAD + 12 * seq * model * width,
        bytes_accessed=16 * seq * wide,
        transcendentals=heads * seq * seq // 3,
    )
    return pl.pallas_call(
        lambda *refs: backward_kernel(heads, *refs),
        grid_spec=pltpu.PrefetchScalarGridSpec(
            num_scalar_prefetch=3,
            grid=(steps,),
            in_specs=[
                whole((seq, wide)),
                pl.BlockSpec((BK, wide), lambda i, a, b, m: (i, 0)),
                pl.BlockSpec((BK, width), lambda i, a, b, m: (i, 0)),
            ]
            + [whole((width, own_rows))] * 8
            + [whole((8, seq)), whole((seq, model)), whole((3, model, width)), whole((own_rows, model))],
            out_specs=[
                whole((own_rows, model)),
                whole((own_rows, model)),
                whole((own_rows, model)),
                whole((own_rows // 2, model)),
                whole((own_rows // 2, model)),
                whole((pieces // 8, 4, own, model)),
                whole((pieces // 8, 4, own, model)),
            ],
            scratch_shapes=[
                pltpu.VMEM((width, seq), bf16),
                pltpu.VMEM((width, seq), bf16),
                pltpu.VMEM((width, seq), f32),
                pltpu.VMEM((8, seq), f32),
                pltpu.VMEM((width, BK), f32),
                pltpu.VMEM((width, BK), f32),
                pltpu.VMEM((heads * BK, wide), bf16),
                pltpu.VMEM((heads * BK, width), bf16),
                pltpu.VMEM((3 * width, seq), bf16),
                pltpu.VMEM((3, seq, width), bf16),
                pltpu.VMEM((pieces // 4, 8, 128), f32),
            ],
        ),
        out_shape=[
            jax.ShapeDtypeStruct((own_rows, model), bf16),
            jax.ShapeDtypeStruct((own_rows, model), bf16),
            jax.ShapeDtypeStruct((own_rows, model), f32),
            jax.ShapeDtypeStruct((own_rows // 2, model), f32),
            jax.ShapeDtypeStruct((own_rows // 2, model), f32),
            jax.ShapeDtypeStruct((pieces // 8, 4, own, model), bf16),
            jax.ShapeDtypeStruct((pieces // 8, 4, own, model), bf16),
        ],
        cost_estimate=cost,
        compiler_params=pltpu.CompilerParams(vmem_limit_bytes=60 << 20),
        name="attend_backward",
    )(starts, numbers, place, q, k, v, *g, *o, lse, x, w, gh1)


def pack_kernel(ratio, groups, me_ref, down_ref, up_ref, out_ref, qkv_ref, *refs):
    vectors, (query_ref, value_ref, packed_ref, spread_ref, rows_ref) = refs[:-5], refs[-5:]
    own, model = out_ref.shape
    width = model // groups
    rows_ref[...] = jnp.zeros_like(rows_ref)
    rows_ref[0:1, :own] = query_ref[...].astype(f32)
    rows_ref[1:2, :own] = value_ref[...].astype(f32)
    biases = rows_ref[:, : 3 * width].astype(bf16)
    for g in range(groups):
        parts = [qkv_ref[:, c * model + g * width : c * model + (g + 1) * width] for c in range(3)]
        slot = lax.bitwise_xor(me_ref[0], g)
        spread_ref[slot, :own, :] = jnp.concatenate(parts, 1)
        spread_ref[slot, own:, :] = biases
    at = ratio * own
    packed_ref[:at] = down_ref[...]
    for c in range(ratio):
        packed_ref[at + c * own : at + (c + 1) * own] = up_ref[:, c * model : (c + 1) * model]
    packed_ref[2 * at : 2 * at + own] = out_ref[...]
    rows_ref[...] = jnp.zeros_like(rows_ref)
    for j, vector in enumerate(vectors):
        rows_ref[j : j + 1, : vector.shape[1]] = vector[...].astype(f32)
    packed_ref[2 * at + own :] = rows_ref[...].astype(bf16)


def pack(me, w_down, w_up, w_out, w_qkv, vectors, b_query, b_value, groups):
    own, model = w_out.shape
    ratio = w_down.shape[0] // own
    width = model // groups
    vmem = pl.BlockSpec(memory_space=pltpu.VMEM)
    return pl.pallas_call(
        lambda *refs: pack_kernel(ratio, groups, *refs),
        in_specs=[pl.BlockSpec(memory_space=pltpu.SMEM)] + [vmem] * (6 + len(vectors)),
        out_shape=[
            jax.ShapeDtypeStruct((own * (2 * ratio + 1) + 8, model), bf16),
            jax.ShapeDtypeStruct((groups, own + 8, 3 * width), bf16),
        ],
        scratch_shapes=[pltpu.VMEM((8, model), f32)],
        name="pack",
    )(me, w_down, w_up, w_out, w_qkv, *[item[None] for item in vectors], b_query[None], b_value[None])


def pack_plain(w_down, w_up, w_out, w_qkv, vectors, b_query, b_value, groups):
    own, model = w_out.shape
    ratio = w_down.shape[0] // own
    width = model // groups
    up_blocks = [w_up[:, c * model : (c + 1) * model] for c in range(ratio)]
    rows = [jnp.pad(item, (0, model - item.shape[0]))[None] for item in vectors]
    rows.append(jnp.zeros((8 - len(rows), model), bf16))
    packed = jnp.concatenate([w_down] + up_blocks + [w_out] + rows, 0)
    block = w_qkv.reshape(own, 3, groups, width).transpose(2, 0, 1, 3).reshape(groups, own, 3 * width)
    rows = jnp.pad(jnp.stack([b_query, b_value]), ((0, 6), (0, 3 * width - own)))
    return packed, jnp.concatenate([block, jnp.broadcast_to(rows, (groups, 8, 3 * width))], 1)


def project_kernel(
    heads, me_ref, x0_ref, x1u_ref, x1l_ref, x2u_ref, x2l_ref, x3u_ref, x3l_ref, seg_ref, near_ref, far_ref,
    q_ref, k_ref, v_ref, all_ref, wide_w, rows_ref, bias_ref,
):
    step = pl.program_id(0)
    rows = x0_ref.shape[0]
    half = rows // 2
    width = heads * HEAD
    wide = q_ref.shape[1]
    slot = lax.bitwise_xor(step, me_ref[0])

    own = near_ref.shape[2] - 8
    columns, groups = near_ref.shape[:2]

    @pl.when(step == 0)
    def _():
        for c, part_ref in ((0, near_ref), (1, far_ref)):
            for z in range(columns):
                shard = lax.bitwise_xor(me_ref[2], z) * 2 + lax.bitwise_xor(me_ref[3], c)
                for g in range(groups):
                    piece = lax.bitwise_xor(me_ref[1], g) * (2 * columns) + shard
                    at = pl.ds(pl.multiple_of(piece * own, 8), own)
                    for k in range(3):
                        wide_w[k, at, :] = part_ref[z, g, :own, k * width : (k + 1) * width]
                lines = part_ref[z, 0, own:, :128].astype(f32)
                for k in range(2):
                    rows_ref[k, pl.ds(shard, 1), :] = lines[k : k + 1]
        lane = lax.broadcasted_iota(jnp.int32, (128, width), 1)
        row = lax.broadcasted_iota(jnp.int32, (128, width), 0)
        tile = jnp.where(lax.rem(lane, own) == row, 1.0, 0.0).astype(bf16)
        lane = lax.broadcasted_iota(jnp.int32, (2 * columns, width), 1)
        row = lax.broadcasted_iota(jnp.int32, (2 * columns, width), 0)
        for k in range(2):
            value = jnp.where(lane // own == row, mm(rows_ref[k].astype(bf16), tile), 0.0)
            bias_ref[k : k + 1, :] = jnp.sum(value, 0, keepdims=True)

    @pl.when(slot == 0)
    def _():
        all_ref[...] = x0_ref[...]

    for k, upper, lower in ((1, x1u_ref, x1l_ref), (2, x2u_ref, x2l_ref), (3, x3u_ref, x3l_ref)):

        @pl.when(slot == k)
        def _():
            all_ref[:half] = upper[...]
            all_ref[half:] = lower[...]

    size = 256

    def part(i, carry):
        at = pl.ds(pl.multiple_of(i * size, size), size)
        x = all_ref[at, :]
        lane = lax.broadcasted_iota(jnp.int32, (size, wide - width), 1)
        same = lane == seg_ref[at, :]
        q = (mm(x, wide_w[0]) + bias_ref[0:1, :]).astype(bf16)
        q_ref[at, :width] = q * jnp.asarray(0.125, bf16)
        q_ref[at, width:] = jnp.where(same, 1.0, 0.0).astype(bf16)
        k_ref[at, :width] = mm(x, wide_w[1]).astype(bf16)
        k_ref[at, width:] = jnp.where(same, 0.0, -far).astype(bf16)
        v_ref[at, :] = (mm(x, wide_w[2]) + bias_ref[1:2, :]).astype(bf16)
        return carry

    lax.fori_loop(0, rows // size, part, 0)


def project(place, blocks, seg_row, near, away, heads):
    own_rows, model = blocks[0].shape
    width = heads * HEAD
    wide = padded_width(width)
    seq = 4 * own_rows
    once = dict(pipeline_mode=pl.Buffered(1))
    fixed = lambda a: pl.BlockSpec(a, lambda s, m: (0,) * len(a), **once)
    cost = pl.CostEstimate(
        flops=6 * seq * model * width, bytes_accessed=4 * seq * (model + wide), transcendentals=0
    )
    return pl.pallas_call(
        lambda *refs: project_kernel(heads, *refs),
        grid_spec=pltpu.PrefetchScalarGridSpec(
            num_scalar_prefetch=1,
            grid=(4,),
            in_specs=[
                fixed((own_rows, model)),
            ]
            + [fixed((own_rows // 2, model))] * 6
            + [
                pl.BlockSpec((own_rows, 1), lambda s, m: (s, 0)),
                fixed(near.shape),
                fixed(near.shape),
            ],
            out_specs=[
                pl.BlockSpec((own_rows, wide), lambda s, m: (s, 0)),
                pl.BlockSpec((own_rows, wide), lambda s, m: (s, 0)),
                pl.BlockSpec((own_rows, width), lambda s, m: (s, 0)),
                pl.BlockSpec((own_rows, model), lambda s, m: (s, 0)),
                fixed((3, model, width)),
            ],
            scratch_shapes=[
                pltpu.VMEM((2, 2 * near.shape[0], 128), f32),
                pltpu.VMEM((8, width), f32),
            ],
        ),
        out_shape=[
            jax.ShapeDtypeStruct((seq, wide), bf16),
            jax.ShapeDtypeStruct((seq, wide), bf16),
            jax.ShapeDtypeStruct((seq, width), bf16),
            jax.ShapeDtypeStruct((seq, model), bf16),
            jax.ShapeDtypeStruct((3, model, width), bf16),
        ],
        cost_estimate=cost,
        compiler_params=pltpu.CompilerParams(vmem_limit_bytes=40 << 20),
        name="project",
    )(place, *blocks, seg_row[:, None], near, away)


def normal_rows(z):
    center = jnp.mean(z, -1, keepdims=True)
    moved = z - center
    rstd = lax.rsqrt(jnp.mean(moved * moved, -1, keepdims=True) + norm_eps)
    return moved * rstd, rstd


def norm_pull(s, hat, rstd):
    inner = jnp.mean(s * hat, -1, keepdims=True)
    return rstd * (s - jnp.mean(s, -1, keepdims=True) - hat * inner)


def gelu_both(x):
    z = jnp.abs(x) * 0.7071067811865476
    t = 1.0 / (1.0 + 0.3275911 * z)
    e = jnp.exp(-(z * z))
    poly = t * (
        0.127414796 + t * (-0.142248368 + t * (0.7107068705 + t * (-0.7265760135 + t * 0.5307027145)))
    )
    tail = poly * e
    cdf = jnp.where(x >= 0.0, 1.0 - tail, tail)
    return x * cdf, cdf + x * (e * 0.3989422804014327)


def spread_vectors(chunks, small_ref, vec_ref):
    pieces, _, model = small_ref.shape

    def spread(block, size):
        count = block.shape[0]
        lane = lax.broadcasted_iota(jnp.int32, (128, model), 1)
        row = lax.broadcasted_iota(jnp.int32, (128, model), 0)
        tile = jnp.where(lax.rem(lane, size) == row, 1.0, 0.0).astype(bf16)
        wide = mm(block, tile)
        lane = lax.broadcasted_iota(jnp.int32, (count, model), 1)
        row = lax.broadcasted_iota(jnp.int32, (count, model), 0)
        keep = lane // size == row
        return jnp.sum(jnp.where(keep, wide, 0.0), 0, keepdims=True)

    vec_ref[...] = jnp.zeros_like(vec_ref)
    for j in range(6):
        vec_ref[j : j + 1, :] = spread(small_ref[:, j, :128], model // pieces)
    share = pieces // chunks
    for c in range(chunks):
        block = small_ref[c * share : (c + 1) * share, 6, :128]
        vec_ref[8 + c : 9 + c, :] = spread(block, model // share)


def gather_vectors(chunks, vec_ref, wide_ref):
    pieces, _, model = wide_ref.shape
    wide_ref[...] = jnp.zeros_like(wide_ref)

    def gather(vector, size, count):
        lane = lax.broadcasted_iota(jnp.int32, (128, model), 1)
        row = lax.broadcasted_iota(jnp.int32, (128, model), 0)
        tile = jnp.where(lax.rem(lane, size) == row, 1.0, 0.0).astype(bf16)
        lane = lax.broadcasted_iota(jnp.int32, (count, model), 1)
        row = lax.broadcasted_iota(jnp.int32, (count, model), 0)
        kept = jnp.where(lane // size == row, vector, 0.0).astype(bf16)
        return mm_nt(kept, tile)

    for j in range(6):
        wide_ref[:, j, :128] = gather(vec_ref[j : j + 1, :], model // pieces, pieces)
    share = pieces // chunks
    for c in range(chunks):
        block = gather(vec_ref[8 + c : 9 + c, :], model // share, share)
        wide_ref[c * share : (c + 1) * share, 6, :128] = block


def middle_kernel(
    groups, chunks, place_ref, x_ref, cot_ref, m0_ref, m1_ref, m2_ref, m3_ref, out_w_ref, up_ref, down_ref, small_ref,
    y_ref, gh1_ref, gm0_ref, gm1_ref, gm2_ref, gm3_ref, kept_ref, sent_ref,
    first_low, first_t, hat1, rstd1, activ_t, slope, total, gffn, gpre, vec_ref,
    gvec_ref, gdown, gup, gout, gwide, gsmall, down_sem, up_sem, out_sem, small_sem,
):
    step = pl.program_id(0)
    rows, model = x_ref.shape
    parts = rows // ROWS
    width = m0_ref.shape[0]
    mixed_refs = (m0_ref, m1_ref, m2_ref, m3_ref)
    gmix_refs = (gm0_ref, gm1_ref, gm2_ref, gm3_ref)

    def group(r):
        return lax.bitwise_xor(place_ref[1], r)

    def out_w(r):
        share = out_w_ref.shape[0] // groups
        return out_w_ref[pl.ds(group(r) * share, share)].reshape(width, model)

    def up_w():
        return up_ref[...].reshape(model, model)

    def down_w():
        return down_ref[...].reshape(model, model)

    pieces, own = out_w_ref.shape[:2]
    share = pieces // groups

    def pair(source, sem, *place):
        return [
            [
                pltpu.make_async_copy(source.at[p], target.at[place], sem.at[p])
                for target in (kept_ref, sent_ref)
            ]
            for p in range(2)
        ]

    def begin(copies):
        for p in range(2):

            @pl.when(place_ref[0] == p)
            def _():
                copies[p][0].start()
                copies[1 - p][1].start()

    def finish(copies):
        for p in range(2):
            copies[p][0].wait()

    def down_copies(slot, chunk):
        return pair(
            gdown.at[slot], down_sem.at[slot], chunk, slice(None), slice(0, chunks * own), slice(None)
        )

    def up_copies(slot, chunk):
        at = pl.ds(pl.multiple_of((chunks + chunk) * own, 8), own)
        return pair(gup.at[slot], up_sem.at[slot], slice(None), slice(None), at, slice(None))

    def out_copies():
        at = slice(2 * chunks * own, 2 * chunks * own + own)
        return pair(gout, out_sem, slice(None), slice(None), at, slice(None))

    def small_copies():
        at = slice(2 * chunks * own + own, 2 * chunks * own + own + 8)
        return pair(gsmall, small_sem, slice(None), slice(None), at, slice(None))

    def vec(i):
        return vec_ref[i : i + 1, :]

    def sums(value):
        return jnp.sum(value, 0, keepdims=True)

    @pl.when(step == 0)
    def _():
        gvec_ref[...] = jnp.zeros_like(gvec_ref)
        spread_vectors(chunks, small_ref, vec_ref)

        def part(i, carry):
            at = pl.ds(pl.multiple_of(i * ROWS, ROWS), ROWS)
            branch = vec(0)
            for r in range(groups):
                branch = branch + mm_tn(mixed_refs[r][:, at], out_w(r))
            hat, rstd = normal_rows(x_ref[at, :].astype(f32) + branch)
            value = hat * vec(1) + vec(2)
            hat1[at, :] = hat
            rstd1[at, :] = jnp.broadcast_to(rstd, (ROWS, 128))
            low = value.astype(bf16)
            first_low[at, :] = low
            first_t[:, at] = low.T
            total[at, :] = value + vec(3)
            return carry

        lax.fori_loop(0, parts, part, 0)

    @pl.when(step < chunks)
    def _():
        def part(i, carry):
            at = pl.ds(pl.multiple_of(i * ROWS, ROWS), ROWS)
            pre = mm(first_low[at, :], up_w()) + vec_ref[pl.ds(8 + step, 1), :]
            value, pull = gelu_both(pre)
            low = value.astype(bf16)
            slope[step, at, :] = pull
            activ_t[step, :, at] = low.T
            total[at, :] += mm(low, down_w())
            return carry

        lax.fori_loop(0, parts, part, 0)

    @pl.when(step == chunks - 1)
    def _():
        def part(i, carry):
            at = pl.ds(pl.multiple_of(i * ROWS, ROWS), ROWS)
            hat, rstd = normal_rows(total[at, :])
            y_ref[at, :] = (hat * vec(4) + vec(5)).astype(bf16)
            g = cot_ref[at, :].astype(f32)
            gh2 = norm_pull(g * vec(4), hat, rstd)
            total[at, :] = gh2
            low = gh2.astype(bf16)
            gffn[at, :] = low
            gvec_ref[3:4, :] += sums(low.astype(f32))
            gvec_ref[4:5, :] += sums(g * hat)
            gvec_ref[5:6, :] += sums(g)
            return carry

        lax.fori_loop(0, parts, part, 0)

    @pl.when(step >= chunks)
    def _():
        chunk = 2 * chunks - 1 - step
        slot = lax.rem(step, 2)

        @pl.when(step >= chunks + 2)
        def _():
            finish(down_copies(slot, chunk))
            finish(up_copies(slot, chunk))

        def part(i, carry):
            at = pl.ds(pl.multiple_of(i * ROWS, ROWS), ROWS)
            low = (mm_nt(gffn[at, :], down_w()) * slope[chunk, at, :]).astype(bf16)
            gpre[at, :] = low
            gvec_ref[pl.ds(8 + chunk, 1), :] += sums(low.astype(f32))
            total[at, :] += mm_nt(low, up_w())
            return carry

        lax.fori_loop(0, parts, part, 0)
        tall = 4 * chunks * own

        def weights_down(i, carry):
            at = pl.ds(pl.multiple_of(i * tall, tall), tall)
            value = mm(activ_t[chunk, at, :], gffn[...]).astype(bf16).reshape(4, chunks * own, model)
            for f in range(4):
                gdown[slot, f % 2, 2 * i + f // 2] = value[f]
            return carry

        lax.fori_loop(0, model // tall, weights_down, 0)
        begin(down_copies(slot, chunk))
        high = 16 * own

        def weights_up(i, carry):
            at = pl.ds(pl.multiple_of(i * high, high), high)
            value = mm(first_t[at, :], gpre[...]).astype(bf16).reshape(16, own, model)
            for f in range(16):
                gup[slot, f % 2, 2 * i + f // 8, (f % 8) // 2] = value[f]
            return carry

        lax.fori_loop(0, model // high, weights_up, 0)
        begin(up_copies(slot, chunk))

    @pl.when(step == 2 * chunks - 1)
    def _():
        def part(i, carry):
            at = pl.ds(pl.multiple_of(i * ROWS, ROWS), ROWS)
            g = total[at, :]
            hat = hat1[at, :]
            gh1 = norm_pull(g * vec(1), hat, rstd1[at, :1])
            gh1_ref[at, :] = gh1
            low = gh1.astype(bf16)
            gpre[at, :] = low
            gvec_ref[0:1, :] += sums(low.astype(f32))
            gvec_ref[1:2, :] += sums(g * hat)
            gvec_ref[2:3, :] += sums(g)
            for r in range(groups):
                gmix_refs[r][:, at] = mm_nt(out_w(r), low).astype(bf16)
            return carry

        lax.fori_loop(0, parts, part, 0)
        for r in range(groups):
            value = mm(mixed_refs[r][...], gpre[...]).astype(bf16).reshape(share, own, model)
            for f in range(share):
                gout[f % 2, group(r), f // 2] = value[f]
        begin(out_copies())
        gather_vectors(chunks, gvec_ref, gwide)
        for g in range(groups):
            for f in range(share):
                gsmall[f % 2, g, f // 2] = gwide[g * share + f].astype(bf16)
        begin(small_copies())
        for back in range(2):
            finish(down_copies(back, 0))
            finish(up_copies(back, 0))
        finish(out_copies())
        finish(small_copies())


def middle(place, x, cot, mixed, packed):
    rows, model = x.shape
    groups = len(mixed)
    width = mixed[0].shape[0]
    pieces = packed.shape[0]
    own = model // pieces
    chunks = (packed.shape[1] - 8 - own) // (2 * own)
    last = 2 * chunks - 1
    back = lambda s: jnp.minimum(s, last - s)
    assert chunks == groups and pieces == 8 * groups
    once = dict(pipeline_mode=pl.Buffered(1))
    fixed2 = lambda a: pl.BlockSpec(a, lambda s: (0, 0), **once)
    vectors_at = own * (2 * chunks + 1) // 8
    cost = pl.CostEstimate(
        flops=2 * rows * model * model * (3 + 6 * chunks),
        bytes_accessed=2 * model * model * (4 * chunks + 8),
        transcendentals=rows * model * chunks,
    )
    share = pieces // groups
    half = jax.ShapeDtypeStruct((groups, share // 2, packed.shape[1], model), bf16)
    return pl.pallas_call(
        lambda *refs: middle_kernel(groups, chunks, *refs),
        grid=(2 * chunks,),
        in_specs=[
            pl.BlockSpec(memory_space=pltpu.SMEM),
            fixed2((rows, model)),
            fixed2((rows, model)),
            fixed2((width, rows)),
            fixed2((width, rows)),
            fixed2((width, rows)),
            fixed2((width, rows)),
            pl.BlockSpec((pieces, own, model), lambda s: (0, 2 * chunks, 0), **once),
            pl.BlockSpec((pieces, own, model), lambda s: (0, chunks + back(s), 0)),
            pl.BlockSpec((pieces // chunks, chunks * own, model), lambda s: (back(s), 0, 0)),
            pl.BlockSpec((pieces, 8, model), lambda s: (0, vectors_at, 0), **once),
        ],
        out_specs=[
            fixed2((rows, model)),
            fixed2((rows, model)),
            fixed2((width, rows)),
            fixed2((width, rows)),
            fixed2((width, rows)),
            fixed2((width, rows)),
            pl.BlockSpec(memory_space=pl.ANY),
            pl.BlockSpec(memory_space=pl.ANY),
        ],
        out_shape=[
            jax.ShapeDtypeStruct((rows, model), bf16),
            jax.ShapeDtypeStruct((rows, model), f32),
            jax.ShapeDtypeStruct((width, rows), bf16),
            jax.ShapeDtypeStruct((width, rows), bf16),
            jax.ShapeDtypeStruct((width, rows), bf16),
            jax.ShapeDtypeStruct((width, rows), bf16),
            half,
            half,
        ],
        scratch_shapes=[
            pltpu.VMEM((rows, model), bf16),
            pltpu.VMEM((model, rows), bf16),
            pltpu.VMEM((rows, model), f32),
            pltpu.VMEM((rows, 128), f32),
            pltpu.VMEM((chunks, model, rows), bf16),
            pltpu.VMEM((chunks, rows, model), f32),
            pltpu.VMEM((rows, model), f32),
            pltpu.VMEM((rows, model), bf16),
            pltpu.VMEM((rows, model), bf16),
            pltpu.VMEM((16, model), f32),
            pltpu.VMEM((16, model), f32),
            pltpu.VMEM((2, 2, share // 2, chunks * own, model), bf16),
            pltpu.VMEM((2, 2, groups, share // 2, own, model), bf16),
            pltpu.VMEM((2, groups, share // 2, own, model), bf16),
            pltpu.VMEM((pieces, 8, model), f32),
            pltpu.VMEM((2, groups, share // 2, 8, model), bf16),
            pltpu.SemaphoreType.DMA((2, 2)),
            pltpu.SemaphoreType.DMA((2, 2)),
            pltpu.SemaphoreType.DMA((2,)),
            pltpu.SemaphoreType.DMA((2,)),
        ],
        cost_estimate=cost,
        compiler_params=pltpu.CompilerParams(vmem_limit_bytes=60 << 20),
        name="middle",
    )(place, x, cot, *mixed, packed, packed, packed, packed)


def by_sp(value, flip):
    groups = lax.axis_size("sp")
    return lax.ppermute(value, "sp", [(i, i ^ flip) for i in range(groups)])


def by_fsdp(value, flip):
    shards = lax.axis_size("fsdp")
    return lax.ppermute(value, "fsdp", [(i, i ^ flip) for i in range(shards)])


def scatter_rows(sent_x, sent_y, mine, low, up):
    half = low.shape[0]
    got_x = by_sp(sent_x, 1).astype(f32)
    got_y = by_sp(sent_y, 2).astype(f32)
    next_y = by_sp((up + got_x[half:]).astype(bf16), 2).astype(f32)
    next_x = by_sp((low + got_y[half:]).astype(bf16), 1).astype(f32)
    return mine + jnp.concatenate([got_x[:half] + next_y, got_y[:half] + next_x], 0)


def unpack(packed, ratio):
    pieces, _, model = packed.shape
    own = model // pieces
    at = ratio * own
    down = packed[:, :at].reshape(ratio * model, model)
    up = packed[:, at : 2 * at].reshape(pieces, ratio, own, model).transpose(1, 0, 2, 3)
    out = packed[:, 2 * at : 2 * at + own].reshape(model, model)
    vectors = [packed[:, 2 * at + own + j, :own].reshape(-1) for j in range(6)]
    vectors.append(packed[:, 2 * at + own + 6, :at].reshape(-1))
    return down, up.reshape(ratio, model, model), out, vectors


def repack(packed, ratio, pieces):
    if packed.shape[0] == pieces:
        return packed
    down, up, out, vectors = unpack(packed, ratio)
    model = out.shape[0]
    own = model // pieces
    up = up.reshape(ratio, pieces, own, model).transpose(1, 0, 2, 3)
    rows = [jnp.pad(v.reshape(pieces, -1), ((0, 0), (0, model - v.shape[0] // pieces))) for v in vectors]
    rows.append(jnp.zeros_like(rows[0]))
    return jnp.concatenate(
        [
            down.reshape(pieces, ratio * own, model),
            up.reshape(pieces, ratio * own, model),
            out.reshape(pieces, own, model),
            jnp.stack(rows, 1),
        ],
        1,
    )


def body(
    tokens,
    segments,
    cotangent,
    w_qkv,
    b_query,
    b_value,
    w_out,
    b_out,
    ln1_gain,
    ln1_bias,
    w_up,
    b_up,
    w_down,
    b_down,
    ln2_gain,
    ln2_bias,
):
    both = ("sp", "fsdp")
    groups = lax.axis_size("sp")
    shards = lax.axis_size("fsdp")
    devices = groups * shards
    rows, model = tokens.shape
    hidden = w_up.shape[1]
    ratio = hidden // model
    own = w_qkv.shape[0]
    pieces = devices if own % 8 == 0 else 8 * groups
    heads_local = HEADS // groups
    width = heads_local * HEAD
    seq_len = rows * groups
    seg_row = segments[0]

    me = lax.axis_index("sp").astype(jnp.int32).reshape(1)
    core = lax.rem(lax.axis_index("fsdp"), 2).astype(jnp.int32).reshape(1)
    direct = pieces == devices

    half = rows // 2
    first = by_sp(tokens[:half], 2), by_sp(tokens[half:], 1)
    second = by_sp(tokens[:half], 1), by_sp(tokens[half:], 2)
    vectors = [b_out, ln1_gain, ln1_bias, b_down, ln2_gain, ln2_bias, b_up]
    if direct:
        packed, mine = pack(me, w_down, w_up, w_out, w_qkv, vectors, b_query, b_value, groups)
        mine = jnp.stack([mine[0]] + [by_sp(mine[r], r) for r in range(1, groups)])
        near = jnp.stack([mine] + [by_fsdp(mine, 2 * z) for z in range(1, shards // 2)])
        near, first, second = lax.optimization_barrier((near, first, second))
        away = by_fsdp(near, 1)
        column = (lax.axis_index("fsdp").astype(jnp.int32) // 2).reshape(1)
        order = jnp.concatenate([me, me, column, core])
    else:
        packed, mine = pack_plain(w_down, w_up, w_out, w_qkv, vectors, b_query, b_value, groups)
        mine = jnp.broadcast_to(mine[:, None], (groups, shards) + mine.shape[1:])
        mine = mine.reshape(devices, own + 8, 3 * width)
        mine = lax.all_to_all(mine, both, split_axis=0, concat_axis=0, tiled=True)
        cut = model // pieces
        biases = lax.dynamic_slice(mine, (me[0] * shards, own, 0), (shards, 2, own))
        biases = biases.transpose(1, 0, 2).reshape(2, 8, cut).transpose(1, 0, 2)
        biases = jnp.pad(biases, ((0, 0), (0, 6), (0, 3 * width - cut)))
        mine = mine[:, :own].reshape(groups, 8, cut, 3 * width)
        mine = jnp.concatenate([mine, jnp.broadcast_to(biases[None], (groups, 8, 8, 3 * width))], 2)
        mine = mine.reshape(groups, 4, 2, cut + 8, 3 * width).transpose(2, 1, 0, 3, 4)
        near, away = mine[0], mine[1]
        order = jnp.concatenate([me, jnp.zeros((3,), jnp.int32)])
    blocks = tokens, second[0], first[1], first[0], second[1], by_sp(first[0], 1), by_sp(first[1], 2)
    packed_weights = repack(lax.all_gather(packed, both, axis=0, tiled=False), ratio, pieces)
    queries, keys, values, tokens_all, weights = project(
        order, blocks, seg_row, near, away, heads_local
    )
    forward_start, forward_number = windows(seg_row, FQ, FK, 128)
    backward_start, backward_number = windows(seg_row, BK, BQ, 128)
    *attended, logsum = attend_forward(
        queries, keys, values, forward_start, forward_number, me, heads_local
    )
    mixed = [attended[0]] + [by_sp(attended[r], r) for r in range(1, 4)]
    place = jnp.concatenate([core if direct else jnp.zeros_like(core), me])
    output, grad_h1, *grad_mixed, kept, sent = middle(place, tokens, cotangent, mixed, packed_weights)
    grad_heads = [grad_mixed[0]] + [by_sp(grad_mixed[r], r) for r in range(1, 4)]

    if not direct:
        halves = jnp.stack([kept, sent], 2).reshape(pieces, kept.shape[2], model)
        halves = repack(halves, ratio, devices).reshape(groups, shards // 2, 2, -1, model)
        kept = lax.dynamic_index_in_dim(halves, core[0], 2, keepdims=False)
        sent = lax.dynamic_index_in_dim(halves, 1 - core[0], 2, keepdims=False)
    partner = by_fsdp(sent, 1)
    total = (kept.astype(f32) + partner.astype(f32)).astype(bf16)
    total, grad_heads = lax.optimization_barrier((total, grad_heads))
    total = lax.psum_scatter(total.reshape(-1, model), "sp", scatter_dimension=0, tiled=True)
    cores = [[2 * i + c for i in range(shards // 2)] for c in range(2)]
    reduced = lax.psum_scatter(
        total, "fsdp", scatter_dimension=0, tiled=True, axis_index_groups=cores
    ).astype(f32)

    *parts, kept, sent = attend_backward(
        queries,
        keys,
        values,
        grad_heads,
        attended,
        logsum,
        backward_start,
        backward_number,
        order,
        tokens_all,
        weights,
        grad_h1,
        pieces,
        heads_local,
    )
    grad_input = scatter_rows(*parts)
    if direct:
        total = (kept.astype(f32) + by_fsdp(sent, 1).astype(f32)).astype(bf16)
        moved = [by_fsdp(total[z], 2 * z).astype(f32) for z in range(1, shards // 2)]
        total = sum(moved, total[0].astype(f32))
        by_head = jnp.stack([total[0]] + [by_sp(total[r], r) for r in range(1, groups)])
        bias_sums = total[0, :2, model - 128 : model - 128 + own]
        by_head = [lax.dynamic_index_in_dim(by_head, me[0] ^ g, keepdims=False) for g in range(groups)]
        by_head = jnp.stack([item[:, : 3 * width].reshape(own, 3, width) for item in by_head], 2)
    else:
        cut = model // pieces
        halves = jnp.stack([kept, sent], 2).transpose(1, 0, 2, 3, 4).reshape(pieces, cut, model)
        biases = halves[:8, :2, model - 128 : model - 128 + cut]
        biases = biases.transpose(1, 0, 2).reshape(2, shards, own).transpose(1, 0, 2)
        biases = jnp.pad(biases, ((0, 0), (0, 6), (0, 3 * width - own)))
        halves = halves[:, :, : 3 * width].reshape(devices, own, 3 * width)
        halves = jnp.concatenate([halves, jnp.tile(biases, (groups, 1, 1))], 1)
        halves = lax.all_to_all(halves, both, split_axis=0, concat_axis=0, tiled=True)
        halves = jnp.sum(halves.reshape(groups, shards, own + 8, 3 * width).astype(f32), 1)
        bias_sums = lax.dynamic_slice(halves, (me[0], own, 0), (1, 2, own))[0]
        by_head = halves[:, :own].reshape(groups, own, 3, width).transpose(1, 2, 0, 3)
    owned_qkv = by_head.reshape(own, 3 * model)
    grad_query_bias = bias_sums[0]
    grad_value_bias = bias_sums[1]
    at = ratio * own
    owned_up = reduced[at : 2 * at].reshape(ratio, own, model).transpose(1, 0, 2).reshape(own, hidden)
    tail = reduced[2 * at + own :]
    return (
        output,
        grad_input,
        owned_qkv,
        grad_query_bias,
        grad_value_bias,
        reduced[2 * at : 2 * at + own],
        tail[0, :own],
        tail[1, :own],
        tail[2, :own],
        owned_up,
        tail[6, :at],
        reduced[:at],
        tail[3, :own],
        tail[4, :own],
        tail[5, :own],
    )


def solution(mesh):
    in_specs = (
        P(("fsdp", "sp"), None),
        P("fsdp", None),
        P(("fsdp", "sp"), None),
        P(("sp", "fsdp"), None),
        P(("sp", "fsdp")),
        P(("sp", "fsdp")),
        P(("sp", "fsdp"), None),
        P(("sp", "fsdp")),
        P(("sp", "fsdp")),
        P(("sp", "fsdp")),
        P(("sp", "fsdp"), None),
        P(("sp", "fsdp")),
        P(("sp", "fsdp"), None),
        P(("sp", "fsdp")),
        P(("sp", "fsdp")),
        P(("sp", "fsdp")),
    )
    out_specs = (
        P(("fsdp", "sp"), None),
        P(("fsdp", "sp"), None),
        P(("sp", "fsdp"), None),
        P(("sp", "fsdp")),
        P(("sp", "fsdp")),
        P(("sp", "fsdp"), None),
        P(("sp", "fsdp")),
        P(("sp", "fsdp")),
        P(("sp", "fsdp")),
        P(("sp", "fsdp"), None),
        P(("sp", "fsdp")),
        P(("sp", "fsdp"), None),
        P(("sp", "fsdp")),
        P(("sp", "fsdp")),
        P(("sp", "fsdp")),
    )
    return jax.shard_map(body, mesh=mesh, in_specs=in_specs, out_specs=out_specs, check_vma=False)
```

```python
import jax
import jax.numpy as jnp
from jax import lax
from jax.experimental import pallas as pl
from jax.experimental.pallas import tpu as pltpu
from jax.sharding import PartitionSpec as P

HEADS = 12
HEAD = 64
IDS = 32
far = 1e30
FQ, FK = 512, 512
BQ, BK = 512, 256
ROWS = 384
f32 = jnp.float32
bf16 = jnp.bfloat16
norm_eps = 1e-06


def padded_width(width):
    return -(-(width + IDS) // 128) * 128


def spans(seg_row, block):
    seq = seg_row.shape[0]
    count = seq // block
    first = seg_row[::block]
    last = seg_row[block - 1 :: block]
    lo = jnp.sum((seg_row[None, :] < first[:, None]).astype(jnp.int32), 1)
    hi = jnp.sum((seg_row[None, :] <= last[:, None]).astype(jnp.int32), 1)
    return lo, hi


def windows(seg_row, block, step, grain):
    lo, hi = spans(seg_row, block)
    seq = seg_row.shape[0]
    start = lo // grain * grain
    number = -(-(hi - start) // step)
    start = jnp.minimum(start, seq - number * step)
    return start.astype(jnp.int32), number.astype(jnp.int32)


def lanes_of(head, shape):
    lane = lax.broadcasted_iota(jnp.int32, shape, len(shape) - 1)
    return (lane >= head * HEAD) & (lane < (head + 1) * HEAD)


def mm(a, b):
    return jnp.dot(a, b, preferred_element_type=f32)


def mm_nt(a, b):
    return lax.dot_general(a, b, (((1,), (1,)), ((), ())), preferred_element_type=f32)


def mm_tn(a, b):
    return lax.dot_general(a, b, (((0,), (0,)), ((), ())), preferred_element_type=f32)


def forward_kernel(
    heads, start_ref, number_ref, me_ref, q_ref, k_ref, v_ref,
    o0_ref, o1_ref, o2_ref, o3_ref, lse_ref, kh, vt, scores, acc,
):
    step = pl.program_id(0)
    seq, wide = k_ref.shape
    width = heads * HEAD
    tall = HEAD + 16

    @pl.when(step == 0)
    def _():
        row = lax.broadcasted_iota(jnp.int32, (16, FK), 0)
        ones = jnp.where(row == 0, 1.0, 0.0).astype(bf16)

        def part(i, carry):
            rows = pl.ds(pl.multiple_of(i * FK, FK), FK)
            k = k_ref[rows, :]
            lane = lax.broadcasted_iota(jnp.int32, k.shape, 1)
            turned = v_ref[rows, :].T
            for h in range(heads):
                keep = lanes_of(h, k.shape) | (lane >= width)
                kept = jnp.where(keep, k, jnp.zeros_like(k))
                for c in range(FK // 128):
                    at = pl.multiple_of(i * (FK * heads) + (c * heads + h) * 128, 128)
                    kh[pl.ds(at, 128), :] = kept[c * 128 : (c + 1) * 128]
                vt[h * tall : h * tall + HEAD, rows] = turned[h * HEAD : (h + 1) * HEAD]
                vt[h * tall + HEAD : (h + 1) * tall, rows] = ones
            return carry

        lax.fori_loop(0, seq // FK, part, 0)

    q = q_ref[...]
    start = start_ref[step]
    number = number_ref[step]

    def score(j, tops):
        at = pl.multiple_of((start + j * FK) * heads, 128)
        every = mm_nt(kh[pl.ds(at, FK * heads), :], q)
        news = list(tops)
        for c in range(FK // 128):
            for h in range(heads):
                s = every[(c * heads + h) * 128 : (c * heads + h + 1) * 128]
                scores[h, pl.ds(pl.multiple_of(j * FK + c * 128, 128), 128), :] = s
                news[h] = jnp.maximum(news[h], jnp.max(s.reshape(16, 8, FQ), 0))
        return tuple(news)

    tops = lax.fori_loop(0, number, score, (jnp.full((8, FQ), -jnp.inf, f32),) * heads)
    tops = [jnp.max(top, 0, keepdims=True) for top in tops]
    acc[...] = jnp.zeros_like(acc)

    def mix(j, carry):
        rows = pl.ds(pl.multiple_of(start + j * FK, 128), FK)
        out = pl.ds(pl.multiple_of(j * FK, FK), FK)
        for h in range(heads):
            p = jnp.exp(scores[h, out, :] - tops[h]).astype(bf16)
            acc[h] += mm(vt[h * tall : (h + 1) * tall, rows], p)
        return carry

    lax.fori_loop(0, number, mix, 0)
    outs = []
    for h in range(heads):
        total = acc[h, HEAD : HEAD + 1, :]
        outs.append(acc[h, :HEAD, :] / total)
        lse_ref[h : h + 1, :] = tops[h] + jnp.log(total)
    mixed = jnp.concatenate(outs, 0).astype(bf16)
    per = o0_ref.shape[1] // 256
    for u in range(FQ // 256):
        block = step * (FQ // 256) + u
        at = pl.ds(pl.multiple_of(lax.rem(block, per) * 256, 256), 256)
        slot = lax.bitwise_xor(block // per, me_ref[0])
        for r, out_ref in enumerate((o0_ref, o1_ref, o2_ref, o3_ref)):

            @pl.when(slot == r)
            def _():
                out_ref[:, at] = mixed[:, u * 256 : (u + 1) * 256]


def attend_forward(q, k, v, starts, numbers, me, heads):
    seq, wide = q.shape
    width = heads * HEAD
    steps = seq // FQ
    cost = pl.CostEstimate(
        flops=2 * heads * seq * seq * HEAD, bytes_accessed=8 * seq * wide, transcendentals=heads * seq * seq // 3
    )
    return pl.pallas_call(
        lambda *refs: forward_kernel(heads, *refs),
        grid_spec=pltpu.PrefetchScalarGridSpec(
            num_scalar_prefetch=3,
            grid=(steps,),
            in_specs=[
                pl.BlockSpec((FQ, wide), lambda i, a, b, m: (i, 0)),
                pl.BlockSpec((seq, wide), lambda i, a, b, m: (0, 0)),
                pl.BlockSpec((seq, width), lambda i, a, b, m: (0, 0)),
            ],
            out_specs=[
                pl.BlockSpec((width, seq // 4), lambda i, a, b, m: (0, 0)),
                pl.BlockSpec((width, seq // 4), lambda i, a, b, m: (0, 0)),
                pl.BlockSpec((width, seq // 4), lambda i, a, b, m: (0, 0)),
                pl.BlockSpec((width, seq // 4), lambda i, a, b, m: (0, 0)),
                pl.BlockSpec((8, FQ), lambda i, a, b, m: (0, i)),
            ],
            scratch_shapes=[
                pltpu.VMEM((heads * seq, wide), bf16),
                pltpu.VMEM((heads * (HEAD + 16), seq), bf16),
                pltpu.VMEM((heads, seq, FQ), f32),
                pltpu.VMEM((heads, HEAD + 16, FQ), f32),
            ],
        ),
        out_shape=[
            jax.ShapeDtypeStruct((width, seq // 4), bf16),
            jax.ShapeDtypeStruct((width, seq // 4), bf16),
            jax.ShapeDtypeStruct((width, seq // 4), bf16),
            jax.ShapeDtypeStruct((width, seq // 4), bf16),
            jax.ShapeDtypeStruct((8, seq), f32),
        ],
        cost_estimate=cost,
        compiler_params=pltpu.CompilerParams(vmem_limit_bytes=48 << 20),
        name="attend_forward",
    )(starts, numbers, me, q, k, v)


def backward_kernel(
    heads, start_ref, number_ref, me_ref, q_ref, k_ref, v_ref,
    g0_ref, g1_ref, g2_ref, g3_ref, o0_ref, o1_ref, o2_ref, o3_ref, lse_ref,
    x0_ref, x1_ref, x2_ref, x3u_ref, x3l_ref, w_ref, gh1_ref,
    sx_ref, sy_ref, mine_ref, low_ref, up_ref, kept_ref, sent_ref,
    qt, gt, dqt, delta, dkt, dvt, kh, vh, turned, grads, rows_ref,
):
    step = pl.program_id(0)
    seq, wide = q_ref.shape
    width = heads * HEAD
    own_rows = seq // 4
    per = own_rows // 256
    me = me_ref[0]

    @pl.when(step == 0)
    def _():
        def part(i, carry):
            rows = pl.ds(pl.multiple_of(i * 256, 256), 256)
            at = pl.ds(pl.multiple_of(lax.rem(i, per) * 256, 256), 256)
            slot = lax.bitwise_xor(i // per, me)
            qt[:, rows] = q_ref[rows, :].T[:width]
            dqt[:, rows] = jnp.zeros((width, 256), f32)
            pairs = ((g0_ref, o0_ref), (g1_ref, o1_ref), (g2_ref, o2_ref), (g3_ref, o3_ref))
            for r, (g_ref, o_ref) in enumerate(pairs):

                @pl.when(slot == r)
                def _():
                    g = g_ref[:, at]
                    gt[:, rows] = g
                    product = g.astype(f32) * o_ref[:, at].astype(f32)
                    for h in range(heads):
                        mine = slice(h * HEAD, (h + 1) * HEAD)
                        delta[h : h + 1, rows] = jnp.sum(product[mine], 0, keepdims=True)

            return carry

        lax.fori_loop(0, seq // 256, part, 0)

    start = start_ref[step]
    k = k_ref[...]
    v = v_ref[...]
    lane = lax.broadcasted_iota(jnp.int32, k.shape, 1)
    for h in range(heads):
        part = slice(h * BK, (h + 1) * BK)
        kh[part, :] = jnp.where(lanes_of(h, k.shape) | (lane >= width), k, jnp.zeros_like(k))
        vh[part, :] = jnp.where(lanes_of(h, v.shape), v, jnp.zeros_like(v))
    kt = k.T
    dkt[...] = jnp.zeros_like(dkt)
    dvt[...] = jnp.zeros_like(dvt)

    def one(i, carry):
        rows = pl.ds(pl.multiple_of(start + i * BQ, 128), BQ)
        q = q_ref[rows, :]
        ss = mm_nt(kh[...], q)
        dps = mm(vh[...], gt[:, rows])
        for h in range(heads):
            mine = slice(h * HEAD, (h + 1) * HEAD)
            part = slice(h * BK, (h + 1) * BK)
            p = jnp.exp(ss[part] - lse_ref[h : h + 1, rows])
            dp = dps[part]
            ds = (p * (dp - delta[h : h + 1, rows])).astype(bf16)
            dvt[mine, :] += mm_nt(gt[mine, rows], p.astype(bf16))
            dkt[mine, :] += mm_nt(qt[mine, rows], ds)
            dqt[mine, rows] += mm(kt[mine, :], ds)
        return carry

    lax.fori_loop(0, number_ref[step], one, 0)
    here = pl.ds(pl.multiple_of(step * BK, BK), BK)
    for c, total in ((1, dkt), (2, dvt)):
        low = total[...].astype(bf16)
        turned[c * width : (c + 1) * width, here] = low
        grads[c, here, :] = low.T

    @pl.when(step == pl.num_programs(0) - 1)
    def _():
        def part(i, carry):
            rows = pl.ds(pl.multiple_of(i * 256, 256), 256)
            low = (dqt[:, rows] * 0.125).astype(bf16)
            turned[:width, rows] = low
            grads[0, rows, :] = low.T
            return carry

        lax.fori_loop(0, seq // 256, part, 0)
        half = own_rows // 2

        def back(i, carry):
            def rows_of(lower):
                at = pl.ds(pl.multiple_of(i * own_rows + lower * half, 128), half)
                value = mm_nt(grads[0, at, :], w_ref[0])
                value = value + mm_nt(grads[1, at, :], w_ref[1])
                return value + mm_nt(grads[2, at, :], w_ref[2])

            slot = lax.bitwise_xor(i, me)
            for lower in range(2):
                value = rows_of(lower)
                here = slice(lower * half, (lower + 1) * half)

                @pl.when(slot == 0)
                def _():
                    mine_ref[here, :] = value + gh1_ref[here, :]

                @pl.when(slot == 1)
                def _():
                    if lower:
                        low_ref[...] = value
                    else:
                        sx_ref[:half] = value.astype(bf16)

                @pl.when(slot == 2)
                def _():
                    if lower:
                        sy_ref[:half] = value.astype(bf16)
                    else:
                        up_ref[...] = value

                @pl.when(slot == 3)
                def _():
                    if lower:
                        sy_ref[half:] = value.astype(bf16)
                    else:
                        sx_ref[half:] = value.astype(bf16)

            return carry

        lax.fori_loop(0, 4, back, 0)
        model = x0_ref.shape[1]
        columns, _, own = kept_ref.shape[:3]
        shards = 2 * columns
        lane = lax.broadcasted_iota(jnp.int32, (128, width), 1)
        row = lax.broadcasted_iota(jnp.int32, (128, width), 0)
        tile = jnp.where(lax.rem(lane, own) == row, 1.0, 0.0).astype(bf16)
        lane = lax.broadcasted_iota(jnp.int32, (shards, width), 1)
        row = lax.broadcasted_iota(jnp.int32, (shards, width), 0)
        ones = jnp.ones((8, seq), bf16)
        rows_ref[...] = jnp.zeros_like(rows_ref)
        for j, c in enumerate((0, 2)):
            sums = mm(ones, grads[c])[:1]
            rows_ref[:, j, :] = mm_nt(jnp.where(lane // own == row, sums, 0.0).astype(bf16), tile)
        total = jnp.zeros((3 * width, model), f32)
        for r, parts in enumerate(((x0_ref,), (x1_ref,), (x2_ref,), (x3u_ref, x3l_ref))):
            first = lax.bitwise_xor(me, r) * own_rows
            for part_ref in parts:
                count = part_ref.shape[0]
                total = total + mm(turned[:, pl.ds(pl.multiple_of(first, 128), count)], part_ref[...])
                first = first + count
        value = total.T.astype(bf16).reshape(4 * shards, own, 3 * width)
        for core in range(2):

            @pl.when(me_ref[3] == core)
            def _():
                for piece in range(4 * shards):
                    group, shard = piece // shards, piece % shards
                    target = kept_ref if shard % 2 == core else sent_ref
                    z = lax.bitwise_xor(me_ref[2], shard // 2)
                    r = lax.bitwise_xor(me_ref[1], group)
                    target[z, r, :, : 3 * width] = value[piece]
                    target[z, r, :, 3 * width :] = jnp.zeros((own, model - 3 * width), bf16)
                    target[z, r, :8, model - 128 :] = rows_ref[shard].astype(bf16)


def attend_backward(q, k, v, g, o, lse, starts, numbers, place, x, w, gh1, pieces, heads):
    seq, wide = q.shape
    width = heads * HEAD
    steps = seq // BK
    own_rows, model = gh1.shape
    half = own_rows // 2
    own = model // pieces
    once = dict(pipeline_mode=pl.Buffered(1))
    whole = lambda a: pl.BlockSpec(a, lambda i, a_, b_, m_: (0,) * len(a), **once)
    cost = pl.CostEstimate(
        flops=5 * heads * seq * seq * HEAD + 12 * seq * model * width,
        bytes_accessed=16 * seq * wide,
        transcendentals=heads * seq * seq // 3,
    )
    return pl.pallas_call(
        lambda *refs: backward_kernel(heads, *refs),
        grid_spec=pltpu.PrefetchScalarGridSpec(
            num_scalar_prefetch=3,
            grid=(steps,),
            in_specs=[
                whole((seq, wide)),
                pl.BlockSpec((BK, wide), lambda i, a, b, m: (i, 0)),
                pl.BlockSpec((BK, width), lambda i, a, b, m: (i, 0)),
            ]
            + [whole((width, own_rows))] * 8
            + [whole((8, seq))]
            + [whole((own_rows, model))] * 3
            + [whole((half, model))] * 2
            + [whole((3, model, width)), whole((own_rows, model))],
            out_specs=[
                whole((own_rows, model)),
                whole((own_rows, model)),
                whole((own_rows, model)),
                whole((own_rows // 2, model)),
                whole((own_rows // 2, model)),
                whole((pieces // 8, 4, own, model)),
                whole((pieces // 8, 4, own, model)),
            ],
            scratch_shapes=[
                pltpu.VMEM((width, seq), bf16),
                pltpu.VMEM((width, seq), bf16),
                pltpu.VMEM((width, seq), f32),
                pltpu.VMEM((8, seq), f32),
                pltpu.VMEM((width, BK), f32),
                pltpu.VMEM((width, BK), f32),
                pltpu.VMEM((heads * BK, wide), bf16),
                pltpu.VMEM((heads * BK, width), bf16),
                pltpu.VMEM((3 * width, seq), bf16),
                pltpu.VMEM((3, seq, width), bf16),
                pltpu.VMEM((pieces // 4, 8, 128), f32),
            ],
        ),
        out_shape=[
            jax.ShapeDtypeStruct((own_rows, model), bf16),
            jax.ShapeDtypeStruct((own_rows, model), bf16),
            jax.ShapeDtypeStruct((own_rows, model), f32),
            jax.ShapeDtypeStruct((own_rows // 2, model), f32),
            jax.ShapeDtypeStruct((own_rows // 2, model), f32),
            jax.ShapeDtypeStruct((pieces // 8, 4, own, model), bf16),
            jax.ShapeDtypeStruct((pieces // 8, 4, own, model), bf16),
        ],
        cost_estimate=cost,
        compiler_params=pltpu.CompilerParams(vmem_limit_bytes=60 << 20),
        name="attend_backward",
    )(starts, numbers, place, q, k, v, *g, *o, lse, *x, w, gh1)


def pack_kernel(ratio, groups, me_ref, down_ref, up_ref, out_ref, qkv_ref, *refs):
    vectors, (query_ref, value_ref, packed_ref, spread_ref, rows_ref) = refs[:-5], refs[-5:]
    own, model = out_ref.shape
    width = model // groups
    rows_ref[...] = jnp.zeros_like(rows_ref)
    rows_ref[0:1, :own] = query_ref[...].astype(f32)
    rows_ref[1:2, :own] = value_ref[...].astype(f32)
    biases = rows_ref[:, : 3 * width].astype(bf16)
    for g in range(groups):
        parts = [qkv_ref[:, c * model + g * width : c * model + (g + 1) * width] for c in range(3)]
        slot = lax.bitwise_xor(me_ref[0], g)
        spread_ref[slot, :own, :] = jnp.concatenate(parts, 1)
        spread_ref[slot, own:, :] = biases
    at = ratio * own
    packed_ref[:at] = down_ref[...]
    for c in range(ratio):
        packed_ref[at + c * own : at + (c + 1) * own] = up_ref[:, c * model : (c + 1) * model]
    packed_ref[2 * at : 2 * at + own] = out_ref[...]
    rows_ref[...] = jnp.zeros_like(rows_ref)
    for j, vector in enumerate(vectors):
        rows_ref[j : j + 1, : vector.shape[1]] = vector[...].astype(f32)
    packed_ref[2 * at + own :] = rows_ref[...].astype(bf16)


def pack(me, w_down, w_up, w_out, w_qkv, vectors, b_query, b_value, groups):
    own, model = w_out.shape
    ratio = w_down.shape[0] // own
    width = model // groups
    vmem = pl.BlockSpec(memory_space=pltpu.VMEM)
    return pl.pallas_call(
        lambda *refs: pack_kernel(ratio, groups, *refs),
        in_specs=[pl.BlockSpec(memory_space=pltpu.SMEM)] + [vmem] * (6 + len(vectors)),
        out_shape=[
            jax.ShapeDtypeStruct((own * (2 * ratio + 1) + 8, model), bf16),
            jax.ShapeDtypeStruct((groups, own + 8, 3 * width), bf16),
        ],
        scratch_shapes=[pltpu.VMEM((8, model), f32)],
        name="pack",
    )(me, w_down, w_up, w_out, w_qkv, *[item[None] for item in vectors], b_query[None], b_value[None])


def pack_plain(w_down, w_up, w_out, w_qkv, vectors, b_query, b_value, groups):
    own, model = w_out.shape
    ratio = w_down.shape[0] // own
    width = model // groups
    up_blocks = [w_up[:, c * model : (c + 1) * model] for c in range(ratio)]
    rows = [jnp.pad(item, (0, model - item.shape[0]))[None] for item in vectors]
    rows.append(jnp.zeros((8 - len(rows), model), bf16))
    packed = jnp.concatenate([w_down] + up_blocks + [w_out] + rows, 0)
    block = w_qkv.reshape(own, 3, groups, width).transpose(2, 0, 1, 3).reshape(groups, own, 3 * width)
    rows = jnp.pad(jnp.stack([b_query, b_value]), ((0, 6), (0, 3 * width - own)))
    return packed, jnp.concatenate([block, jnp.broadcast_to(rows, (groups, 8, 3 * width))], 1)


def project_block(heads, x_ref, first, seg_ref, bias_ref, w_ref, q_ref, k_ref, v_ref):
    size = 384
    width = heads * HEAD
    wide = q_ref.shape[1]

    def part(i, carry):
        x = x_ref[pl.ds(pl.multiple_of(i * size, size), size), :]
        at = pl.ds(pl.multiple_of(first + i * size, size), size)
        lane = lax.broadcasted_iota(jnp.int32, (size, wide - width), 1)
        same = lane == seg_ref[at, :]
        q = (mm(x, w_ref[0]) + bias_ref[0:1, :]).astype(bf16)
        q_ref[at, :width] = q * jnp.asarray(0.125, bf16)
        q_ref[at, width:] = jnp.where(same, 1.0, 0.0).astype(bf16)
        k_ref[at, :width] = mm(x, w_ref[1]).astype(bf16)
        k_ref[at, width:] = jnp.where(same, 0.0, -far).astype(bf16)
        v_ref[at, :] = (mm(x, w_ref[2]) + bias_ref[1:2, :]).astype(bf16)
        return carry

    lax.fori_loop(0, x_ref.shape[0] // size, part, 0)


def project_kernel(
    heads, me_ref, x0_ref, x1_ref, x2_ref, seg_ref, near_ref, far_ref,
    q_ref, k_ref, v_ref, wide_w, bias_ref, rows_ref,
):
    step = pl.program_id(0)
    width = heads * HEAD
    own = near_ref.shape[2] - 8
    columns, groups = near_ref.shape[:2]

    @pl.when(step == 0)
    def _():
        for c, part_ref in ((0, near_ref), (1, far_ref)):
            for z in range(columns):
                shard = lax.bitwise_xor(me_ref[2], z) * 2 + lax.bitwise_xor(me_ref[3], c)
                for g in range(groups):
                    piece = lax.bitwise_xor(me_ref[1], g) * (2 * columns) + shard
                    at = pl.ds(pl.multiple_of(piece * own, 8), own)
                    for k in range(3):
                        wide_w[k, at, :] = part_ref[z, g, :own, k * width : (k + 1) * width]
                lines = part_ref[z, 0, own:, :128].astype(f32)
                for k in range(2):
                    rows_ref[k, pl.ds(shard, 1), :] = lines[k : k + 1]
        lane = lax.broadcasted_iota(jnp.int32, (128, width), 1)
        row = lax.broadcasted_iota(jnp.int32, (128, width), 0)
        tile = jnp.where(lax.rem(lane, own) == row, 1.0, 0.0).astype(bf16)
        lane = lax.broadcasted_iota(jnp.int32, (2 * columns, width), 1)
        row = lax.broadcasted_iota(jnp.int32, (2 * columns, width), 0)
        bias_ref[...] = jnp.zeros_like(bias_ref)
        for k in range(2):
            value = jnp.where(lane // own == row, mm(rows_ref[k].astype(bf16), tile), 0.0)
            bias_ref[k : k + 1, :] = jnp.sum(value, 0, keepdims=True)

    for k, part_ref in ((0, x0_ref), (1, x1_ref), (2, x2_ref)):

        @pl.when(step == k)
        def _():
            project_block(heads, part_ref, 0, seg_ref, bias_ref, wide_w, q_ref, k_ref, v_ref)


def project_last_kernel(heads, me_ref, upper_ref, lower_ref, seg_ref, w_ref, bias_ref, *refs):
    project_block(heads, upper_ref, 0, seg_ref, bias_ref, w_ref, *refs[-3:])
    project_block(heads, lower_ref, upper_ref.shape[0], seg_ref, bias_ref, w_ref, *refs[-3:])


def project(place, blocks, seg_row, near, away, heads):
    own_rows, model = blocks[0].shape
    width = heads * HEAD
    wide = padded_width(width)
    seq = 4 * own_rows
    once = dict(pipeline_mode=pl.Buffered(1))
    fixed = lambda a: pl.BlockSpec(a, lambda s, m: (0,) * len(a), **once)

    def rows_of(slot):
        at = lambda s, m: (lax.bitwise_xor(s + slot, m[0]), 0)
        return [pl.BlockSpec((own_rows, n), at) for n in (1, wide, wide, width)]

    def cost(part):
        return pl.CostEstimate(
            flops=6 * part * own_rows * model * width,
            bytes_accessed=4 * part * own_rows * (model + wide),
            transcendentals=0,
        )

    params = pltpu.CompilerParams(vmem_limit_bytes=40 << 20)
    arrays = [
        jax.ShapeDtypeStruct((seq, wide), bf16),
        jax.ShapeDtypeStruct((seq, wide), bf16),
        jax.ShapeDtypeStruct((seq, width), bf16),
    ]
    segments = seg_row[:, None]
    *made, weights, biases = pl.pallas_call(
        lambda *refs: project_kernel(heads, *refs),
        grid_spec=pltpu.PrefetchScalarGridSpec(
            num_scalar_prefetch=1,
            grid=(3,),
            in_specs=[fixed((own_rows, model))] * 3 + rows_of(0)[:1] + [fixed(near.shape)] * 2,
            out_specs=rows_of(0)[1:] + [fixed((3, model, width)), fixed((8, width))],
            scratch_shapes=[pltpu.VMEM((2, 2 * near.shape[0], 128), f32)],
        ),
        out_shape=arrays
        + [jax.ShapeDtypeStruct((3, model, width), bf16), jax.ShapeDtypeStruct((8, width), f32)],
        cost_estimate=cost(3),
        compiler_params=params,
        name="project",
    )(place, *blocks[:3], segments, near, away)
    made = pl.pallas_call(
        lambda *refs: project_last_kernel(heads, *refs),
        grid_spec=pltpu.PrefetchScalarGridSpec(
            num_scalar_prefetch=1,
            grid=(1,),
            in_specs=[fixed((own_rows // 2, model))] * 2
            + rows_of(3)[:1]
            + [fixed((3, model, width)), fixed((8, width))]
            + [pl.BlockSpec(memory_space=pl.ANY)] * 3,
            out_specs=rows_of(3)[1:],
        ),
        out_shape=arrays,
        input_output_aliases={6: 0, 7: 1, 8: 2},
        cost_estimate=cost(1),
        compiler_params=params,
        name="project_last",
    )(place, *blocks[3:], segments, weights, biases, *made)
    return *made, weights


def finish_kernel(ratio, place_ref, *refs):
    head_refs, reduced_ref = refs[:4], refs[4]
    qkv_ref, down_ref, up_ref, out_ref = refs[5:9]
    vector_refs, query_ref, value_ref = refs[9:16], refs[16], refs[17]
    own, model = out_ref.shape
    width = model // 4
    at = ratio * own
    for m in range(4):

        @pl.when(place_ref[1] == m)
        def _():
            for r in range(4):
                for c in range(3):
                    spot = c * model + (m ^ r) * width
                    qkv_ref[:, spot : spot + width] = head_refs[r][:, c * width : (c + 1) * width]

    down_ref[...] = reduced_ref[:at].astype(f32)
    for c in range(ratio):
        up_ref[:, c * model : (c + 1) * model] = reduced_ref[at + c * own : at + (c + 1) * own].astype(f32)
    out_ref[...] = reduced_ref[2 * at : 2 * at + own].astype(f32)
    lines = reduced_ref[2 * at + own :].astype(f32)
    for j, ref in enumerate(vector_refs):
        ref[...] = lines[j : j + 1, : ref.shape[1]]
    for j, ref in enumerate((query_ref, value_ref)):
        ref[...] = head_refs[0][j : j + 1, model - 128 : model - 128 + own]


def finish(place, by_head, reduced, ratio):
    own, model = by_head[0].shape
    vmem = pl.BlockSpec(memory_space=pltpu.VMEM)
    shapes = [(own, 3 * model), (ratio * own, model), (own, ratio * model), (own, model)]
    shapes += [(1, own)] * 6 + [(1, ratio * own)] + [(1, own)] * 2
    return pl.pallas_call(
        lambda *refs: finish_kernel(ratio, *refs),
        in_specs=[pl.BlockSpec(memory_space=pltpu.SMEM)] + [vmem] * 5,
        out_shape=[jax.ShapeDtypeStruct(shape, f32) for shape in shapes],
        name="finish",
    )(place, *by_head, reduced)


def normal_rows(z):
    center = jnp.mean(z, -1, keepdims=True)
    moved = z - center
    rstd = lax.rsqrt(jnp.mean(moved * moved, -1, keepdims=True) + norm_eps)
    return moved * rstd, rstd


def norm_pull(s, hat, rstd):
    inner = jnp.mean(s * hat, -1, keepdims=True)
    return rstd * (s - jnp.mean(s, -1, keepdims=True) - hat * inner)


def gelu_both(x):
    z = jnp.abs(x) * 0.7071067811865476
    t = 1.0 / (1.0 + 0.3275911 * z)
    e = jnp.exp(-(z * z))
    poly = t * (
        0.127414796 + t * (-0.142248368 + t * (0.7107068705 + t * (-0.7265760135 + t * 0.5307027145)))
    )
    tail = poly * e
    cdf = jnp.where(x >= 0.0, 1.0 - tail, tail)
    return x * cdf, cdf + x * (e * 0.3989422804014327)


def spread_vectors(chunks, small_ref, vec_ref):
    pieces, _, model = small_ref.shape

    def spread(block, size):
        count = block.shape[0]
        lane = lax.broadcasted_iota(jnp.int32, (128, model), 1)
        row = lax.broadcasted_iota(jnp.int32, (128, model), 0)
        tile = jnp.where(lax.rem(lane, size) == row, 1.0, 0.0).astype(bf16)
        wide = mm(block, tile)
        lane = lax.broadcasted_iota(jnp.int32, (count, model), 1)
        row = lax.broadcasted_iota(jnp.int32, (count, model), 0)
        keep = lane // size == row
        return jnp.sum(jnp.where(keep, wide, 0.0), 0, keepdims=True)

    vec_ref[...] = jnp.zeros_like(vec_ref)
    for j in range(6):
        vec_ref[j : j + 1, :] = spread(small_ref[:, j, :128], model // pieces)
    share = pieces // chunks
    for c in range(chunks):
        block = small_ref[c * share : (c + 1) * share, 6, :128]
        vec_ref[8 + c : 9 + c, :] = spread(block, model // share)


def gather_vectors(chunks, vec_ref, wide_ref):
    pieces, _, model = wide_ref.shape
    wide_ref[...] = jnp.zeros_like(wide_ref)

    def gather(vector, size, count):
        lane = lax.broadcasted_iota(jnp.int32, (128, model), 1)
        row = lax.broadcasted_iota(jnp.int32, (128, model), 0)
        tile = jnp.where(lax.rem(lane, size) == row, 1.0, 0.0).astype(bf16)
        lane = lax.broadcasted_iota(jnp.int32, (count, model), 1)
        row = lax.broadcasted_iota(jnp.int32, (count, model), 0)
        kept = jnp.where(lane // size == row, vector, 0.0).astype(bf16)
        return mm_nt(kept, tile)

    for j in range(6):
        wide_ref[:, j, :128] = gather(vec_ref[j : j + 1, :], model // pieces, pieces)
    share = pieces // chunks
    for c in range(chunks):
        block = gather(vec_ref[8 + c : 9 + c, :], model // share, share)
        wide_ref[c * share : (c + 1) * share, 6, :128] = block


def middle_kernel(
    groups, chunks, place_ref, x_ref, cot_ref, m0_ref, m1_ref, m2_ref, m3_ref, out_w_ref, up_ref, down_ref, small_ref,
    y_ref, gh1_ref, gm0_ref, gm1_ref, gm2_ref, gm3_ref, kept_ref, sent_ref,
    first_low, first_t, hat1, rstd1, activ_t, slope, total, gffn, gpre, vec_ref,
    gvec_ref, gdown, gup, gout, gwide, gsmall, down_sem, up_sem, out_sem, small_sem,
):
    step = pl.program_id(0)
    rows, model = x_ref.shape
    parts = rows // ROWS
    width = m0_ref.shape[0]
    mixed_refs = (m0_ref, m1_ref, m2_ref, m3_ref)
    gmix_refs = (gm0_ref, gm1_ref, gm2_ref, gm3_ref)

    def group(r):
        return lax.bitwise_xor(place_ref[1], r)

    def out_w(r):
        share = out_w_ref.shape[0] // groups
        return out_w_ref[pl.ds(group(r) * share, share)].reshape(width, model)

    def up_w():
        return up_ref[...].reshape(model, model)

    def down_w():
        return down_ref[...].reshape(model, model)

    pieces, own = out_w_ref.shape[:2]
    share = pieces // groups

    def pair(source, sem, *place):
        return [
            [
                pltpu.make_async_copy(source.at[p], target.at[place], sem.at[p])
                for target in (kept_ref, sent_ref)
            ]
            for p in range(2)
        ]

    def begin(copies):
        for p in range(2):

            @pl.when(place_ref[0] == p)
            def _():
                copies[p][0].start()
                copies[1 - p][1].start()

    def finish(copies):
        for p in range(2):
            copies[p][0].wait()

    def down_copies(slot, chunk):
        return pair(
            gdown.at[slot], down_sem.at[slot], chunk, slice(None), slice(0, chunks * own), slice(None)
        )

    def up_copies(slot, chunk):
        at = pl.ds(pl.multiple_of((chunks + chunk) * own, 8), own)
        return pair(gup.at[slot], up_sem.at[slot], slice(None), slice(None), at, slice(None))

    def out_copies():
        at = slice(2 * chunks * own, 2 * chunks * own + own)
        return pair(gout, out_sem, slice(None), slice(None), at, slice(None))

    def small_copies():
        at = slice(2 * chunks * own + own, 2 * chunks * own + own + 8)
        return pair(gsmall, small_sem, slice(None), slice(None), at, slice(None))

    def vec(i):
        return vec_ref[i : i + 1, :]

    def sums(value):
        return jnp.sum(value, 0, keepdims=True)

    @pl.when(step == 0)
    def _():
        gvec_ref[...] = jnp.zeros_like(gvec_ref)
        spread_vectors(chunks, small_ref, vec_ref)

        def part(i, carry):
            at = pl.ds(pl.multiple_of(i * ROWS, ROWS), ROWS)
            branch = vec(0)
            for r in range(groups):
                branch = branch + mm_tn(mixed_refs[r][:, at], out_w(r))
            hat, rstd = normal_rows(x_ref[at, :].astype(f32) + branch)
            value = hat * vec(1) + vec(2)
            hat1[at, :] = hat
            rstd1[at, :] = jnp.broadcast_to(rstd, (ROWS, 128))
            low = value.astype(bf16)
            first_low[at, :] = low
            first_t[:, at] = low.T
            total[at, :] = value + vec(3)
            return carry

        lax.fori_loop(0, parts, part, 0)

    @pl.when(step < chunks)
    def _():
        def part(i, carry):
            at = pl.ds(pl.multiple_of(i * ROWS, ROWS), ROWS)
            pre = mm(first_low[at, :], up_w()) + vec_ref[pl.ds(8 + step, 1), :]
            value, pull = gelu_both(pre)
            low = value.astype(bf16)
            slope[step, at, :] = pull
            activ_t[step, :, at] = low.T
            total[at, :] += mm(low, down_w())
            return carry

        lax.fori_loop(0, parts, part, 0)

    @pl.when(step == chunks - 1)
    def _():
        def part(i, carry):
            at = pl.ds(pl.multiple_of(i * ROWS, ROWS), ROWS)
            hat, rstd = normal_rows(total[at, :])
            y_ref[at, :] = (hat * vec(4) + vec(5)).astype(bf16)
            g = cot_ref[at, :].astype(f32)
            gh2 = norm_pull(g * vec(4), hat, rstd)
            total[at, :] = gh2
            low = gh2.astype(bf16)
            gffn[at, :] = low
            gvec_ref[3:4, :] += sums(low.astype(f32))
            gvec_ref[4:5, :] += sums(g * hat)
            gvec_ref[5:6, :] += sums(g)
            return carry

        lax.fori_loop(0, parts, part, 0)

    @pl.when(step >= chunks)
    def _():
        chunk = 2 * chunks - 1 - step
        slot = lax.rem(step, 2)

        @pl.when(step >= chunks + 2)
        def _():
            finish(down_copies(slot, chunk))
            finish(up_copies(slot, chunk))

        def part(i, carry):
            at = pl.ds(pl.multiple_of(i * ROWS, ROWS), ROWS)
            low = (mm_nt(gffn[at, :], down_w()) * slope[chunk, at, :]).astype(bf16)
            gpre[at, :] = low
            gvec_ref[pl.ds(8 + chunk, 1), :] += sums(low.astype(f32))
            total[at, :] += mm_nt(low, up_w())
            return carry

        lax.fori_loop(0, parts, part, 0)
        tall = 4 * chunks * own

        def weights_down(i, carry):
            at = pl.ds(pl.multiple_of(i * tall, tall), tall)
            value = mm(activ_t[chunk, at, :], gffn[...]).astype(bf16).reshape(4, chunks * own, model)
            for f in range(4):
                gdown[slot, f % 2, 2 * i + f // 2] = value[f]
            return carry

        lax.fori_loop(0, model // tall, weights_down, 0)
        begin(down_copies(slot, chunk))
        high = 16 * own

        def weights_up(i, carry):
            at = pl.ds(pl.multiple_of(i * high, high), high)
            value = mm(first_t[at, :], gpre[...]).astype(bf16).reshape(16, own, model)
            for f in range(16):
                gup[slot, f % 2, 2 * i + f // 8, (f % 8) // 2] = value[f]
            return carry

        lax.fori_loop(0, model // high, weights_up, 0)
        begin(up_copies(slot, chunk))

    @pl.when(step == 2 * chunks - 1)
    def _():
        def part(i, carry):
            at = pl.ds(pl.multiple_of(i * ROWS, ROWS), ROWS)
            g = total[at, :]
            hat = hat1[at, :]
            gh1 = norm_pull(g * vec(1), hat, rstd1[at, :1])
            gh1_ref[at, :] = gh1
            low = gh1.astype(bf16)
            gpre[at, :] = low
            gvec_ref[0:1, :] += sums(low.astype(f32))
            gvec_ref[1:2, :] += sums(g * hat)
            gvec_ref[2:3, :] += sums(g)
            for r in range(groups):
                gmix_refs[r][:, at] = mm_nt(out_w(r), low).astype(bf16)
            return carry

        lax.fori_loop(0, parts, part, 0)
        for r in range(groups):
            value = mm(mixed_refs[r][...], gpre[...]).astype(bf16).reshape(share, own, model)
            for f in range(share):
                gout[f % 2, group(r), f // 2] = value[f]
        begin(out_copies())
        gather_vectors(chunks, gvec_ref, gwide)
        for g in range(groups):
            for f in range(share):
                gsmall[f % 2, g, f // 2] = gwide[g * share + f].astype(bf16)
        begin(small_copies())
        for back in range(2):
            finish(down_copies(back, 0))
            finish(up_copies(back, 0))
        finish(out_copies())
        finish(small_copies())


def middle(place, x, cot, mixed, packed):
    rows, model = x.shape
    groups = len(mixed)
    width = mixed[0].shape[0]
    pieces = packed.shape[0]
    own = model // pieces
    chunks = (packed.shape[1] - 8 - own) // (2 * own)
    last = 2 * chunks - 1
    back = lambda s: jnp.minimum(s, last - s)
    assert chunks == groups and pieces == 8 * groups
    once = dict(pipeline_mode=pl.Buffered(1))
    fixed2 = lambda a: pl.BlockSpec(a, lambda s: (0, 0), **once)
    vectors_at = own * (2 * chunks + 1) // 8
    cost = pl.CostEstimate(
        flops=2 * rows * model * model * (3 + 6 * chunks),
        bytes_accessed=2 * model * model * (4 * chunks + 8),
        transcendentals=rows * model * chunks,
    )
    share = pieces // groups
    half = jax.ShapeDtypeStruct((groups, share // 2, packed.shape[1], model), bf16)
    return pl.pallas_call(
        lambda *refs: middle_kernel(groups, chunks, *refs),
        grid=(2 * chunks,),
        in_specs=[
            pl.BlockSpec(memory_space=pltpu.SMEM),
            fixed2((rows, model)),
            fixed2((rows, model)),
            fixed2((width, rows)),
            fixed2((width, rows)),
            fixed2((width, rows)),
            fixed2((width, rows)),
            pl.BlockSpec((pieces, own, model), lambda s: (0, 2 * chunks, 0), **once),
            pl.BlockSpec((pieces, own, model), lambda s: (0, chunks + back(s), 0)),
            pl.BlockSpec((pieces // chunks, chunks * own, model), lambda s: (back(s), 0, 0)),
            pl.BlockSpec((pieces, 8, model), lambda s: (0, vectors_at, 0), **once),
        ],
        out_specs=[
            fixed2((rows, model)),
            fixed2((rows, model)),
            fixed2((width, rows)),
            fixed2((width, rows)),
            fixed2((width, rows)),
            fixed2((width, rows)),
            pl.BlockSpec(memory_space=pl.ANY),
            pl.BlockSpec(memory_space=pl.ANY),
        ],
        out_shape=[
            jax.ShapeDtypeStruct((rows, model), bf16),
            jax.ShapeDtypeStruct((rows, model), f32),
            jax.ShapeDtypeStruct((width, rows), bf16),
            jax.ShapeDtypeStruct((width, rows), bf16),
            jax.ShapeDtypeStruct((width, rows), bf16),
            jax.ShapeDtypeStruct((width, rows), bf16),
            half,
            half,
        ],
        scratch_shapes=[
            pltpu.VMEM((rows, model), bf16),
            pltpu.VMEM((model, rows), bf16),
            pltpu.VMEM((rows, model), f32),
            pltpu.VMEM((rows, 128), f32),
            pltpu.VMEM((chunks, model, rows), bf16),
            pltpu.VMEM((chunks, rows, model), f32),
            pltpu.VMEM((rows, model), f32),
            pltpu.VMEM((rows, model), bf16),
            pltpu.VMEM((rows, model), bf16),
            pltpu.VMEM((16, model), f32),
            pltpu.VMEM((16, model), f32),
            pltpu.VMEM((2, 2, share // 2, chunks * own, model), bf16),
            pltpu.VMEM((2, 2, groups, share // 2, own, model), bf16),
            pltpu.VMEM((2, groups, share // 2, own, model), bf16),
            pltpu.VMEM((pieces, 8, model), f32),
            pltpu.VMEM((2, groups, share // 2, 8, model), bf16),
            pltpu.SemaphoreType.DMA((2, 2)),
            pltpu.SemaphoreType.DMA((2, 2)),
            pltpu.SemaphoreType.DMA((2,)),
            pltpu.SemaphoreType.DMA((2,)),
        ],
        cost_estimate=cost,
        compiler_params=pltpu.CompilerParams(vmem_limit_bytes=60 << 20),
        name="middle",
    )(place, x, cot, *mixed, packed, packed, packed, packed)


def by_sp(value, flip):
    groups = lax.axis_size("sp")
    return lax.ppermute(value, "sp", [(i, i ^ flip) for i in range(groups)])


def by_fsdp(value, flip):
    shards = lax.axis_size("fsdp")
    return lax.ppermute(value, "fsdp", [(i, i ^ flip) for i in range(shards)])


def scatter_rows(sent_x, sent_y, mine, low, up):
    half = low.shape[0]
    got_x = by_sp(sent_x, 1).astype(f32)
    got_y = by_sp(sent_y, 2).astype(f32)
    next_y = by_sp((up + got_x[half:]).astype(bf16), 2).astype(f32)
    next_x = by_sp((low + got_y[half:]).astype(bf16), 1).astype(f32)
    return mine + jnp.concatenate([got_x[:half] + next_y, got_y[:half] + next_x], 0)


def unpack(packed, ratio):
    pieces, _, model = packed.shape
    own = model // pieces
    at = ratio * own
    down = packed[:, :at].reshape(ratio * model, model)
    up = packed[:, at : 2 * at].reshape(pieces, ratio, own, model).transpose(1, 0, 2, 3)
    out = packed[:, 2 * at : 2 * at + own].reshape(model, model)
    vectors = [packed[:, 2 * at + own + j, :own].reshape(-1) for j in range(6)]
    vectors.append(packed[:, 2 * at + own + 6, :at].reshape(-1))
    return down, up.reshape(ratio, model, model), out, vectors


def repack(packed, ratio, pieces):
    if packed.shape[0] == pieces:
        return packed
    down, up, out, vectors = unpack(packed, ratio)
    model = out.shape[0]
    own = model // pieces
    up = up.reshape(ratio, pieces, own, model).transpose(1, 0, 2, 3)
    rows = [jnp.pad(v.reshape(pieces, -1), ((0, 0), (0, model - v.shape[0] // pieces))) for v in vectors]
    rows.append(jnp.zeros_like(rows[0]))
    return jnp.concatenate(
        [
            down.reshape(pieces, ratio * own, model),
            up.reshape(pieces, ratio * own, model),
            out.reshape(pieces, own, model),
            jnp.stack(rows, 1),
        ],
        1,
    )


def body(
    tokens,
    segments,
    cotangent,
    w_qkv,
    b_query,
    b_value,
    w_out,
    b_out,
    ln1_gain,
    ln1_bias,
    w_up,
    b_up,
    w_down,
    b_down,
    ln2_gain,
    ln2_bias,
):
    both = ("sp", "fsdp")
    groups = lax.axis_size("sp")
    shards = lax.axis_size("fsdp")
    devices = groups * shards
    rows, model = tokens.shape
    hidden = w_up.shape[1]
    ratio = hidden // model
    own = w_qkv.shape[0]
    pieces = devices if own % 8 == 0 else 8 * groups
    heads_local = HEADS // groups
    width = heads_local * HEAD
    seq_len = rows * groups
    seg_row = segments[0]

    me = lax.axis_index("sp").astype(jnp.int32).reshape(1)
    core = lax.rem(lax.axis_index("fsdp"), 2).astype(jnp.int32).reshape(1)
    direct = pieces == devices

    half = rows // 2
    vectors = [b_out, ln1_gain, ln1_bias, b_down, ln2_gain, ln2_bias, b_up]
    if direct:
        packed, mine = pack(me, w_down, w_up, w_out, w_qkv, vectors, b_query, b_value, groups)
        mine = jnp.stack([mine[0]] + [by_sp(mine[r], r) for r in range(1, groups)])
        mine, moved = lax.optimization_barrier((mine, tokens))
        along_x, along_y = by_sp(moved, 1), by_sp(moved, 2)
        near = jnp.stack([mine] + [by_fsdp(mine, 2 * z) for z in range(1, shards // 2)])
        sent, along_x, along_y = lax.optimization_barrier((near, along_x, along_y))
        away = by_fsdp(sent, 1)
        column = (lax.axis_index("fsdp").astype(jnp.int32) // 2).reshape(1)
        order = jnp.concatenate([me, me, column, core])
    else:
        packed, mine = pack_plain(w_down, w_up, w_out, w_qkv, vectors, b_query, b_value, groups)
        mine = jnp.broadcast_to(mine[:, None], (groups, shards) + mine.shape[1:])
        mine = mine.reshape(devices, own + 8, 3 * width)
        mine = lax.all_to_all(mine, both, split_axis=0, concat_axis=0, tiled=True)
        cut = model // pieces
        biases = lax.dynamic_slice(mine, (me[0] * shards, own, 0), (shards, 2, own))
        biases = biases.transpose(1, 0, 2).reshape(2, 8, cut).transpose(1, 0, 2)
        biases = jnp.pad(biases, ((0, 0), (0, 6), (0, 3 * width - cut)))
        mine = mine[:, :own].reshape(groups, 8, cut, 3 * width)
        mine = jnp.concatenate([mine, jnp.broadcast_to(biases[None], (groups, 8, 8, 3 * width))], 2)
        mine = mine.reshape(groups, 4, 2, cut + 8, 3 * width).transpose(2, 1, 0, 3, 4)
        near, away = mine[0], mine[1]
        order = jnp.concatenate([me, jnp.zeros((3,), jnp.int32)])
        along_x, along_y = by_sp(tokens, 1), by_sp(tokens, 2)
    blocks = tokens, along_x, along_y, by_sp(along_y[:half], 1), by_sp(along_x[half:], 2)
    packed_weights = repack(lax.all_gather(packed, both, axis=0, tiled=False), ratio, pieces)
    queries, keys, values, weights = project(
        order, blocks, seg_row, near, away, heads_local
    )
    forward_start, forward_number = windows(seg_row, FQ, FK, 128)
    backward_start, backward_number = windows(seg_row, BK, BQ, 128)
    *attended, logsum = attend_forward(
        queries, keys, values, forward_start, forward_number, me, heads_local
    )
    mixed = [attended[0]] + [by_sp(attended[r], r) for r in range(1, 4)]
    place = jnp.concatenate([core if direct else jnp.zeros_like(core), me])
    output, grad_h1, *grad_mixed, kept, sent = middle(place, tokens, cotangent, mixed, packed_weights)
    grad_heads = [grad_mixed[0]] + [by_sp(grad_mixed[r], r) for r in range(1, 4)]

    if not direct:
        halves = jnp.stack([kept, sent], 2).reshape(pieces, kept.shape[2], model)
        halves = repack(halves, ratio, devices).reshape(groups, shards // 2, 2, -1, model)
        kept = lax.dynamic_index_in_dim(halves, core[0], 2, keepdims=False)
        sent = lax.dynamic_index_in_dim(halves, 1 - core[0], 2, keepdims=False)
    partner = by_fsdp(sent, 1)
    total = (kept.astype(f32) + partner.astype(f32)).astype(bf16)
    total, grad_heads = lax.optimization_barrier((total, grad_heads))
    total = lax.psum_scatter(total.reshape(-1, model), "sp", scatter_dimension=0, tiled=True)
    cores = [[2 * i + c for i in range(shards // 2)] for c in range(2)]
    reduced = lax.psum_scatter(
        total, "fsdp", scatter_dimension=0, tiled=True, axis_index_groups=cores
    )

    *parts, kept, sent = attend_backward(
        queries,
        keys,
        values,
        grad_heads,
        attended,
        logsum,
        backward_start,
        backward_number,
        order,
        blocks,
        weights,
        grad_h1,
        pieces,
        heads_local,
    )
    grad_input = scatter_rows(*parts)
    if direct:
        total = (kept.astype(f32) + by_fsdp(sent, 1).astype(f32)).astype(bf16)
        moved = [by_fsdp(total[z], 2 * z).astype(f32) for z in range(1, shards // 2)]
        total = sum(moved, total[0].astype(f32))
        by_head = [total[0]] + [by_sp(total[r], r) for r in range(1, groups)]
        weights = finish(order, by_head, reduced, ratio)
        vectors = [item.reshape(-1) for item in weights[4:]]
        owned_qkv, owned_down, owned_up, owned_out = weights[:4]
    else:
        cut = model // pieces
        halves = jnp.stack([kept, sent], 2).transpose(1, 0, 2, 3, 4).reshape(pieces, cut, model)
        biases = halves[:8, :2, model - 128 : model - 128 + cut]
        biases = biases.transpose(1, 0, 2).reshape(2, shards, own).transpose(1, 0, 2)
        biases = jnp.pad(biases, ((0, 0), (0, 6), (0, 3 * width - own)))
        halves = halves[:, :, : 3 * width].reshape(devices, own, 3 * width)
        halves = jnp.concatenate([halves, jnp.tile(biases, (groups, 1, 1))], 1)
        halves = lax.all_to_all(halves, both, split_axis=0, concat_axis=0, tiled=True)
        halves = jnp.sum(halves.reshape(groups, shards, own + 8, 3 * width).astype(f32), 1)
        bias_sums = lax.dynamic_slice(halves, (me[0], own, 0), (1, 2, own))[0]
        by_head = halves[:, :own].reshape(groups, own, 3, width).transpose(1, 2, 0, 3)
        owned_qkv = by_head.reshape(own, 3 * model)
        at = ratio * own
        reduced = reduced.astype(f32)
        owned_up = reduced[at : 2 * at].reshape(ratio, own, model).transpose(1, 0, 2)
        owned_up = owned_up.reshape(own, hidden)
        owned_down, owned_out = reduced[:at], reduced[2 * at : 2 * at + own]
        tail = reduced[2 * at + own :]
        vectors = [tail[i, :own] for i in range(6)] + [tail[6, :at], bias_sums[0], bias_sums[1]]
    return (
        output,
        grad_input,
        owned_qkv,
        vectors[7],
        vectors[8],
        owned_out,
        *vectors[:3],
        owned_up,
        vectors[6],
        owned_down,
        *vectors[3:6],
    )


def solution(mesh):
    in_specs = (
        P(("fsdp", "sp"), None),
        P("fsdp", None),
        P(("fsdp", "sp"), None),
        P(("sp", "fsdp"), None),
        P(("sp", "fsdp")),
        P(("sp", "fsdp")),
        P(("sp", "fsdp"), None),
        P(("sp", "fsdp")),
        P(("sp", "fsdp")),
        P(("sp", "fsdp")),
        P(("sp", "fsdp"), None),
        P(("sp", "fsdp")),
        P(("sp", "fsdp"), None),
        P(("sp", "fsdp")),
        P(("sp", "fsdp")),
        P(("sp", "fsdp")),
    )
    out_specs = (
        P(("fsdp", "sp"), None),
        P(("fsdp", "sp"), None),
        P(("sp", "fsdp"), None),
        P(("sp", "fsdp")),
        P(("sp", "fsdp")),
        P(("sp", "fsdp"), None),
        P(("sp", "fsdp")),
        P(("sp", "fsdp")),
        P(("sp", "fsdp")),
        P(("sp", "fsdp"), None),
        P(("sp", "fsdp")),
        P(("sp", "fsdp"), None),
        P(("sp", "fsdp")),
        P(("sp", "fsdp")),
        P(("sp", "fsdp")),
    )
    return jax.shard_map(body, mesh=mesh, in_specs=in_specs, out_specs=out_specs, check_vma=False)
```

```python
import jax
import jax.numpy as jnp
from jax import lax
from jax.experimental import pallas as pl
from jax.experimental.pallas import tpu as pltpu
from jax.sharding import PartitionSpec as P

HEADS = 12
HEAD = 64
IDS = 32
far = 1e30
FQ, FK = 512, 512
BQ, BK = 512, 256
ROWS = 384
f32 = jnp.float32
bf16 = jnp.bfloat16
norm_eps = 1e-06


def padded_width(width):
    return -(-(width + IDS) // 128) * 128


def spans(seg_row, block):
    seq = seg_row.shape[0]
    count = seq // block
    first = seg_row[::block]
    last = seg_row[block - 1 :: block]
    lo = jnp.sum((seg_row[None, :] < first[:, None]).astype(jnp.int32), 1)
    hi = jnp.sum((seg_row[None, :] <= last[:, None]).astype(jnp.int32), 1)
    return lo, hi


def windows(seg_row, block, step, grain):
    lo, hi = spans(seg_row, block)
    seq = seg_row.shape[0]
    start = lo // grain * grain
    number = -(-(hi - start) // step)
    start = jnp.minimum(start, seq - number * step)
    return start.astype(jnp.int32), number.astype(jnp.int32)


def lanes_of(head, shape):
    lane = lax.broadcasted_iota(jnp.int32, shape, len(shape) - 1)
    return (lane >= head * HEAD) & (lane < (head + 1) * HEAD)


def mm(a, b):
    return jnp.dot(a, b, preferred_element_type=f32)


def mm_nt(a, b):
    return lax.dot_general(a, b, (((1,), (1,)), ((), ())), preferred_element_type=f32)


def mm_tn(a, b):
    return lax.dot_general(a, b, (((0,), (0,)), ((), ())), preferred_element_type=f32)


def forward_kernel(
    heads, start_ref, number_ref, me_ref, q_ref, k_ref, v_ref,
    o0_ref, o1_ref, o2_ref, o3_ref, lse_ref, kh, vt, scores, acc,
):
    step = pl.program_id(0)
    seq, wide = k_ref.shape
    width = heads * HEAD
    tall = HEAD + 16

    @pl.when(step == 0)
    def _():
        row = lax.broadcasted_iota(jnp.int32, (16, FK), 0)
        ones = jnp.where(row == 0, 1.0, 0.0).astype(bf16)

        def part(i, carry):
            rows = pl.ds(pl.multiple_of(i * FK, FK), FK)
            k = k_ref[rows, :]
            lane = lax.broadcasted_iota(jnp.int32, k.shape, 1)
            turned = v_ref[rows, :].T
            for h in range(heads):
                keep = lanes_of(h, k.shape) | (lane >= width)
                kept = jnp.where(keep, k, jnp.zeros_like(k))
                for c in range(FK // 128):
                    at = pl.multiple_of(i * (FK * heads) + (c * heads + h) * 128, 128)
                    kh[pl.ds(at, 128), :] = kept[c * 128 : (c + 1) * 128]
                vt[h * tall : h * tall + HEAD, rows] = turned[h * HEAD : (h + 1) * HEAD]
                vt[h * tall + HEAD : (h + 1) * tall, rows] = ones
            return carry

        lax.fori_loop(0, seq // FK, part, 0)

    q = q_ref[...]
    start = start_ref[step]
    number = number_ref[step]

    def score(j, tops):
        at = pl.multiple_of((start + j * FK) * heads, 128)
        every = mm_nt(kh[pl.ds(at, FK * heads), :], q)
        news = list(tops)
        for c in range(FK // 128):
            for h in range(heads):
                s = every[(c * heads + h) * 128 : (c * heads + h + 1) * 128]
                scores[h, pl.ds(pl.multiple_of(j * FK + c * 128, 128), 128), :] = s
                news[h] = jnp.maximum(news[h], jnp.max(s.reshape(16, 8, FQ), 0))
        return tuple(news)

    tops = lax.fori_loop(0, number, score, (jnp.full((8, FQ), -jnp.inf, f32),) * heads)
    tops = [jnp.max(top, 0, keepdims=True) for top in tops]
    acc[...] = jnp.zeros_like(acc)

    def mix(j, carry):
        rows = pl.ds(pl.multiple_of(start + j * FK, 128), FK)
        out = pl.ds(pl.multiple_of(j * FK, FK), FK)
        for h in range(heads):
            p = jnp.exp(scores[h, out, :] - tops[h]).astype(bf16)
            acc[h] += mm(vt[h * tall : (h + 1) * tall, rows], p)
        return carry

    lax.fori_loop(0, number, mix, 0)
    outs = []
    for h in range(heads):
        total = acc[h, HEAD : HEAD + 1, :]
        outs.append(acc[h, :HEAD, :] / total)
        lse_ref[h : h + 1, :] = tops[h] + jnp.log(total)
    mixed = jnp.concatenate(outs, 0).astype(bf16)
    per = o0_ref.shape[1] // 256
    for u in range(FQ // 256):
        block = step * (FQ // 256) + u
        at = pl.ds(pl.multiple_of(lax.rem(block, per) * 256, 256), 256)
        slot = lax.bitwise_xor(block // per, me_ref[0])
        for r, out_ref in enumerate((o0_ref, o1_ref, o2_ref, o3_ref)):

            @pl.when(slot == r)
            def _():
                out_ref[:, at] = mixed[:, u * 256 : (u + 1) * 256]


def attend_forward(q, k, v, starts, numbers, me, heads):
    seq, wide = q.shape
    width = heads * HEAD
    steps = seq // FQ
    cost = pl.CostEstimate(
        flops=2 * heads * seq * seq * HEAD, bytes_accessed=8 * seq * wide, transcendentals=heads * seq * seq // 3
    )
    return pl.pallas_call(
        lambda *refs: forward_kernel(heads, *refs),
        grid_spec=pltpu.PrefetchScalarGridSpec(
            num_scalar_prefetch=3,
            grid=(steps,),
            in_specs=[
                pl.BlockSpec((FQ, wide), lambda i, a, b, m: (i, 0)),
                pl.BlockSpec((seq, wide), lambda i, a, b, m: (0, 0)),
                pl.BlockSpec((seq, width), lambda i, a, b, m: (0, 0)),
            ],
            out_specs=[
                pl.BlockSpec((width, seq // 4), lambda i, a, b, m: (0, 0)),
                pl.BlockSpec((width, seq // 4), lambda i, a, b, m: (0, 0)),
                pl.BlockSpec((width, seq // 4), lambda i, a, b, m: (0, 0)),
                pl.BlockSpec((width, seq // 4), lambda i, a, b, m: (0, 0)),
                pl.BlockSpec((8, FQ), lambda i, a, b, m: (0, i)),
            ],
            scratch_shapes=[
                pltpu.VMEM((heads * seq, wide), bf16),
                pltpu.VMEM((heads * (HEAD + 16), seq), bf16),
                pltpu.VMEM((heads, seq, FQ), f32),
                pltpu.VMEM((heads, HEAD + 16, FQ), f32),
            ],
        ),
        out_shape=[
            jax.ShapeDtypeStruct((width, seq // 4), bf16),
            jax.ShapeDtypeStruct((width, seq // 4), bf16),
            jax.ShapeDtypeStruct((width, seq // 4), bf16),
            jax.ShapeDtypeStruct((width, seq // 4), bf16),
            jax.ShapeDtypeStruct((8, seq), f32),
        ],
        cost_estimate=cost,
        compiler_params=pltpu.CompilerParams(vmem_limit_bytes=48 << 20),
        name="attend_forward",
    )(starts, numbers, me, q, k, v)


def backward_kernel(
    heads, start_ref, number_ref, me_ref, q_ref, k_ref, v_ref,
    g0_ref, g1_ref, g2_ref, g3_ref, o0_ref, o1_ref, o2_ref, o3_ref, lse_ref, w_ref, gh1_ref,
    sx_ref, sy_ref, mine_ref, low_ref, up_ref, turned,
    qt, gt, dqt, delta, dkt, dvt, kh, vh, grads,
):
    step = pl.program_id(0)
    seq, wide = q_ref.shape
    width = heads * HEAD
    own_rows = seq // 4
    per = own_rows // 256
    me = me_ref[0]

    @pl.when(step == 0)
    def _():
        def part(i, carry):
            rows = pl.ds(pl.multiple_of(i * 256, 256), 256)
            at = pl.ds(pl.multiple_of(lax.rem(i, per) * 256, 256), 256)
            slot = lax.bitwise_xor(i // per, me)
            qt[:, rows] = q_ref[rows, :].T[:width]
            dqt[:, rows] = jnp.zeros((width, 256), f32)
            pairs = ((g0_ref, o0_ref), (g1_ref, o1_ref), (g2_ref, o2_ref), (g3_ref, o3_ref))
            for r, (g_ref, o_ref) in enumerate(pairs):

                @pl.when(slot == r)
                def _():
                    g = g_ref[:, at]
                    gt[:, rows] = g
                    product = g.astype(f32) * o_ref[:, at].astype(f32)
                    for h in range(heads):
                        mine = slice(h * HEAD, (h + 1) * HEAD)
                        delta[h : h + 1, rows] = jnp.sum(product[mine], 0, keepdims=True)

            return carry

        lax.fori_loop(0, seq // 256, part, 0)

    start = start_ref[step]
    k = k_ref[...]
    v = v_ref[...]
    lane = lax.broadcasted_iota(jnp.int32, k.shape, 1)
    for h in range(heads):
        part = slice(h * BK, (h + 1) * BK)
        kh[part, :] = jnp.where(lanes_of(h, k.shape) | (lane >= width), k, jnp.zeros_like(k))
        vh[part, :] = jnp.where(lanes_of(h, v.shape), v, jnp.zeros_like(v))
    kt = k.T
    dkt[...] = jnp.zeros_like(dkt)
    dvt[...] = jnp.zeros_like(dvt)

    def one(i, carry):
        rows = pl.ds(pl.multiple_of(start + i * BQ, 128), BQ)
        q = q_ref[rows, :]
        ss = mm_nt(kh[...], q)
        dps = mm(vh[...], gt[:, rows])
        for h in range(heads):
            mine = slice(h * HEAD, (h + 1) * HEAD)
            part = slice(h * BK, (h + 1) * BK)
            p = jnp.exp(ss[part] - lse_ref[h : h + 1, rows])
            dp = dps[part]
            ds = (p * (dp - delta[h : h + 1, rows])).astype(bf16)
            dvt[mine, :] += mm_nt(gt[mine, rows], p.astype(bf16))
            dkt[mine, :] += mm_nt(qt[mine, rows], ds)
            dqt[mine, rows] += mm(kt[mine, :], ds)
        return carry

    lax.fori_loop(0, number_ref[step], one, 0)
    here = pl.ds(pl.multiple_of(step * BK, BK), BK)
    for c, total in ((1, dkt), (2, dvt)):
        low = total[...].astype(bf16)
        turned[c * width : (c + 1) * width, here] = low
        grads[c, here, :] = low.T

    @pl.when(step == pl.num_programs(0) - 1)
    def _():
        def part(i, carry):
            rows = pl.ds(pl.multiple_of(i * 256, 256), 256)
            low = (dqt[:, rows] * 0.125).astype(bf16)
            turned[:width, rows] = low
            grads[0, rows, :] = low.T
            return carry

        lax.fori_loop(0, seq // 256, part, 0)
        half = own_rows // 2

        def back(i, carry):
            def rows_of(lower):
                at = pl.ds(pl.multiple_of(i * own_rows + lower * half, 128), half)
                value = mm_nt(grads[0, at, :], w_ref[0])
                value = value + mm_nt(grads[1, at, :], w_ref[1])
                return value + mm_nt(grads[2, at, :], w_ref[2])

            slot = lax.bitwise_xor(i, me)
            for lower in range(2):
                value = rows_of(lower)
                here = slice(lower * half, (lower + 1) * half)

                @pl.when(slot == 0)
                def _():
                    mine_ref[here, :] = value + gh1_ref[here, :]

                @pl.when(slot == 1)
                def _():
                    if lower:
                        low_ref[...] = value
                    else:
                        sx_ref[:half] = value.astype(bf16)

                @pl.when(slot == 2)
                def _():
                    if lower:
                        sy_ref[:half] = value.astype(bf16)
                    else:
                        up_ref[...] = value

                @pl.when(slot == 3)
                def _():
                    if lower:
                        sy_ref[half:] = value.astype(bf16)
                    else:
                        sx_ref[half:] = value.astype(bf16)

            return carry

        lax.fori_loop(0, 4, back, 0)


def attend_backward(q, k, v, g, o, lse, starts, numbers, place, w, gh1, heads):
    seq, wide = q.shape
    width = heads * HEAD
    steps = seq // BK
    own_rows, model = gh1.shape
    half = own_rows // 2
    once = dict(pipeline_mode=pl.Buffered(1))
    whole = lambda a: pl.BlockSpec(a, lambda i, a_, b_, m_: (0,) * len(a), **once)
    cost = pl.CostEstimate(
        flops=5 * heads * seq * seq * HEAD + 6 * seq * model * width,
        bytes_accessed=16 * seq * wide,
        transcendentals=heads * seq * seq // 3,
    )
    return pl.pallas_call(
        lambda *refs: backward_kernel(heads, *refs),
        grid_spec=pltpu.PrefetchScalarGridSpec(
            num_scalar_prefetch=3,
            grid=(steps,),
            in_specs=[
                whole((seq, wide)),
                pl.BlockSpec((BK, wide), lambda i, a, b, m: (i, 0)),
                pl.BlockSpec((BK, width), lambda i, a, b, m: (i, 0)),
            ]
            + [whole((width, own_rows))] * 8
            + [whole((8, seq))]
            + [whole((3, model, width)), whole((own_rows, model))],
            out_specs=[
                whole((own_rows, model)),
                whole((own_rows, model)),
                whole((own_rows, model)),
                whole((own_rows // 2, model)),
                whole((own_rows // 2, model)),
                whole((3 * width, seq)),
            ],
            scratch_shapes=[
                pltpu.VMEM((width, seq), bf16),
                pltpu.VMEM((width, seq), bf16),
                pltpu.VMEM((width, seq), f32),
                pltpu.VMEM((8, seq), f32),
                pltpu.VMEM((width, BK), f32),
                pltpu.VMEM((width, BK), f32),
                pltpu.VMEM((heads * BK, wide), bf16),
                pltpu.VMEM((heads * BK, width), bf16),
                pltpu.VMEM((3, seq, width), bf16),
            ],
        ),
        out_shape=[
            jax.ShapeDtypeStruct((own_rows, model), bf16),
            jax.ShapeDtypeStruct((own_rows, model), bf16),
            jax.ShapeDtypeStruct((own_rows, model), f32),
            jax.ShapeDtypeStruct((own_rows // 2, model), f32),
            jax.ShapeDtypeStruct((own_rows // 2, model), f32),
            jax.ShapeDtypeStruct((3 * width, seq), bf16),
        ],
        cost_estimate=cost,
        compiler_params=pltpu.CompilerParams(vmem_limit_bytes=60 << 20),
        name="attend_backward",
    )(starts, numbers, place, q, k, v, *g, *o, lse, w, gh1)


def weight_kernel(me_ref, turned, x0_ref, x1_ref, x2_ref, x3u_ref, x3l_ref, kept_ref, sent_ref, rows_ref):
    seq = turned.shape[1]
    width = turned.shape[0] // 3
    model = x0_ref.shape[1]
    columns, _, own = kept_ref.shape[:3]
    shards = 2 * columns
    lane = lax.broadcasted_iota(jnp.int32, (128, width), 1)
    row = lax.broadcasted_iota(jnp.int32, (128, width), 0)
    tile = jnp.where(lax.rem(lane, own) == row, 1.0, 0.0).astype(bf16)
    lane = lax.broadcasted_iota(jnp.int32, (shards, width), 1)
    row = lax.broadcasted_iota(jnp.int32, (shards, width), 0)
    ones = jnp.ones((8, seq), bf16)
    rows_ref[...] = jnp.zeros_like(rows_ref)
    for j, c in enumerate((0, 2)):
        sums = mm_nt(ones, turned[c * width : (c + 1) * width, :])[:1]
        rows_ref[:, j, :] = mm_nt(jnp.where(lane // own == row, sums, 0.0).astype(bf16), tile)
    me = me_ref[0]
    own_rows = x0_ref.shape[0]
    total = jnp.zeros((3 * width, model), f32)
    for r, parts in enumerate(((x0_ref,), (x1_ref,), (x2_ref,), (x3u_ref, x3l_ref))):
        first = lax.bitwise_xor(me, r) * own_rows
        for part_ref in parts:
            count = part_ref.shape[0]
            total = total + mm(turned[:, pl.ds(pl.multiple_of(first, 128), count)], part_ref[...])
            first = first + count
    value = total.T.astype(bf16).reshape(4 * shards, own, 3 * width)
    for core in range(2):

        @pl.when(me_ref[3] == core)
        def _():
            for piece in range(4 * shards):
                group, shard = piece // shards, piece % shards
                target = kept_ref if shard % 2 == core else sent_ref
                z = lax.bitwise_xor(me_ref[2], shard // 2)
                r = lax.bitwise_xor(me_ref[1], group)
                target[z, r, :, : 3 * width] = value[piece]
                target[z, r, :, 3 * width :] = jnp.zeros((own, model - 3 * width), bf16)
                target[z, r, :8, model - 128 :] = rows_ref[shard].astype(bf16)


def weight_gradient(place, turned, x, pieces):
    model = x[0].shape[1]
    own = model // pieces
    vmem = pl.BlockSpec(memory_space=pltpu.VMEM)
    return pl.pallas_call(
        weight_kernel,
        in_specs=[pl.BlockSpec(memory_space=pltpu.SMEM)] + [vmem] * 6,
        out_shape=[jax.ShapeDtypeStruct((pieces // 8, 4, own, model), bf16)] * 2,
        scratch_shapes=[pltpu.VMEM((pieces // 4, 8, 128), f32)],
        cost_estimate=pl.CostEstimate(
            flops=16 * turned.size * model, bytes_accessed=2 * turned.size * 3, transcendentals=0
        ),
        compiler_params=pltpu.CompilerParams(vmem_limit_bytes=40 << 20),
        name="weight_gradient",
    )(place, turned, *x)


def pack_kernel(ratio, groups, me_ref, down_ref, up_ref, out_ref, qkv_ref, *refs):
    vectors, (query_ref, value_ref, packed_ref, spread_ref, rows_ref) = refs[:-5], refs[-5:]
    own, model = out_ref.shape
    width = model // groups
    rows_ref[...] = jnp.zeros_like(rows_ref)
    rows_ref[0:1, :own] = query_ref[...].astype(f32)
    rows_ref[1:2, :own] = value_ref[...].astype(f32)
    biases = rows_ref[:, : 3 * width].astype(bf16)
    for g in range(groups):
        parts = [qkv_ref[:, c * model + g * width : c * model + (g + 1) * width] for c in range(3)]
        slot = lax.bitwise_xor(me_ref[0], g)
        spread_ref[slot, :own, :] = jnp.concatenate(parts, 1)
        spread_ref[slot, own:, :] = biases
    at = ratio * own
    packed_ref[:at] = down_ref[...]
    for c in range(ratio):
        packed_ref[at + c * own : at + (c + 1) * own] = up_ref[:, c * model : (c + 1) * model]
    packed_ref[2 * at : 2 * at + own] = out_ref[...]
    rows_ref[...] = jnp.zeros_like(rows_ref)
    for j, vector in enumerate(vectors):
        rows_ref[j : j + 1, : vector.shape[1]] = vector[...].astype(f32)
    packed_ref[2 * at + own :] = rows_ref[...].astype(bf16)


def pack(me, w_down, w_up, w_out, w_qkv, vectors, b_query, b_value, groups):
    own, model = w_out.shape
    ratio = w_down.shape[0] // own
    width = model // groups
    vmem = pl.BlockSpec(memory_space=pltpu.VMEM)
    return pl.pallas_call(
        lambda *refs: pack_kernel(ratio, groups, *refs),
        in_specs=[pl.BlockSpec(memory_space=pltpu.SMEM)] + [vmem] * (6 + len(vectors)),
        out_shape=[
            jax.ShapeDtypeStruct((own * (2 * ratio + 1) + 8, model), bf16),
            jax.ShapeDtypeStruct((groups, own + 8, 3 * width), bf16),
        ],
        scratch_shapes=[pltpu.VMEM((8, model), f32)],
        name="pack",
    )(me, w_down, w_up, w_out, w_qkv, *[item[None] for item in vectors], b_query[None], b_value[None])


def pack_plain(w_down, w_up, w_out, w_qkv, vectors, b_query, b_value, groups):
    own, model = w_out.shape
    ratio = w_down.shape[0] // own
    width = model // groups
    up_blocks = [w_up[:, c * model : (c + 1) * model] for c in range(ratio)]
    rows = [jnp.pad(item, (0, model - item.shape[0]))[None] for item in vectors]
    rows.append(jnp.zeros((8 - len(rows), model), bf16))
    packed = jnp.concatenate([w_down] + up_blocks + [w_out] + rows, 0)
    block = w_qkv.reshape(own, 3, groups, width).transpose(2, 0, 1, 3).reshape(groups, own, 3 * width)
    rows = jnp.pad(jnp.stack([b_query, b_value]), ((0, 6), (0, 3 * width - own)))
    return packed, jnp.concatenate([block, jnp.broadcast_to(rows, (groups, 8, 3 * width))], 1)


def project_block(heads, x_ref, first, seg_ref, bias_ref, w_ref, q_ref, k_ref, v_ref):
    size = 384
    width = heads * HEAD
    wide = q_ref.shape[1]

    def part(i, carry):
        x = x_ref[pl.ds(pl.multiple_of(i * size, size), size), :]
        at = pl.ds(pl.multiple_of(first + i * size, size), size)
        lane = lax.broadcasted_iota(jnp.int32, (size, wide - width), 1)
        same = lane == seg_ref[at, :]
        q = (mm(x, w_ref[0]) + bias_ref[0:1, :]).astype(bf16)
        q_ref[at, :width] = q * jnp.asarray(0.125, bf16)
        q_ref[at, width:] = jnp.where(same, 1.0, 0.0).astype(bf16)
        k_ref[at, :width] = mm(x, w_ref[1]).astype(bf16)
        k_ref[at, width:] = jnp.where(same, 0.0, -far).astype(bf16)
        v_ref[at, :] = (mm(x, w_ref[2]) + bias_ref[1:2, :]).astype(bf16)
        return carry

    lax.fori_loop(0, x_ref.shape[0] // size, part, 0)


def project_kernel(
    heads, me_ref, x0_ref, x1_ref, x2_ref, seg_ref, near_ref, far_ref,
    q_ref, k_ref, v_ref, wide_w, bias_ref, rows_ref,
):
    step = pl.program_id(0)
    width = heads * HEAD
    own = near_ref.shape[2] - 8
    columns, groups = near_ref.shape[:2]

    @pl.when(step == 0)
    def _():
        for c, part_ref in ((0, near_ref), (1, far_ref)):
            for z in range(columns):
                shard = lax.bitwise_xor(me_ref[2], z) * 2 + lax.bitwise_xor(me_ref[3], c)
                for g in range(groups):
                    piece = lax.bitwise_xor(me_ref[1], g) * (2 * columns) + shard
                    at = pl.ds(pl.multiple_of(piece * own, 8), own)
                    for k in range(3):
                        wide_w[k, at, :] = part_ref[z, g, :own, k * width : (k + 1) * width]
                lines = part_ref[z, 0, own:, :128].astype(f32)
                for k in range(2):
                    rows_ref[k, pl.ds(shard, 1), :] = lines[k : k + 1]
        lane = lax.broadcasted_iota(jnp.int32, (128, width), 1)
        row = lax.broadcasted_iota(jnp.int32, (128, width), 0)
        tile = jnp.where(lax.rem(lane, own) == row, 1.0, 0.0).astype(bf16)
        lane = lax.broadcasted_iota(jnp.int32, (2 * columns, width), 1)
        row = lax.broadcasted_iota(jnp.int32, (2 * columns, width), 0)
        bias_ref[...] = jnp.zeros_like(bias_ref)
        for k in range(2):
            value = jnp.where(lane // own == row, mm(rows_ref[k].astype(bf16), tile), 0.0)
            bias_ref[k : k + 1, :] = jnp.sum(value, 0, keepdims=True)

    for k, part_ref in ((0, x0_ref), (1, x1_ref), (2, x2_ref)):

        @pl.when(step == k)
        def _():
            project_block(heads, part_ref, 0, seg_ref, bias_ref, wide_w, q_ref, k_ref, v_ref)


def project_last_kernel(heads, me_ref, upper_ref, lower_ref, seg_ref, w_ref, bias_ref, *refs):
    project_block(heads, upper_ref, 0, seg_ref, bias_ref, w_ref, *refs[-3:])
    project_block(heads, lower_ref, upper_ref.shape[0], seg_ref, bias_ref, w_ref, *refs[-3:])


def project(place, blocks, seg_row, near, away, heads):
    own_rows, model = blocks[0].shape
    width = heads * HEAD
    wide = padded_width(width)
    seq = 4 * own_rows
    once = dict(pipeline_mode=pl.Buffered(1))
    fixed = lambda a: pl.BlockSpec(a, lambda s, m: (0,) * len(a), **once)

    def rows_of(slot):
        at = lambda s, m: (lax.bitwise_xor(s + slot, m[0]), 0)
        return [pl.BlockSpec((own_rows, n), at) for n in (1, wide, wide, width)]

    def cost(part):
        return pl.CostEstimate(
            flops=6 * part * own_rows * model * width,
            bytes_accessed=4 * part * own_rows * (model + wide),
            transcendentals=0,
        )

    params = pltpu.CompilerParams(vmem_limit_bytes=40 << 20)
    arrays = [
        jax.ShapeDtypeStruct((seq, wide), bf16),
        jax.ShapeDtypeStruct((seq, wide), bf16),
        jax.ShapeDtypeStruct((seq, width), bf16),
    ]
    segments = seg_row[:, None]
    *made, weights, biases = pl.pallas_call(
        lambda *refs: project_kernel(heads, *refs),
        grid_spec=pltpu.PrefetchScalarGridSpec(
            num_scalar_prefetch=1,
            grid=(3,),
            in_specs=[fixed((own_rows, model))] * 3 + rows_of(0)[:1] + [fixed(near.shape)] * 2,
            out_specs=rows_of(0)[1:] + [fixed((3, model, width)), fixed((8, width))],
            scratch_shapes=[pltpu.VMEM((2, 2 * near.shape[0], 128), f32)],
        ),
        out_shape=arrays
        + [jax.ShapeDtypeStruct((3, model, width), bf16), jax.ShapeDtypeStruct((8, width), f32)],
        cost_estimate=cost(3),
        compiler_params=params,
        name="project",
    )(place, *blocks[:3], segments, near, away)
    made = pl.pallas_call(
        lambda *refs: project_last_kernel(heads, *refs),
        grid_spec=pltpu.PrefetchScalarGridSpec(
            num_scalar_prefetch=1,
            grid=(1,),
            in_specs=[fixed((own_rows // 2, model))] * 2
            + rows_of(3)[:1]
            + [fixed((3, model, width)), fixed((8, width))]
            + [pl.BlockSpec(memory_space=pl.ANY)] * 3,
            out_specs=rows_of(3)[1:],
        ),
        out_shape=arrays,
        input_output_aliases={6: 0, 7: 1, 8: 2},
        cost_estimate=cost(1),
        compiler_params=params,
        name="project_last",
    )(place, *blocks[3:], segments, weights, biases, *made)
    return *made, weights


def finish_kernel(ratio, place_ref, *refs):
    head_refs, reduced_ref = refs[:4], refs[4]
    qkv_ref, down_ref, up_ref, out_ref = refs[5:9]
    vector_refs, query_ref, value_ref = refs[9:16], refs[16], refs[17]
    own, model = out_ref.shape
    width = model // 4
    at = ratio * own
    for m in range(4):

        @pl.when(place_ref[1] == m)
        def _():
            for r in range(4):
                for c in range(3):
                    spot = c * model + (m ^ r) * width
                    qkv_ref[:, spot : spot + width] = head_refs[r][:, c * width : (c + 1) * width]

    down_ref[...] = reduced_ref[:at].astype(f32)
    for c in range(ratio):
        up_ref[:, c * model : (c + 1) * model] = reduced_ref[at + c * own : at + (c + 1) * own].astype(f32)
    out_ref[...] = reduced_ref[2 * at : 2 * at + own].astype(f32)
    lines = reduced_ref[2 * at + own :].astype(f32)
    for j, ref in enumerate(vector_refs):
        ref[...] = lines[j : j + 1, : ref.shape[1]]
    for j, ref in enumerate((query_ref, value_ref)):
        ref[...] = head_refs[0][j : j + 1, model - 128 : model - 128 + own]


def finish(place, by_head, reduced, ratio):
    own, model = by_head[0].shape
    vmem = pl.BlockSpec(memory_space=pltpu.VMEM)
    shapes = [(own, 3 * model), (ratio * own, model), (own, ratio * model), (own, model)]
    shapes += [(1, own)] * 6 + [(1, ratio * own)] + [(1, own)] * 2
    return pl.pallas_call(
        lambda *refs: finish_kernel(ratio, *refs),
        in_specs=[pl.BlockSpec(memory_space=pltpu.SMEM)] + [vmem] * 5,
        out_shape=[jax.ShapeDtypeStruct(shape, f32) for shape in shapes],
        name="finish",
    )(place, *by_head, reduced)


def normal_rows(z):
    center = jnp.mean(z, -1, keepdims=True)
    moved = z - center
    rstd = lax.rsqrt(jnp.mean(moved * moved, -1, keepdims=True) + norm_eps)
    return moved * rstd, rstd


def norm_pull(s, hat, rstd):
    inner = jnp.mean(s * hat, -1, keepdims=True)
    return rstd * (s - jnp.mean(s, -1, keepdims=True) - hat * inner)


def gelu_both(x):
    z = jnp.abs(x) * 0.7071067811865476
    t = 1.0 / (1.0 + 0.3275911 * z)
    e = jnp.exp(-(z * z))
    poly = t * (
        0.127414796 + t * (-0.142248368 + t * (0.7107068705 + t * (-0.7265760135 + t * 0.5307027145)))
    )
    tail = poly * e
    cdf = jnp.where(x >= 0.0, 1.0 - tail, tail)
    return x * cdf, cdf + x * (e * 0.3989422804014327)


def spread_vectors(chunks, small_ref, vec_ref):
    pieces, _, model = small_ref.shape

    def spread(block, size):
        count = block.shape[0]
        lane = lax.broadcasted_iota(jnp.int32, (128, model), 1)
        row = lax.broadcasted_iota(jnp.int32, (128, model), 0)
        tile = jnp.where(lax.rem(lane, size) == row, 1.0, 0.0).astype(bf16)
        wide = mm(block, tile)
        lane = lax.broadcasted_iota(jnp.int32, (count, model), 1)
        row = lax.broadcasted_iota(jnp.int32, (count, model), 0)
        keep = lane // size == row
        return jnp.sum(jnp.where(keep, wide, 0.0), 0, keepdims=True)

    vec_ref[...] = jnp.zeros_like(vec_ref)
    for j in range(6):
        vec_ref[j : j + 1, :] = spread(small_ref[:, j, :128], model // pieces)
    share = pieces // chunks
    for c in range(chunks):
        block = small_ref[c * share : (c + 1) * share, 6, :128]
        vec_ref[8 + c : 9 + c, :] = spread(block, model // share)


def gather_vectors(chunks, vec_ref, wide_ref):
    pieces, _, model = wide_ref.shape
    wide_ref[...] = jnp.zeros_like(wide_ref)

    def gather(vector, size, count):
        lane = lax.broadcasted_iota(jnp.int32, (128, model), 1)
        row = lax.broadcasted_iota(jnp.int32, (128, model), 0)
        tile = jnp.where(lax.rem(lane, size) == row, 1.0, 0.0).astype(bf16)
        lane = lax.broadcasted_iota(jnp.int32, (count, model), 1)
        row = lax.broadcasted_iota(jnp.int32, (count, model), 0)
        kept = jnp.where(lane // size == row, vector, 0.0).astype(bf16)
        return mm_nt(kept, tile)

    for j in range(6):
        wide_ref[:, j, :128] = gather(vec_ref[j : j + 1, :], model // pieces, pieces)
    share = pieces // chunks
    for c in range(chunks):
        block = gather(vec_ref[8 + c : 9 + c, :], model // share, share)
        wide_ref[c * share : (c + 1) * share, 6, :128] = block


def middle_kernel(
    groups, chunks, place_ref, x_ref, cot_ref, m0_ref, m1_ref, m2_ref, m3_ref, out_w_ref, up_ref, down_ref, small_ref,
    y_ref, gh1_ref, gm0_ref, gm1_ref, gm2_ref, gm3_ref, kept_ref, sent_ref,
    first_low, first_t, hat1, rstd1, activ_t, slope, total, gffn, gpre, vec_ref,
    gvec_ref, gdown, gup, gout, gwide, gsmall, down_sem, up_sem, out_sem, small_sem,
):
    step = pl.program_id(0)
    rows, model = x_ref.shape
    parts = rows // ROWS
    width = m0_ref.shape[0]
    mixed_refs = (m0_ref, m1_ref, m2_ref, m3_ref)
    gmix_refs = (gm0_ref, gm1_ref, gm2_ref, gm3_ref)

    def group(r):
        return lax.bitwise_xor(place_ref[1], r)

    def out_w(r):
        share = out_w_ref.shape[0] // groups
        return out_w_ref[pl.ds(group(r) * share, share)].reshape(width, model)

    def up_w():
        return up_ref[...].reshape(model, model)

    def down_w():
        return down_ref[...].reshape(model, model)

    pieces, own = out_w_ref.shape[:2]
    share = pieces // groups

    def pair(source, sem, *place):
        return [
            [
                pltpu.make_async_copy(source.at[p], target.at[place], sem.at[p])
                for target in (kept_ref, sent_ref)
            ]
            for p in range(2)
        ]

    def begin(copies):
        for p in range(2):

            @pl.when(place_ref[0] == p)
            def _():
                copies[p][0].start()
                copies[1 - p][1].start()

    def finish(copies):
        for p in range(2):
            copies[p][0].wait()

    def down_copies(slot, chunk):
        return pair(
            gdown.at[slot], down_sem.at[slot], chunk, slice(None), slice(0, chunks * own), slice(None)
        )

    def up_copies(slot, chunk):
        at = pl.ds(pl.multiple_of((chunks + chunk) * own, 8), own)
        return pair(gup.at[slot], up_sem.at[slot], slice(None), slice(None), at, slice(None))

    def out_copies():
        at = slice(2 * chunks * own, 2 * chunks * own + own)
        return pair(gout, out_sem, slice(None), slice(None), at, slice(None))

    def small_copies():
        at = slice(2 * chunks * own + own, 2 * chunks * own + own + 8)
        return pair(gsmall, small_sem, slice(None), slice(None), at, slice(None))

    def vec(i):
        return vec_ref[i : i + 1, :]

    def sums(value):
        return jnp.sum(value, 0, keepdims=True)

    @pl.when(step == 0)
    def _():
        gvec_ref[...] = jnp.zeros_like(gvec_ref)
        spread_vectors(chunks, small_ref, vec_ref)

        def part(i, carry):
            at = pl.ds(pl.multiple_of(i * ROWS, ROWS), ROWS)
            branch = vec(0)
            for r in range(groups):
                branch = branch + mm_tn(mixed_refs[r][:, at], out_w(r))
            hat, rstd = normal_rows(x_ref[at, :].astype(f32) + branch)
            value = hat * vec(1) + vec(2)
            hat1[at, :] = hat
            rstd1[at, :] = jnp.broadcast_to(rstd, (ROWS, 128))
            low = value.astype(bf16)
            first_low[at, :] = low
            first_t[:, at] = low.T
            total[at, :] = value + vec(3)
            return carry

        lax.fori_loop(0, parts, part, 0)

    @pl.when(step < chunks)
    def _():
        def part(i, carry):
            at = pl.ds(pl.multiple_of(i * ROWS, ROWS), ROWS)
            pre = mm(first_low[at, :], up_w()) + vec_ref[pl.ds(8 + step, 1), :]
            value, pull = gelu_both(pre)
            low = value.astype(bf16)
            slope[step, at, :] = pull
            activ_t[step, :, at] = low.T
            total[at, :] += mm(low, down_w())
            return carry

        lax.fori_loop(0, parts, part, 0)

    @pl.when(step == chunks - 1)
    def _():
        def part(i, carry):
            at = pl.ds(pl.multiple_of(i * ROWS, ROWS), ROWS)
            hat, rstd = normal_rows(total[at, :])
            y_ref[at, :] = (hat * vec(4) + vec(5)).astype(bf16)
            g = cot_ref[at, :].astype(f32)
            gh2 = norm_pull(g * vec(4), hat, rstd)
            total[at, :] = gh2
            low = gh2.astype(bf16)
            gffn[at, :] = low
            gvec_ref[3:4, :] += sums(low.astype(f32))
            gvec_ref[4:5, :] += sums(g * hat)
            gvec_ref[5:6, :] += sums(g)
            return carry

        lax.fori_loop(0, parts, part, 0)

    @pl.when(step >= chunks)
    def _():
        chunk = 2 * chunks - 1 - step
        slot = lax.rem(step, 2)

        @pl.when(step >= chunks + 2)
        def _():
            finish(down_copies(slot, chunk))
            finish(up_copies(slot, chunk))

        def part(i, carry):
            at = pl.ds(pl.multiple_of(i * ROWS, ROWS), ROWS)
            low = (mm_nt(gffn[at, :], down_w()) * slope[chunk, at, :]).astype(bf16)
            gpre[at, :] = low
            gvec_ref[pl.ds(8 + chunk, 1), :] += sums(low.astype(f32))
            total[at, :] += mm_nt(low, up_w())
            return carry

        lax.fori_loop(0, parts, part, 0)
        tall = 4 * chunks * own

        def weights_down(i, carry):
            at = pl.ds(pl.multiple_of(i * tall, tall), tall)
            value = mm(activ_t[chunk, at, :], gffn[...]).astype(bf16).reshape(4, chunks * own, model)
            for f in range(4):
                gdown[slot, f % 2, 2 * i + f // 2] = value[f]
            return carry

        lax.fori_loop(0, model // tall, weights_down, 0)
        begin(down_copies(slot, chunk))
        high = 16 * own

        def weights_up(i, carry):
            at = pl.ds(pl.multiple_of(i * high, high), high)
            value = mm(first_t[at, :], gpre[...]).astype(bf16).reshape(16, own, model)
            for f in range(16):
                gup[slot, f % 2, 2 * i + f // 8, (f % 8) // 2] = value[f]
            return carry

        lax.fori_loop(0, model // high, weights_up, 0)
        begin(up_copies(slot, chunk))

    @pl.when(step == 2 * chunks - 1)
    def _():
        def part(i, carry):
            at = pl.ds(pl.multiple_of(i * ROWS, ROWS), ROWS)
            g = total[at, :]
            hat = hat1[at, :]
            gh1 = norm_pull(g * vec(1), hat, rstd1[at, :1])
            gh1_ref[at, :] = gh1
            low = gh1.astype(bf16)
            gpre[at, :] = low
            gvec_ref[0:1, :] += sums(low.astype(f32))
            gvec_ref[1:2, :] += sums(g * hat)
            gvec_ref[2:3, :] += sums(g)
            for r in range(groups):
                gmix_refs[r][:, at] = mm_nt(out_w(r), low).astype(bf16)
            return carry

        lax.fori_loop(0, parts, part, 0)
        for r in range(groups):
            value = mm(mixed_refs[r][...], gpre[...]).astype(bf16).reshape(share, own, model)
            for f in range(share):
                gout[f % 2, group(r), f // 2] = value[f]
        begin(out_copies())
        gather_vectors(chunks, gvec_ref, gwide)
        for g in range(groups):
            for f in range(share):
                gsmall[f % 2, g, f // 2] = gwide[g * share + f].astype(bf16)
        begin(small_copies())
        for back in range(2):
            finish(down_copies(back, 0))
            finish(up_copies(back, 0))
        finish(out_copies())
        finish(small_copies())


def middle(place, x, cot, mixed, packed):
    rows, model = x.shape
    groups = len(mixed)
    width = mixed[0].shape[0]
    pieces = packed.shape[0]
    own = model // pieces
    chunks = (packed.shape[1] - 8 - own) // (2 * own)
    last = 2 * chunks - 1
    back = lambda s: jnp.minimum(s, last - s)
    assert chunks == groups and pieces == 8 * groups
    once = dict(pipeline_mode=pl.Buffered(1))
    fixed2 = lambda a: pl.BlockSpec(a, lambda s: (0, 0), **once)
    vectors_at = own * (2 * chunks + 1) // 8
    cost = pl.CostEstimate(
        flops=2 * rows * model * model * (3 + 6 * chunks),
        bytes_accessed=2 * model * model * (4 * chunks + 8),
        transcendentals=rows * model * chunks,
    )
    share = pieces // groups
    half = jax.ShapeDtypeStruct((groups, share // 2, packed.shape[1], model), bf16)
    return pl.pallas_call(
        lambda *refs: middle_kernel(groups, chunks, *refs),
        grid=(2 * chunks,),
        in_specs=[
            pl.BlockSpec(memory_space=pltpu.SMEM),
            fixed2((rows, model)),
            fixed2((rows, model)),
            fixed2((width, rows)),
            fixed2((width, rows)),
            fixed2((width, rows)),
            fixed2((width, rows)),
            pl.BlockSpec((pieces, own, model), lambda s: (0, 2 * chunks, 0), **once),
            pl.BlockSpec((pieces, own, model), lambda s: (0, chunks + back(s), 0)),
            pl.BlockSpec((pieces // chunks, chunks * own, model), lambda s: (back(s), 0, 0)),
            pl.BlockSpec((pieces, 8, model), lambda s: (0, vectors_at, 0), **once),
        ],
        out_specs=[
            fixed2((rows, model)),
            fixed2((rows, model)),
            fixed2((width, rows)),
            fixed2((width, rows)),
            fixed2((width, rows)),
            fixed2((width, rows)),
            pl.BlockSpec(memory_space=pl.ANY),
            pl.BlockSpec(memory_space=pl.ANY),
        ],
        out_shape=[
            jax.ShapeDtypeStruct((rows, model), bf16),
            jax.ShapeDtypeStruct((rows, model), f32),
            jax.ShapeDtypeStruct((width, rows), bf16),
            jax.ShapeDtypeStruct((width, rows), bf16),
            jax.ShapeDtypeStruct((width, rows), bf16),
            jax.ShapeDtypeStruct((width, rows), bf16),
            half,
            half,
        ],
        scratch_shapes=[
            pltpu.VMEM((rows, model), bf16),
            pltpu.VMEM((model, rows), bf16),
            pltpu.VMEM((rows, model), f32),
            pltpu.VMEM((rows, 128), f32),
            pltpu.VMEM((chunks, model, rows), bf16),
            pltpu.VMEM((chunks, rows, model), f32),
            pltpu.VMEM((rows, model), f32),
            pltpu.VMEM((rows, model), bf16),
            pltpu.VMEM((rows, model), bf16),
            pltpu.VMEM((16, model), f32),
            pltpu.VMEM((16, model), f32),
            pltpu.VMEM((2, 2, share // 2, chunks * own, model), bf16),
            pltpu.VMEM((2, 2, groups, share // 2, own, model), bf16),
            pltpu.VMEM((2, groups, share // 2, own, model), bf16),
            pltpu.VMEM((pieces, 8, model), f32),
            pltpu.VMEM((2, groups, share // 2, 8, model), bf16),
            pltpu.SemaphoreType.DMA((2, 2)),
            pltpu.SemaphoreType.DMA((2, 2)),
            pltpu.SemaphoreType.DMA((2,)),
            pltpu.SemaphoreType.DMA((2,)),
        ],
        cost_estimate=cost,
        compiler_params=pltpu.CompilerParams(vmem_limit_bytes=60 << 20),
        name="middle",
    )(place, x, cot, *mixed, packed, packed, packed, packed)


def by_sp(value, flip):
    groups = lax.axis_size("sp")
    return lax.ppermute(value, "sp", [(i, i ^ flip) for i in range(groups)])


def by_fsdp(value, flip):
    shards = lax.axis_size("fsdp")
    return lax.ppermute(value, "fsdp", [(i, i ^ flip) for i in range(shards)])


def scatter_rows(sent_x, sent_y, mine, low, up):
    half = low.shape[0]
    got_x, got_y = lax.optimization_barrier((by_sp(sent_x, 1), by_sp(sent_y, 2)))
    next_y = by_sp((up + got_x[half:].astype(f32)).astype(bf16), 2)
    next_x = by_sp((low + got_y[half:].astype(f32)).astype(bf16), 1)
    upper = got_x[:half].astype(f32) + next_y.astype(f32)
    lower = got_y[:half].astype(f32) + next_x.astype(f32)
    return mine + jnp.concatenate([upper, lower], 0)


def unpack(packed, ratio):
    pieces, _, model = packed.shape
    own = model // pieces
    at = ratio * own
    down = packed[:, :at].reshape(ratio * model, model)
    up = packed[:, at : 2 * at].reshape(pieces, ratio, own, model).transpose(1, 0, 2, 3)
    out = packed[:, 2 * at : 2 * at + own].reshape(model, model)
    vectors = [packed[:, 2 * at + own + j, :own].reshape(-1) for j in range(6)]
    vectors.append(packed[:, 2 * at + own + 6, :at].reshape(-1))
    return down, up.reshape(ratio, model, model), out, vectors


def repack(packed, ratio, pieces):
    if packed.shape[0] == pieces:
        return packed
    down, up, out, vectors = unpack(packed, ratio)
    model = out.shape[0]
    own = model // pieces
    up = up.reshape(ratio, pieces, own, model).transpose(1, 0, 2, 3)
    rows = [jnp.pad(v.reshape(pieces, -1), ((0, 0), (0, model - v.shape[0] // pieces))) for v in vectors]
    rows.append(jnp.zeros_like(rows[0]))
    return jnp.concatenate(
        [
            down.reshape(pieces, ratio * own, model),
            up.reshape(pieces, ratio * own, model),
            out.reshape(pieces, own, model),
            jnp.stack(rows, 1),
        ],
        1,
    )


def body(
    tokens,
    segments,
    cotangent,
    w_qkv,
    b_query,
    b_value,
    w_out,
    b_out,
    ln1_gain,
    ln1_bias,
    w_up,
    b_up,
    w_down,
    b_down,
    ln2_gain,
    ln2_bias,
):
    both = ("sp", "fsdp")
    groups = lax.axis_size("sp")
    shards = lax.axis_size("fsdp")
    devices = groups * shards
    rows, model = tokens.shape
    hidden = w_up.shape[1]
    ratio = hidden // model
    own = w_qkv.shape[0]
    pieces = devices if own % 8 == 0 else 8 * groups
    heads_local = HEADS // groups
    width = heads_local * HEAD
    seq_len = rows * groups
    seg_row = segments[0]

    me = lax.axis_index("sp").astype(jnp.int32).reshape(1)
    core = lax.rem(lax.axis_index("fsdp"), 2).astype(jnp.int32).reshape(1)
    direct = pieces == devices

    half = rows // 2
    vectors = [b_out, ln1_gain, ln1_bias, b_down, ln2_gain, ln2_bias, b_up]
    if direct:
        packed, mine = pack(me, w_down, w_up, w_out, w_qkv, vectors, b_query, b_value, groups)
        mine = jnp.stack([mine[0]] + [by_sp(mine[r], r) for r in range(1, groups)])
        mine, moved = lax.optimization_barrier((mine, tokens))
        along_x, along_y = by_sp(moved, 1), by_sp(moved, 2)
        near = jnp.stack([mine] + [by_fsdp(mine, 2 * z) for z in range(1, shards // 2)])
        sent, along_x, along_y = lax.optimization_barrier((near, along_x, along_y))
        away = by_fsdp(sent, 1)
        column = (lax.axis_index("fsdp").astype(jnp.int32) // 2).reshape(1)
        order = jnp.concatenate([me, me, column, core])
    else:
        packed, mine = pack_plain(w_down, w_up, w_out, w_qkv, vectors, b_query, b_value, groups)
        mine = jnp.broadcast_to(mine[:, None], (groups, shards) + mine.shape[1:])
        mine = mine.reshape(devices, own + 8, 3 * width)
        mine = lax.all_to_all(mine, both, split_axis=0, concat_axis=0, tiled=True)
        cut = model // pieces
        biases = lax.dynamic_slice(mine, (me[0] * shards, own, 0), (shards, 2, own))
        biases = biases.transpose(1, 0, 2).reshape(2, 8, cut).transpose(1, 0, 2)
        biases = jnp.pad(biases, ((0, 0), (0, 6), (0, 3 * width - cut)))
        mine = mine[:, :own].reshape(groups, 8, cut, 3 * width)
        mine = jnp.concatenate([mine, jnp.broadcast_to(biases[None], (groups, 8, 8, 3 * width))], 2)
        mine = mine.reshape(groups, 4, 2, cut + 8, 3 * width).transpose(2, 1, 0, 3, 4)
        near, away = mine[0], mine[1]
        order = jnp.concatenate([me, jnp.zeros((3,), jnp.int32)])
        along_x, along_y = by_sp(tokens, 1), by_sp(tokens, 2)
    blocks = tokens, along_x, along_y, by_sp(along_y[:half], 1), by_sp(along_x[half:], 2)
    packed_weights = repack(lax.all_gather(packed, both, axis=0, tiled=False), ratio, pieces)
    queries, keys, values, weights = project(
        order, blocks, seg_row, near, away, heads_local
    )
    forward_start, forward_number = windows(seg_row, FQ, FK, 128)
    backward_start, backward_number = windows(seg_row, BK, BQ, 128)
    *attended, logsum = attend_forward(
        queries, keys, values, forward_start, forward_number, me, heads_local
    )
    mixed = [attended[0]] + [by_sp(attended[r], r) for r in range(1, 4)]
    place = jnp.concatenate([core if direct else jnp.zeros_like(core), me])
    output, grad_h1, *grad_mixed, kept, sent = middle(place, tokens, cotangent, mixed, packed_weights)
    grad_heads = [grad_mixed[0]] + [by_sp(grad_mixed[r], r) for r in range(1, 4)]

    if not direct:
        halves = jnp.stack([kept, sent], 2).reshape(pieces, kept.shape[2], model)
        halves = repack(halves, ratio, devices).reshape(groups, shards // 2, 2, -1, model)
        kept = lax.dynamic_index_in_dim(halves, core[0], 2, keepdims=False)
        sent = lax.dynamic_index_in_dim(halves, 1 - core[0], 2, keepdims=False)
    partner = by_fsdp(sent, 1)
    total = (kept.astype(f32) + partner.astype(f32)).astype(bf16)
    total, grad_heads = lax.optimization_barrier((total, grad_heads))
    total = lax.psum_scatter(total.reshape(-1, model), "sp", scatter_dimension=0, tiled=True)
    *parts, turned = attend_backward(
        queries,
        keys,
        values,
        grad_heads,
        attended,
        logsum,
        backward_start,
        backward_number,
        me,
        weights,
        grad_h1,
        heads_local,
    )
    kept, sent = weight_gradient(order, turned, blocks, pieces)
    cores = [[2 * i + c for i in range(shards // 2)] for c in range(2)]
    reduced = lax.psum_scatter(
        total, "fsdp", scatter_dimension=0, tiled=True, axis_index_groups=cores
    )
    grad_input = scatter_rows(*parts)
    if direct:
        total = (kept.astype(f32) + by_fsdp(sent, 1).astype(f32)).astype(bf16)
        moved = [by_fsdp(total[z], 2 * z).astype(f32) for z in range(1, shards // 2)]
        total = sum(moved, total[0].astype(f32))
        by_head = [total[0]] + [by_sp(total[r], r) for r in range(1, groups)]
        weights = finish(order, by_head, reduced, ratio)
        vectors = [item.reshape(-1) for item in weights[4:]]
        owned_qkv, owned_down, owned_up, owned_out = weights[:4]
    else:
        cut = model // pieces
        halves = jnp.stack([kept, sent], 2).transpose(1, 0, 2, 3, 4).reshape(pieces, cut, model)
        biases = halves[:8, :2, model - 128 : model - 128 + cut]
        biases = biases.transpose(1, 0, 2).reshape(2, shards, own).transpose(1, 0, 2)
        biases = jnp.pad(biases, ((0, 0), (0, 6), (0, 3 * width - own)))
        halves = halves[:, :, : 3 * width].reshape(devices, own, 3 * width)
        halves = jnp.concatenate([halves, jnp.tile(biases, (groups, 1, 1))], 1)
        halves = lax.all_to_all(halves, both, split_axis=0, concat_axis=0, tiled=True)
        halves = jnp.sum(halves.reshape(groups, shards, own + 8, 3 * width).astype(f32), 1)
        bias_sums = lax.dynamic_slice(halves, (me[0], own, 0), (1, 2, own))[0]
        by_head = halves[:, :own].reshape(groups, own, 3, width).transpose(1, 2, 0, 3)
        owned_qkv = by_head.reshape(own, 3 * model)
        at = ratio * own
        reduced = reduced.astype(f32)
        owned_up = reduced[at : 2 * at].reshape(ratio, own, model).transpose(1, 0, 2)
        owned_up = owned_up.reshape(own, hidden)
        owned_down, owned_out = reduced[:at], reduced[2 * at : 2 * at + own]
        tail = reduced[2 * at + own :]
        vectors = [tail[i, :own] for i in range(6)] + [tail[6, :at], bias_sums[0], bias_sums[1]]
    return (
        output,
        grad_input,
        owned_qkv,
        vectors[7],
        vectors[8],
        owned_out,
        *vectors[:3],
        owned_up,
        vectors[6],
        owned_down,
        *vectors[3:6],
    )


def solution(mesh):
    in_specs = (
        P(("fsdp", "sp"), None),
        P("fsdp", None),
        P(("fsdp", "sp"), None),
        P(("sp", "fsdp"), None),
        P(("sp", "fsdp")),
        P(("sp", "fsdp")),
        P(("sp", "fsdp"), None),
        P(("sp", "fsdp")),
        P(("sp", "fsdp")),
        P(("sp", "fsdp")),
        P(("sp", "fsdp"), None),
        P(("sp", "fsdp")),
        P(("sp", "fsdp"), None),
        P(("sp", "fsdp")),
        P(("sp", "fsdp")),
        P(("sp", "fsdp")),
    )
    out_specs = (
        P(("fsdp", "sp"), None),
        P(("fsdp", "sp"), None),
        P(("sp", "fsdp"), None),
        P(("sp", "fsdp")),
        P(("sp", "fsdp")),
        P(("sp", "fsdp"), None),
        P(("sp", "fsdp")),
        P(("sp", "fsdp")),
        P(("sp", "fsdp")),
        P(("sp", "fsdp"), None),
        P(("sp", "fsdp")),
        P(("sp", "fsdp"), None),
        P(("sp", "fsdp")),
        P(("sp", "fsdp")),
        P(("sp", "fsdp")),
    )
    return jax.shard_map(body, mesh=mesh, in_specs=in_specs, out_specs=out_specs, check_vma=False)
```

```python
import jax
import jax.numpy as jnp
from jax import lax
from jax.experimental import pallas as pl
from jax.experimental.pallas import tpu as pltpu
from jax.sharding import PartitionSpec as P

HEADS = 12
HEAD = 64
IDS = 32
far = 1e30
FQ, FK = 512, 512
BQ, BK = 512, 256
ROWS = 768
f32 = jnp.float32
bf16 = jnp.bfloat16
norm_eps = 1e-06


def padded_width(width):
    return -(-(width + IDS) // 128) * 128


def spans(seg_row, block):
    seq = seg_row.shape[0]
    count = seq // block
    first = seg_row[::block]
    last = seg_row[block - 1 :: block]
    lo = jnp.sum((seg_row[None, :] < first[:, None]).astype(jnp.int32), 1)
    hi = jnp.sum((seg_row[None, :] <= last[:, None]).astype(jnp.int32), 1)
    return lo, hi


def windows(seg_row, block, step, grain):
    lo, hi = spans(seg_row, block)
    seq = seg_row.shape[0]
    start = lo // grain * grain
    number = -(-(hi - start) // step)
    start = jnp.minimum(start, seq - number * step)
    return start.astype(jnp.int32), number.astype(jnp.int32)


def lanes_of(head, shape):
    lane = lax.broadcasted_iota(jnp.int32, shape, len(shape) - 1)
    return (lane >= head * HEAD) & (lane < (head + 1) * HEAD)


def mm(a, b):
    return jnp.dot(a, b, preferred_element_type=f32)


def mm_nt(a, b):
    return lax.dot_general(a, b, (((1,), (1,)), ((), ())), preferred_element_type=f32)


def mm_tn(a, b):
    return lax.dot_general(a, b, (((0,), (0,)), ((), ())), preferred_element_type=f32)


def forward_kernel(
    heads, start_ref, number_ref, me_ref, q_ref, k_ref, v_ref,
    o0_ref, o1_ref, o2_ref, o3_ref, lse_ref, kh, vt, scores, acc,
):
    step = pl.program_id(0)
    seq, wide = k_ref.shape
    width = heads * HEAD
    tall = HEAD + 16

    @pl.when(step == 0)
    def _():
        row = lax.broadcasted_iota(jnp.int32, (16, FK), 0)
        ones = jnp.where(row == 0, 1.0, 0.0).astype(bf16)

        def part(i, carry):
            rows = pl.ds(pl.multiple_of(i * FK, FK), FK)
            k = k_ref[rows, :]
            lane = lax.broadcasted_iota(jnp.int32, k.shape, 1)
            turned = v_ref[rows, :].T
            for h in range(heads):
                keep = lanes_of(h, k.shape) | (lane >= width)
                kept = jnp.where(keep, k, jnp.zeros_like(k))
                for c in range(FK // 128):
                    at = pl.multiple_of(i * (FK * heads) + (c * heads + h) * 128, 128)
                    kh[pl.ds(at, 128), :] = kept[c * 128 : (c + 1) * 128]
                vt[h * tall : h * tall + HEAD, rows] = turned[h * HEAD : (h + 1) * HEAD]
                vt[h * tall + HEAD : (h + 1) * tall, rows] = ones
            return carry

        lax.fori_loop(0, seq // FK, part, 0)

    q = q_ref[...]
    start = start_ref[step]
    number = number_ref[step]

    def score(j, tops):
        at = pl.multiple_of((start + j * FK) * heads, 128)
        every = mm_nt(kh[pl.ds(at, FK * heads), :], q)
        news = list(tops)
        for c in range(FK // 128):
            for h in range(heads):
                s = every[(c * heads + h) * 128 : (c * heads + h + 1) * 128]
                scores[h, pl.ds(pl.multiple_of(j * FK + c * 128, 128), 128), :] = s
                news[h] = jnp.maximum(news[h], jnp.max(s.reshape(16, 8, FQ), 0))
        return tuple(news)

    tops = lax.fori_loop(0, number, score, (jnp.full((8, FQ), -jnp.inf, f32),) * heads)
    tops = [jnp.max(top, 0, keepdims=True) for top in tops]
    acc[...] = jnp.zeros_like(acc)

    def mix(j, carry):
        rows = pl.ds(pl.multiple_of(start + j * FK, 128), FK)
        out = pl.ds(pl.multiple_of(j * FK, FK), FK)
        for h in range(heads):
            p = jnp.exp(scores[h, out, :] - tops[h]).astype(bf16)
            acc[h] += mm(vt[h * tall : (h + 1) * tall, rows], p)
        return carry

    lax.fori_loop(0, number, mix, 0)
    outs = []
    for h in range(heads):
        total = acc[h, HEAD : HEAD + 1, :]
        outs.append(acc[h, :HEAD, :] / total)
        lse_ref[h : h + 1, :] = tops[h] + jnp.log(total)
    mixed = jnp.concatenate(outs, 0).astype(bf16)
    per = o0_ref.shape[1] // 256
    for u in range(FQ // 256):
        block = step * (FQ // 256) + u
        at = pl.ds(pl.multiple_of(lax.rem(block, per) * 256, 256), 256)
        slot = lax.bitwise_xor(block // per, me_ref[0])
        for r, out_ref in enumerate((o0_ref, o1_ref, o2_ref, o3_ref)):

            @pl.when(slot == r)
            def _():
                out_ref[:, at] = mixed[:, u * 256 : (u + 1) * 256]


def attend_forward(q, k, v, starts, numbers, me, heads):
    seq, wide = q.shape
    width = heads * HEAD
    steps = seq // FQ
    cost = pl.CostEstimate(
        flops=2 * heads * seq * seq * HEAD, bytes_accessed=8 * seq * wide, transcendentals=heads * seq * seq // 3
    )
    return pl.pallas_call(
        lambda *refs: forward_kernel(heads, *refs),
        grid_spec=pltpu.PrefetchScalarGridSpec(
            num_scalar_prefetch=3,
            grid=(steps,),
            in_specs=[
                pl.BlockSpec((FQ, wide), lambda i, a, b, m: (i, 0)),
                pl.BlockSpec((seq, wide), lambda i, a, b, m: (0, 0)),
                pl.BlockSpec((seq, width), lambda i, a, b, m: (0, 0)),
            ],
            out_specs=[
                pl.BlockSpec((width, seq // 4), lambda i, a, b, m: (0, 0)),
                pl.BlockSpec((width, seq // 4), lambda i, a, b, m: (0, 0)),
                pl.BlockSpec((width, seq // 4), lambda i, a, b, m: (0, 0)),
                pl.BlockSpec((width, seq // 4), lambda i, a, b, m: (0, 0)),
                pl.BlockSpec((8, FQ), lambda i, a, b, m: (0, i)),
            ],
            scratch_shapes=[
                pltpu.VMEM((heads * seq, wide), bf16),
                pltpu.VMEM((heads * (HEAD + 16), seq), bf16),
                pltpu.VMEM((heads, seq, FQ), f32),
                pltpu.VMEM((heads, HEAD + 16, FQ), f32),
            ],
        ),
        out_shape=[
            jax.ShapeDtypeStruct((width, seq // 4), bf16),
            jax.ShapeDtypeStruct((width, seq // 4), bf16),
            jax.ShapeDtypeStruct((width, seq // 4), bf16),
            jax.ShapeDtypeStruct((width, seq // 4), bf16),
            jax.ShapeDtypeStruct((8, seq), f32),
        ],
        cost_estimate=cost,
        compiler_params=pltpu.CompilerParams(vmem_limit_bytes=48 << 20),
        name="attend_forward",
    )(starts, numbers, me, q, k, v)


def backward_kernel(
    heads, start_ref, number_ref, me_ref, q_ref, k_ref, v_ref,
    g0_ref, g1_ref, g2_ref, g3_ref, o0_ref, o1_ref, o2_ref, o3_ref, lse_ref, w_ref, gh1_ref,
    sx_ref, sy_ref, mine_ref, low_ref, up_ref, turned,
    qt, gt, dqt, delta, dkt, dvt, kh, vh, grads,
):
    step = pl.program_id(0)
    seq, wide = q_ref.shape
    width = heads * HEAD
    own_rows = seq // 4
    per = own_rows // 256
    me = me_ref[0]

    @pl.when(step == 0)
    def _():
        def part(i, carry):
            rows = pl.ds(pl.multiple_of(i * 256, 256), 256)
            at = pl.ds(pl.multiple_of(lax.rem(i, per) * 256, 256), 256)
            slot = lax.bitwise_xor(i // per, me)
            qt[:, rows] = q_ref[rows, :].T[:width]
            dqt[:, rows] = jnp.zeros((width, 256), f32)
            pairs = ((g0_ref, o0_ref), (g1_ref, o1_ref), (g2_ref, o2_ref), (g3_ref, o3_ref))
            for r, (g_ref, o_ref) in enumerate(pairs):

                @pl.when(slot == r)
                def _():
                    g = g_ref[:, at]
                    gt[:, rows] = g
                    product = g.astype(f32) * o_ref[:, at].astype(f32)
                    for h in range(heads):
                        mine = slice(h * HEAD, (h + 1) * HEAD)
                        delta[h : h + 1, rows] = jnp.sum(product[mine], 0, keepdims=True)

            return carry

        lax.fori_loop(0, seq // 256, part, 0)

    start = start_ref[step]
    k = k_ref[...]
    v = v_ref[...]
    lane = lax.broadcasted_iota(jnp.int32, k.shape, 1)
    for h in range(heads):
        part = slice(h * BK, (h + 1) * BK)
        kh[part, :] = jnp.where(lanes_of(h, k.shape) | (lane >= width), k, jnp.zeros_like(k))
        vh[part, :] = jnp.where(lanes_of(h, v.shape), v, jnp.zeros_like(v))
    kt = k.T
    dkt[...] = jnp.zeros_like(dkt)
    dvt[...] = jnp.zeros_like(dvt)

    def one(i, carry):
        rows = pl.ds(pl.multiple_of(start + i * BQ, 128), BQ)
        q = q_ref[rows, :]
        ss = mm_nt(kh[...], q)
        dps = mm(vh[...], gt[:, rows])
        for h in range(heads):
            mine = slice(h * HEAD, (h + 1) * HEAD)
            part = slice(h * BK, (h + 1) * BK)
            p = jnp.exp(ss[part] - lse_ref[h : h + 1, rows])
            dp = dps[part]
            ds = (p * (dp - delta[h : h + 1, rows])).astype(bf16)
            dvt[mine, :] += mm_nt(gt[mine, rows], p.astype(bf16))
            dkt[mine, :] += mm_nt(qt[mine, rows], ds)
            dqt[mine, rows] += mm(kt[mine, :], ds)
        return carry

    lax.fori_loop(0, number_ref[step], one, 0)
    here = pl.ds(pl.multiple_of(step * BK, BK), BK)
    for c, total in ((1, dkt), (2, dvt)):
        low = total[...].astype(bf16)
        turned[c * width : (c + 1) * width, here] = low
        grads[c, here, :] = low.T

    @pl.when(step == pl.num_programs(0) - 1)
    def _():
        def part(i, carry):
            rows = pl.ds(pl.multiple_of(i * 256, 256), 256)
            low = (dqt[:, rows] * 0.125).astype(bf16)
            turned[:width, rows] = low
            grads[0, rows, :] = low.T
            return carry

        lax.fori_loop(0, seq // 256, part, 0)
        half = own_rows // 2

        def back(i, carry):
            def rows_of(lower):
                at = pl.ds(pl.multiple_of(i * own_rows + lower * half, 128), half)
                value = mm_nt(grads[0, at, :], w_ref[0])
                value = value + mm_nt(grads[1, at, :], w_ref[1])
                return value + mm_nt(grads[2, at, :], w_ref[2])

            slot = lax.bitwise_xor(i, me)
            for lower in range(2):
                value = rows_of(lower)
                here = slice(lower * half, (lower + 1) * half)

                @pl.when(slot == 0)
                def _():
                    mine_ref[here, :] = value + gh1_ref[here, :]

                @pl.when(slot == 1)
                def _():
                    if lower:
                        low_ref[...] = value
                    else:
                        sx_ref[:half] = value.astype(bf16)

                @pl.when(slot == 2)
                def _():
                    if lower:
                        sy_ref[:half] = value.astype(bf16)
                    else:
                        up_ref[...] = value

                @pl.when(slot == 3)
                def _():
                    if lower:
                        sy_ref[half:] = value.astype(bf16)
                    else:
                        sx_ref[half:] = value.astype(bf16)

            return carry

        lax.fori_loop(0, 4, back, 0)


def attend_backward(q, k, v, g, o, lse, starts, numbers, place, w, gh1, heads):
    seq, wide = q.shape
    width = heads * HEAD
    steps = seq // BK
    own_rows, model = gh1.shape
    half = own_rows // 2
    once = dict(pipeline_mode=pl.Buffered(1))
    whole = lambda a: pl.BlockSpec(a, lambda i, a_, b_, m_: (0,) * len(a), **once)
    cost = pl.CostEstimate(
        flops=5 * heads * seq * seq * HEAD + 6 * seq * model * width,
        bytes_accessed=16 * seq * wide,
        transcendentals=heads * seq * seq // 3,
    )
    return pl.pallas_call(
        lambda *refs: backward_kernel(heads, *refs),
        grid_spec=pltpu.PrefetchScalarGridSpec(
            num_scalar_prefetch=3,
            grid=(steps,),
            in_specs=[
                whole((seq, wide)),
                pl.BlockSpec((BK, wide), lambda i, a, b, m: (i, 0)),
                pl.BlockSpec((BK, width), lambda i, a, b, m: (i, 0)),
            ]
            + [whole((width, own_rows))] * 8
            + [whole((8, seq))]
            + [whole((3, model, width)), whole((own_rows, model))],
            out_specs=[
                whole((own_rows, model)),
                whole((own_rows, model)),
                whole((own_rows, model)),
                whole((own_rows // 2, model)),
                whole((own_rows // 2, model)),
                whole((3 * width, seq)),
            ],
            scratch_shapes=[
                pltpu.VMEM((width, seq), bf16),
                pltpu.VMEM((width, seq), bf16),
                pltpu.VMEM((width, seq), f32),
                pltpu.VMEM((8, seq), f32),
                pltpu.VMEM((width, BK), f32),
                pltpu.VMEM((width, BK), f32),
                pltpu.VMEM((heads * BK, wide), bf16),
                pltpu.VMEM((heads * BK, width), bf16),
                pltpu.VMEM((3, seq, width), bf16),
            ],
        ),
        out_shape=[
            jax.ShapeDtypeStruct((own_rows, model), bf16),
            jax.ShapeDtypeStruct((own_rows, model), bf16),
            jax.ShapeDtypeStruct((own_rows, model), f32),
            jax.ShapeDtypeStruct((own_rows // 2, model), f32),
            jax.ShapeDtypeStruct((own_rows // 2, model), f32),
            jax.ShapeDtypeStruct((3 * width, seq), bf16),
        ],
        cost_estimate=cost,
        compiler_params=pltpu.CompilerParams(vmem_limit_bytes=60 << 20),
        name="attend_backward",
    )(starts, numbers, place, q, k, v, *g, *o, lse, w, gh1)


def weight_kernel(me_ref, turned, x0_ref, x1_ref, x2_ref, x3u_ref, x3l_ref, kept_ref, sent_ref, rows_ref):
    seq = turned.shape[1]
    width = turned.shape[0] // 3
    model = x0_ref.shape[1]
    columns, _, own = kept_ref.shape[:3]
    shards = 2 * columns
    lane = lax.broadcasted_iota(jnp.int32, (128, width), 1)
    row = lax.broadcasted_iota(jnp.int32, (128, width), 0)
    tile = jnp.where(lax.rem(lane, own) == row, 1.0, 0.0).astype(bf16)
    lane = lax.broadcasted_iota(jnp.int32, (shards, width), 1)
    row = lax.broadcasted_iota(jnp.int32, (shards, width), 0)
    ones = jnp.ones((8, seq), bf16)
    rows_ref[...] = jnp.zeros_like(rows_ref)
    for j, c in enumerate((0, 2)):
        sums = mm_nt(ones, turned[c * width : (c + 1) * width, :])[:1]
        rows_ref[:, j, :] = mm_nt(jnp.where(lane // own == row, sums, 0.0).astype(bf16), tile)
    me = me_ref[0]
    own_rows = x0_ref.shape[0]
    total = jnp.zeros((3 * width, model), f32)
    for r, parts in enumerate(((x0_ref,), (x1_ref,), (x2_ref,), (x3u_ref, x3l_ref))):
        first = lax.bitwise_xor(me, r) * own_rows
        for part_ref in parts:
            count = part_ref.shape[0]
            total = total + mm(turned[:, pl.ds(pl.multiple_of(first, 128), count)], part_ref[...])
            first = first + count
    value = total.T.astype(bf16).reshape(4 * shards, own, 3 * width)
    for core in range(2):

        @pl.when(me_ref[3] == core)
        def _():
            for piece in range(4 * shards):
                group, shard = piece // shards, piece % shards
                target = kept_ref if shard % 2 == core else sent_ref
                z = lax.bitwise_xor(me_ref[2], shard // 2)
                r = lax.bitwise_xor(me_ref[1], group)
                target[z, r, :, : 3 * width] = value[piece]
                target[z, r, :, 3 * width :] = jnp.zeros((own, model - 3 * width), bf16)
                target[z, r, :8, model - 128 :] = rows_ref[shard].astype(bf16)


def weight_gradient(place, turned, x, pieces):
    model = x[0].shape[1]
    own = model // pieces
    vmem = pl.BlockSpec(memory_space=pltpu.VMEM)
    return pl.pallas_call(
        weight_kernel,
        in_specs=[pl.BlockSpec(memory_space=pltpu.SMEM)] + [vmem] * 6,
        out_shape=[jax.ShapeDtypeStruct((pieces // 8, 4, own, model), bf16)] * 2,
        scratch_shapes=[pltpu.VMEM((pieces // 4, 8, 128), f32)],
        cost_estimate=pl.CostEstimate(
            flops=16 * turned.size * model, bytes_accessed=2 * turned.size * 3, transcendentals=0
        ),
        compiler_params=pltpu.CompilerParams(vmem_limit_bytes=40 << 20),
        name="weight_gradient",
    )(place, turned, *x)


def pack_kernel(ratio, groups, me_ref, down_ref, up_ref, out_ref, qkv_ref, *refs):
    vectors, (query_ref, value_ref, packed_ref, spread_ref, rows_ref) = refs[:-5], refs[-5:]
    own, model = out_ref.shape
    width = model // groups
    rows_ref[...] = jnp.zeros_like(rows_ref)
    rows_ref[0:1, :own] = query_ref[...].astype(f32)
    rows_ref[1:2, :own] = value_ref[...].astype(f32)
    biases = rows_ref[:, : 3 * width].astype(bf16)
    for g in range(groups):
        parts = [qkv_ref[:, c * model + g * width : c * model + (g + 1) * width] for c in range(3)]
        slot = lax.bitwise_xor(me_ref[0], g)
        spread_ref[slot, :own, :] = jnp.concatenate(parts, 1)
        spread_ref[slot, own:, :] = biases
    at = ratio * own
    packed_ref[:at] = down_ref[...]
    for c in range(ratio):
        packed_ref[at + c * own : at + (c + 1) * own] = up_ref[:, c * model : (c + 1) * model]
    packed_ref[2 * at : 2 * at + own] = out_ref[...]
    rows_ref[...] = jnp.zeros_like(rows_ref)
    for j, vector in enumerate(vectors):
        rows_ref[j : j + 1, : vector.shape[1]] = vector[...].astype(f32)
    packed_ref[2 * at + own :] = rows_ref[...].astype(bf16)


def pack(me, w_down, w_up, w_out, w_qkv, vectors, b_query, b_value, groups):
    own, model = w_out.shape
    ratio = w_down.shape[0] // own
    width = model // groups
    vmem = pl.BlockSpec(memory_space=pltpu.VMEM)
    return pl.pallas_call(
        lambda *refs: pack_kernel(ratio, groups, *refs),
        in_specs=[pl.BlockSpec(memory_space=pltpu.SMEM)] + [vmem] * (6 + len(vectors)),
        out_shape=[
            jax.ShapeDtypeStruct((own * (2 * ratio + 1) + 8, model), bf16),
            jax.ShapeDtypeStruct((groups, own + 8, 3 * width), bf16),
        ],
        scratch_shapes=[pltpu.VMEM((8, model), f32)],
        name="pack",
    )(me, w_down, w_up, w_out, w_qkv, *[item[None] for item in vectors], b_query[None], b_value[None])


def pack_plain(w_down, w_up, w_out, w_qkv, vectors, b_query, b_value, groups):
    own, model = w_out.shape
    ratio = w_down.shape[0] // own
    width = model // groups
    up_blocks = [w_up[:, c * model : (c + 1) * model] for c in range(ratio)]
    rows = [jnp.pad(item, (0, model - item.shape[0]))[None] for item in vectors]
    rows.append(jnp.zeros((8 - len(rows), model), bf16))
    packed = jnp.concatenate([w_down] + up_blocks + [w_out] + rows, 0)
    block = w_qkv.reshape(own, 3, groups, width).transpose(2, 0, 1, 3).reshape(groups, own, 3 * width)
    rows = jnp.pad(jnp.stack([b_query, b_value]), ((0, 6), (0, 3 * width - own)))
    return packed, jnp.concatenate([block, jnp.broadcast_to(rows, (groups, 8, 3 * width))], 1)


def project_block(heads, x_ref, first, seg_ref, bias_ref, w_ref, q_ref, k_ref, v_ref):
    size = 384
    width = heads * HEAD
    wide = q_ref.shape[1]

    def part(i, carry):
        x = x_ref[pl.ds(pl.multiple_of(i * size, size), size), :]
        at = pl.ds(pl.multiple_of(first + i * size, size), size)
        lane = lax.broadcasted_iota(jnp.int32, (size, wide - width), 1)
        same = lane == seg_ref[at, :]
        q = (mm(x, w_ref[0]) + bias_ref[0:1, :]).astype(bf16)
        q_ref[at, :width] = q * jnp.asarray(0.125, bf16)
        q_ref[at, width:] = jnp.where(same, 1.0, 0.0).astype(bf16)
        k_ref[at, :width] = mm(x, w_ref[1]).astype(bf16)
        k_ref[at, width:] = jnp.where(same, 0.0, -far).astype(bf16)
        v_ref[at, :] = (mm(x, w_ref[2]) + bias_ref[1:2, :]).astype(bf16)
        return carry

    lax.fori_loop(0, x_ref.shape[0] // size, part, 0)


def project_kernel(
    heads, me_ref, x0_ref, x1_ref, x2_ref, seg_ref, near_ref, far_ref,
    q_ref, k_ref, v_ref, wide_w, bias_ref, rows_ref,
):
    step = pl.program_id(0)
    width = heads * HEAD
    own = near_ref.shape[2] - 8
    columns, groups = near_ref.shape[:2]

    @pl.when(step == 0)
    def _():
        for c, part_ref in ((0, near_ref), (1, far_ref)):
            for z in range(columns):
                shard = lax.bitwise_xor(me_ref[2], z) * 2 + lax.bitwise_xor(me_ref[3], c)
                for g in range(groups):
                    piece = lax.bitwise_xor(me_ref[1], g) * (2 * columns) + shard
                    at = pl.ds(pl.multiple_of(piece * own, 8), own)
                    for k in range(3):
                        wide_w[k, at, :] = part_ref[z, g, :own, k * width : (k + 1) * width]
                lines = part_ref[z, 0, own:, :128].astype(f32)
                for k in range(2):
                    rows_ref[k, pl.ds(shard, 1), :] = lines[k : k + 1]
        lane = lax.broadcasted_iota(jnp.int32, (128, width), 1)
        row = lax.broadcasted_iota(jnp.int32, (128, width), 0)
        tile = jnp.where(lax.rem(lane, own) == row, 1.0, 0.0).astype(bf16)
        lane = lax.broadcasted_iota(jnp.int32, (2 * columns, width), 1)
        row = lax.broadcasted_iota(jnp.int32, (2 * columns, width), 0)
        bias_ref[...] = jnp.zeros_like(bias_ref)
        for k in range(2):
            value = jnp.where(lane // own == row, mm(rows_ref[k].astype(bf16), tile), 0.0)
            bias_ref[k : k + 1, :] = jnp.sum(value, 0, keepdims=True)

    for k, part_ref in ((0, x0_ref), (1, x1_ref), (2, x2_ref)):

        @pl.when(step == k)
        def _():
            project_block(heads, part_ref, 0, seg_ref, bias_ref, wide_w, q_ref, k_ref, v_ref)


def project_last_kernel(heads, me_ref, upper_ref, lower_ref, seg_ref, w_ref, bias_ref, *refs):
    project_block(heads, upper_ref, 0, seg_ref, bias_ref, w_ref, *refs[-3:])
    project_block(heads, lower_ref, upper_ref.shape[0], seg_ref, bias_ref, w_ref, *refs[-3:])


def project(place, blocks, seg_row, near, away, heads):
    own_rows, model = blocks[0].shape
    width = heads * HEAD
    wide = padded_width(width)
    seq = 4 * own_rows
    once = dict(pipeline_mode=pl.Buffered(1))
    fixed = lambda a: pl.BlockSpec(a, lambda s, m: (0,) * len(a), **once)

    def rows_of(slot):
        at = lambda s, m: (lax.bitwise_xor(s + slot, m[0]), 0)
        return [pl.BlockSpec((own_rows, n), at) for n in (1, wide, wide, width)]

    def cost(part):
        return pl.CostEstimate(
            flops=6 * part * own_rows * model * width,
            bytes_accessed=4 * part * own_rows * (model + wide),
            transcendentals=0,
        )

    params = pltpu.CompilerParams(vmem_limit_bytes=40 << 20)
    arrays = [
        jax.ShapeDtypeStruct((seq, wide), bf16),
        jax.ShapeDtypeStruct((seq, wide), bf16),
        jax.ShapeDtypeStruct((seq, width), bf16),
    ]
    segments = seg_row[:, None]
    *made, weights, biases = pl.pallas_call(
        lambda *refs: project_kernel(heads, *refs),
        grid_spec=pltpu.PrefetchScalarGridSpec(
            num_scalar_prefetch=1,
            grid=(3,),
            in_specs=[fixed((own_rows, model))] * 3 + rows_of(0)[:1] + [fixed(near.shape)] * 2,
            out_specs=rows_of(0)[1:] + [fixed((3, model, width)), fixed((8, width))],
            scratch_shapes=[pltpu.VMEM((2, 2 * near.shape[0], 128), f32)],
        ),
        out_shape=arrays
        + [jax.ShapeDtypeStruct((3, model, width), bf16), jax.ShapeDtypeStruct((8, width), f32)],
        cost_estimate=cost(3),
        compiler_params=params,
        name="project",
    )(place, *blocks[:3], segments, near, away)
    made = pl.pallas_call(
        lambda *refs: project_last_kernel(heads, *refs),
        grid_spec=pltpu.PrefetchScalarGridSpec(
            num_scalar_prefetch=1,
            grid=(1,),
            in_specs=[fixed((own_rows // 2, model))] * 2
            + rows_of(3)[:1]
            + [fixed((3, model, width)), fixed((8, width))]
            + [pl.BlockSpec(memory_space=pl.ANY)] * 3,
            out_specs=rows_of(3)[1:],
        ),
        out_shape=arrays,
        input_output_aliases={6: 0, 7: 1, 8: 2},
        cost_estimate=cost(1),
        compiler_params=params,
        name="project_last",
    )(place, *blocks[3:], segments, weights, biases, *made)
    return *made, weights


def finish_kernel(ratio, place_ref, *refs):
    head_refs, reduced_ref = refs[:4], refs[4]
    qkv_ref, down_ref, up_ref, out_ref = refs[5:9]
    vector_refs, query_ref, value_ref = refs[9:16], refs[16], refs[17]
    own, model = out_ref.shape
    width = model // 4
    at = ratio * own
    for m in range(4):

        @pl.when(place_ref[1] == m)
        def _():
            for r in range(4):
                for c in range(3):
                    spot = c * model + (m ^ r) * width
                    qkv_ref[:, spot : spot + width] = head_refs[r][:, c * width : (c + 1) * width]

    down_ref[...] = reduced_ref[:at].astype(f32)
    for c in range(ratio):
        up_ref[:, c * model : (c + 1) * model] = reduced_ref[at + c * own : at + (c + 1) * own].astype(f32)
    out_ref[...] = reduced_ref[2 * at : 2 * at + own].astype(f32)
    lines = reduced_ref[2 * at + own :].astype(f32)
    for j, ref in enumerate(vector_refs):
        ref[...] = lines[j : j + 1, : ref.shape[1]]
    for j, ref in enumerate((query_ref, value_ref)):
        ref[...] = head_refs[0][j : j + 1, model - 128 : model - 128 + own]


def finish(place, by_head, reduced, ratio):
    own, model = by_head[0].shape
    vmem = pl.BlockSpec(memory_space=pltpu.VMEM)
    shapes = [(own, 3 * model), (ratio * own, model), (own, ratio * model), (own, model)]
    shapes += [(1, own)] * 6 + [(1, ratio * own)] + [(1, own)] * 2
    return pl.pallas_call(
        lambda *refs: finish_kernel(ratio, *refs),
        in_specs=[pl.BlockSpec(memory_space=pltpu.SMEM)] + [vmem] * 5,
        out_shape=[jax.ShapeDtypeStruct(shape, f32) for shape in shapes],
        name="finish",
    )(place, *by_head, reduced)


def normal_rows(z):
    center = jnp.mean(z, -1, keepdims=True)
    moved = z - center
    rstd = lax.rsqrt(jnp.mean(moved * moved, -1, keepdims=True) + norm_eps)
    return moved * rstd, rstd


def norm_pull(s, hat, rstd):
    inner = jnp.mean(s * hat, -1, keepdims=True)
    return rstd * (s - jnp.mean(s, -1, keepdims=True) - hat * inner)


def gelu_both(x):
    z = jnp.abs(x) * 0.7071067811865476
    t = 1.0 / (1.0 + 0.3275911 * z)
    e = jnp.exp(-(z * z))
    poly = t * (
        0.127414796 + t * (-0.142248368 + t * (0.7107068705 + t * (-0.7265760135 + t * 0.5307027145)))
    )
    tail = poly * e
    cdf = jnp.where(x >= 0.0, 1.0 - tail, tail)
    return x * cdf, cdf + x * (e * 0.3989422804014327)


def spread_vectors(chunks, small_ref, vec_ref):
    pieces, _, model = small_ref.shape

    def spread(block, size):
        count = block.shape[0]
        lane = lax.broadcasted_iota(jnp.int32, (128, model), 1)
        row = lax.broadcasted_iota(jnp.int32, (128, model), 0)
        tile = jnp.where(lax.rem(lane, size) == row, 1.0, 0.0).astype(bf16)
        wide = mm(block, tile)
        lane = lax.broadcasted_iota(jnp.int32, (count, model), 1)
        row = lax.broadcasted_iota(jnp.int32, (count, model), 0)
        keep = lane // size == row
        return jnp.sum(jnp.where(keep, wide, 0.0), 0, keepdims=True)

    vec_ref[...] = jnp.zeros_like(vec_ref)
    for j in range(6):
        vec_ref[j : j + 1, :] = spread(small_ref[:, j, :128], model // pieces)
    share = pieces // chunks
    for c in range(chunks):
        block = small_ref[c * share : (c + 1) * share, 6, :128]
        vec_ref[8 + c : 9 + c, :] = spread(block, model // share)


def gather_vectors(chunks, vec_ref, wide_ref):
    pieces, _, model = wide_ref.shape
    wide_ref[...] = jnp.zeros_like(wide_ref)

    def gather(vector, size, count):
        lane = lax.broadcasted_iota(jnp.int32, (128, model), 1)
        row = lax.broadcasted_iota(jnp.int32, (128, model), 0)
        tile = jnp.where(lax.rem(lane, size) == row, 1.0, 0.0).astype(bf16)
        lane = lax.broadcasted_iota(jnp.int32, (count, model), 1)
        row = lax.broadcasted_iota(jnp.int32, (count, model), 0)
        kept = jnp.where(lane // size == row, vector, 0.0).astype(bf16)
        return mm_nt(kept, tile)

    for j in range(6):
        wide_ref[:, j, :128] = gather(vec_ref[j : j + 1, :], model // pieces, pieces)
    share = pieces // chunks
    for c in range(chunks):
        block = gather(vec_ref[8 + c : 9 + c, :], model // share, share)
        wide_ref[c * share : (c + 1) * share, 6, :128] = block


def middle_kernel(
    groups, chunks, place_ref, x_ref, cot_ref, m0_ref, m1_ref, m2_ref, m3_ref, out_w_ref, up_ref, down_ref, small_ref,
    y_ref, gh1_ref, gm0_ref, gm1_ref, gm2_ref, gm3_ref, kept_ref, sent_ref,
    first_low, first_t, hat1, rstd1, activ_t, slope, total, gffn, gpre, vec_ref,
    gvec_ref, gdown, gup, gout, gwide, gsmall, down_sem, up_sem, out_sem, small_sem,
):
    step = pl.program_id(0)
    rows, model = x_ref.shape
    parts = rows // ROWS
    width = m0_ref.shape[0]
    mixed_refs = (m0_ref, m1_ref, m2_ref, m3_ref)
    gmix_refs = (gm0_ref, gm1_ref, gm2_ref, gm3_ref)

    def group(r):
        return lax.bitwise_xor(place_ref[1], r)

    def out_w(r):
        share = out_w_ref.shape[0] // groups
        return out_w_ref[pl.ds(group(r) * share, share)].reshape(width, model)

    def up_w():
        return up_ref[...].reshape(model, model)

    def down_w():
        return down_ref[...].reshape(model, model)

    pieces, own = out_w_ref.shape[:2]
    share = pieces // groups

    def pair(source, sem, *place):
        return [
            [
                pltpu.make_async_copy(source.at[p], target.at[place], sem.at[p])
                for target in (kept_ref, sent_ref)
            ]
            for p in range(2)
        ]

    def begin(copies):
        for p in range(2):

            @pl.when(place_ref[0] == p)
            def _():
                copies[p][0].start()
                copies[1 - p][1].start()

    def finish(copies):
        for p in range(2):
            copies[p][0].wait()

    def down_copies(slot, chunk):
        return pair(
            gdown.at[slot], down_sem.at[slot], chunk, slice(None), slice(0, chunks * own), slice(None)
        )

    def up_copies(slot, chunk):
        at = pl.ds(pl.multiple_of((chunks + chunk) * own, 8), own)
        return pair(gup.at[slot], up_sem.at[slot], slice(None), slice(None), at, slice(None))

    def out_copies():
        at = slice(2 * chunks * own, 2 * chunks * own + own)
        return pair(gout, out_sem, slice(None), slice(None), at, slice(None))

    def small_copies():
        at = slice(2 * chunks * own + own, 2 * chunks * own + own + 8)
        return pair(gsmall, small_sem, slice(None), slice(None), at, slice(None))

    def vec(i):
        return vec_ref[i : i + 1, :]

    def sums(value):
        return jnp.sum(value, 0, keepdims=True)

    @pl.when(step == 0)
    def _():
        gvec_ref[...] = jnp.zeros_like(gvec_ref)
        spread_vectors(chunks, small_ref, vec_ref)

        def part(i, carry):
            at = pl.ds(pl.multiple_of(i * ROWS, ROWS), ROWS)
            branch = vec(0)
            for r in range(groups):
                branch = branch + mm_tn(mixed_refs[r][:, at], out_w(r))
            hat, rstd = normal_rows(x_ref[at, :].astype(f32) + branch)
            value = hat * vec(1) + vec(2)
            hat1[at, :] = hat
            rstd1[at, :] = jnp.broadcast_to(rstd, (ROWS, 128))
            low = value.astype(bf16)
            first_low[at, :] = low
            first_t[:, at] = low.T
            total[at, :] = value + vec(3)
            return carry

        lax.fori_loop(0, parts, part, 0)

    @pl.when(step < chunks)
    def _():
        def part(i, carry):
            at = pl.ds(pl.multiple_of(i * ROWS, ROWS), ROWS)
            pre = mm(first_low[at, :], up_w()) + vec_ref[pl.ds(8 + step, 1), :]
            value, pull = gelu_both(pre)
            low = value.astype(bf16)
            slope[step, at, :] = pull
            activ_t[step, :, at] = low.T
            total[at, :] += mm(low, down_w())
            return carry

        lax.fori_loop(0, parts, part, 0)

    @pl.when(step == chunks - 1)
    def _():
        def part(i, carry):
            at = pl.ds(pl.multiple_of(i * ROWS, ROWS), ROWS)
            hat, rstd = normal_rows(total[at, :])
            y_ref[at, :] = (hat * vec(4) + vec(5)).astype(bf16)
            g = cot_ref[at, :].astype(f32)
            gh2 = norm_pull(g * vec(4), hat, rstd)
            total[at, :] = gh2
            low = gh2.astype(bf16)
            gffn[at, :] = low
            gvec_ref[3:4, :] += sums(low.astype(f32))
            gvec_ref[4:5, :] += sums(g * hat)
            gvec_ref[5:6, :] += sums(g)
            return carry

        lax.fori_loop(0, parts, part, 0)

    @pl.when(step >= chunks)
    def _():
        chunk = 2 * chunks - 1 - step
        slot = lax.rem(step, 2)

        @pl.when(step >= chunks + 2)
        def _():
            finish(down_copies(slot, chunk))
            finish(up_copies(slot, chunk))

        def part(i, carry):
            at = pl.ds(pl.multiple_of(i * ROWS, ROWS), ROWS)
            low = (mm_nt(gffn[at, :], down_w()) * slope[chunk, at, :]).astype(bf16)
            gpre[at, :] = low
            gvec_ref[pl.ds(8 + chunk, 1), :] += sums(low.astype(f32))
            total[at, :] += mm_nt(low, up_w())
            return carry

        lax.fori_loop(0, parts, part, 0)
        tall = 4 * chunks * own

        def weights_down(i, carry):
            at = pl.ds(pl.multiple_of(i * tall, tall), tall)
            value = mm(activ_t[chunk, at, :], gffn[...]).astype(bf16).reshape(4, chunks * own, model)
            for f in range(4):
                gdown[slot, f % 2, 2 * i + f // 2] = value[f]
            return carry

        lax.fori_loop(0, model // tall, weights_down, 0)
        begin(down_copies(slot, chunk))
        high = 16 * own

        def weights_up(i, carry):
            at = pl.ds(pl.multiple_of(i * high, high), high)
            value = mm(first_t[at, :], gpre[...]).astype(bf16).reshape(16, own, model)
            for f in range(16):
                gup[slot, f % 2, 2 * i + f // 8, (f % 8) // 2] = value[f]
            return carry

        lax.fori_loop(0, model // high, weights_up, 0)
        begin(up_copies(slot, chunk))

    @pl.when(step == 2 * chunks - 1)
    def _():
        def part(i, carry):
            at = pl.ds(pl.multiple_of(i * ROWS, ROWS), ROWS)
            g = total[at, :]
            hat = hat1[at, :]
            gh1 = norm_pull(g * vec(1), hat, rstd1[at, :1])
            gh1_ref[at, :] = gh1
            low = gh1.astype(bf16)
            gpre[at, :] = low
            gvec_ref[0:1, :] += sums(low.astype(f32))
            gvec_ref[1:2, :] += sums(g * hat)
            gvec_ref[2:3, :] += sums(g)
            for r in range(groups):
                gmix_refs[r][:, at] = mm_nt(out_w(r), low).astype(bf16)
            return carry

        lax.fori_loop(0, parts, part, 0)
        for r in range(groups):
            value = mm(mixed_refs[r][...], gpre[...]).astype(bf16).reshape(share, own, model)
            for f in range(share):
                gout[f % 2, group(r), f // 2] = value[f]
        begin(out_copies())
        gather_vectors(chunks, gvec_ref, gwide)
        for g in range(groups):
            for f in range(share):
                gsmall[f % 2, g, f // 2] = gwide[g * share + f].astype(bf16)
        begin(small_copies())
        for back in range(2):
            finish(down_copies(back, 0))
            finish(up_copies(back, 0))
        finish(out_copies())
        finish(small_copies())


def middle(place, x, cot, mixed, packed):
    rows, model = x.shape
    groups = len(mixed)
    width = mixed[0].shape[0]
    pieces = packed.shape[0]
    own = model // pieces
    chunks = (packed.shape[1] - 8 - own) // (2 * own)
    last = 2 * chunks - 1
    back = lambda s: jnp.minimum(s, last - s)
    assert chunks == groups and pieces == 8 * groups
    once = dict(pipeline_mode=pl.Buffered(1))
    fixed2 = lambda a: pl.BlockSpec(a, lambda s: (0, 0), **once)
    vectors_at = own * (2 * chunks + 1) // 8
    cost = pl.CostEstimate(
        flops=2 * rows * model * model * (3 + 6 * chunks),
        bytes_accessed=2 * model * model * (4 * chunks + 8),
        transcendentals=rows * model * chunks,
    )
    share = pieces // groups
    half = jax.ShapeDtypeStruct((groups, share // 2, packed.shape[1], model), bf16)
    return pl.pallas_call(
        lambda *refs: middle_kernel(groups, chunks, *refs),
        grid=(2 * chunks,),
        in_specs=[
            pl.BlockSpec(memory_space=pltpu.SMEM),
            fixed2((rows, model)),
            fixed2((rows, model)),
            fixed2((width, rows)),
            fixed2((width, rows)),
            fixed2((width, rows)),
            fixed2((width, rows)),
            pl.BlockSpec((pieces, own, model), lambda s: (0, 2 * chunks, 0), **once),
            pl.BlockSpec((pieces, own, model), lambda s: (0, chunks + back(s), 0)),
            pl.BlockSpec((pieces // chunks, chunks * own, model), lambda s: (back(s), 0, 0)),
            pl.BlockSpec((pieces, 8, model), lambda s: (0, vectors_at, 0), **once),
        ],
        out_specs=[
            fixed2((rows, model)),
            fixed2((rows, model)),
            fixed2((width, rows)),
            fixed2((width, rows)),
            fixed2((width, rows)),
            fixed2((width, rows)),
            pl.BlockSpec(memory_space=pl.ANY),
            pl.BlockSpec(memory_space=pl.ANY),
        ],
        out_shape=[
            jax.ShapeDtypeStruct((rows, model), bf16),
            jax.ShapeDtypeStruct((rows, model), f32),
            jax.ShapeDtypeStruct((width, rows), bf16),
            jax.ShapeDtypeStruct((width, rows), bf16),
            jax.ShapeDtypeStruct((width, rows), bf16),
            jax.ShapeDtypeStruct((width, rows), bf16),
            half,
            half,
        ],
        scratch_shapes=[
            pltpu.VMEM((rows, model), bf16),
            pltpu.VMEM((model, rows), bf16),
            pltpu.VMEM((rows, model), f32),
            pltpu.VMEM((rows, 128), f32),
            pltpu.VMEM((chunks, model, rows), bf16),
            pltpu.VMEM((chunks, rows, model), f32),
            pltpu.VMEM((rows, model), f32),
            pltpu.VMEM((rows, model), bf16),
            pltpu.VMEM((rows, model), bf16),
            pltpu.VMEM((16, model), f32),
            pltpu.VMEM((16, model), f32),
            pltpu.VMEM((2, 2, share // 2, chunks * own, model), bf16),
            pltpu.VMEM((2, 2, groups, share // 2, own, model), bf16),
            pltpu.VMEM((2, groups, share // 2, own, model), bf16),
            pltpu.VMEM((pieces, 8, model), f32),
            pltpu.VMEM((2, groups, share // 2, 8, model), bf16),
            pltpu.SemaphoreType.DMA((2, 2)),
            pltpu.SemaphoreType.DMA((2, 2)),
            pltpu.SemaphoreType.DMA((2,)),
            pltpu.SemaphoreType.DMA((2,)),
        ],
        cost_estimate=cost,
        compiler_params=pltpu.CompilerParams(vmem_limit_bytes=60 << 20),
        name="middle",
    )(place, x, cot, *mixed, packed, packed, packed, packed)


def by_sp(value, flip):
    groups = lax.axis_size("sp")
    return lax.ppermute(value, "sp", [(i, i ^ flip) for i in range(groups)])


def by_fsdp(value, flip):
    shards = lax.axis_size("fsdp")
    return lax.ppermute(value, "fsdp", [(i, i ^ flip) for i in range(shards)])


def scatter_rows(sent_x, sent_y, mine, low, up):
    half = low.shape[0]
    got_x, got_y = lax.optimization_barrier((by_sp(sent_x, 1), by_sp(sent_y, 2)))
    next_y = by_sp((up + got_x[half:].astype(f32)).astype(bf16), 2)
    next_x = by_sp((low + got_y[half:].astype(f32)).astype(bf16), 1)
    upper = got_x[:half].astype(f32) + next_y.astype(f32)
    lower = got_y[:half].astype(f32) + next_x.astype(f32)
    return mine + jnp.concatenate([upper, lower], 0)


def unpack(packed, ratio):
    pieces, _, model = packed.shape
    own = model // pieces
    at = ratio * own
    down = packed[:, :at].reshape(ratio * model, model)
    up = packed[:, at : 2 * at].reshape(pieces, ratio, own, model).transpose(1, 0, 2, 3)
    out = packed[:, 2 * at : 2 * at + own].reshape(model, model)
    vectors = [packed[:, 2 * at + own + j, :own].reshape(-1) for j in range(6)]
    vectors.append(packed[:, 2 * at + own + 6, :at].reshape(-1))
    return down, up.reshape(ratio, model, model), out, vectors


def repack(packed, ratio, pieces):
    if packed.shape[0] == pieces:
        return packed
    down, up, out, vectors = unpack(packed, ratio)
    model = out.shape[0]
    own = model // pieces
    up = up.reshape(ratio, pieces, own, model).transpose(1, 0, 2, 3)
    rows = [jnp.pad(v.reshape(pieces, -1), ((0, 0), (0, model - v.shape[0] // pieces))) for v in vectors]
    rows.append(jnp.zeros_like(rows[0]))
    return jnp.concatenate(
        [
            down.reshape(pieces, ratio * own, model),
            up.reshape(pieces, ratio * own, model),
            out.reshape(pieces, own, model),
            jnp.stack(rows, 1),
        ],
        1,
    )


def body(
    tokens,
    segments,
    cotangent,
    w_qkv,
    b_query,
    b_value,
    w_out,
    b_out,
    ln1_gain,
    ln1_bias,
    w_up,
    b_up,
    w_down,
    b_down,
    ln2_gain,
    ln2_bias,
):
    both = ("sp", "fsdp")
    groups = lax.axis_size("sp")
    shards = lax.axis_size("fsdp")
    devices = groups * shards
    rows, model = tokens.shape
    hidden = w_up.shape[1]
    ratio = hidden // model
    own = w_qkv.shape[0]
    pieces = devices if own % 8 == 0 else 8 * groups
    heads_local = HEADS // groups
    width = heads_local * HEAD
    seq_len = rows * groups
    seg_row = segments[0]

    me = lax.axis_index("sp").astype(jnp.int32).reshape(1)
    core = lax.rem(lax.axis_index("fsdp"), 2).astype(jnp.int32).reshape(1)
    direct = pieces == devices

    half = rows // 2
    vectors = [b_out, ln1_gain, ln1_bias, b_down, ln2_gain, ln2_bias, b_up]
    if direct:
        packed, mine = pack(me, w_down, w_up, w_out, w_qkv, vectors, b_query, b_value, groups)
        mine = jnp.stack([mine[0]] + [by_sp(mine[r], r) for r in range(1, groups)])
        mine, moved = lax.optimization_barrier((mine, tokens))
        along_x, along_y = by_sp(moved, 1), by_sp(moved, 2)
        near = jnp.stack([mine] + [by_fsdp(mine, 2 * z) for z in range(1, shards // 2)])
        sent, along_x, along_y = lax.optimization_barrier((near, along_x, along_y))
        away = by_fsdp(sent, 1)
        column = (lax.axis_index("fsdp").astype(jnp.int32) // 2).reshape(1)
        order = jnp.concatenate([me, me, column, core])
    else:
        packed, mine = pack_plain(w_down, w_up, w_out, w_qkv, vectors, b_query, b_value, groups)
        mine = jnp.broadcast_to(mine[:, None], (groups, shards) + mine.shape[1:])
        mine = mine.reshape(devices, own + 8, 3 * width)
        mine = lax.all_to_all(mine, both, split_axis=0, concat_axis=0, tiled=True)
        cut = model // pieces
        biases = lax.dynamic_slice(mine, (me[0] * shards, own, 0), (shards, 2, own))
        biases = biases.transpose(1, 0, 2).reshape(2, 8, cut).transpose(1, 0, 2)
        biases = jnp.pad(biases, ((0, 0), (0, 6), (0, 3 * width - cut)))
        mine = mine[:, :own].reshape(groups, 8, cut, 3 * width)
        mine = jnp.concatenate([mine, jnp.broadcast_to(biases[None], (groups, 8, 8, 3 * width))], 2)
        mine = mine.reshape(groups, 4, 2, cut + 8, 3 * width).transpose(2, 1, 0, 3, 4)
        near, away = mine[0], mine[1]
        order = jnp.concatenate([me, jnp.zeros((3,), jnp.int32)])
        along_x, along_y = by_sp(tokens, 1), by_sp(tokens, 2)
    blocks = tokens, along_x, along_y, by_sp(along_y[:half], 1), by_sp(along_x[half:], 2)
    packed_weights = repack(lax.all_gather(packed, both, axis=0, tiled=False), ratio, pieces)
    queries, keys, values, weights = project(
        order, blocks, seg_row, near, away, heads_local
    )
    forward_start, forward_number = windows(seg_row, FQ, FK, 128)
    backward_start, backward_number = windows(seg_row, BK, BQ, 128)
    *attended, logsum = attend_forward(
        queries, keys, values, forward_start, forward_number, me, heads_local
    )
    mixed = [attended[0]] + [by_sp(attended[r], r) for r in range(1, 4)]
    place = jnp.concatenate([core if direct else jnp.zeros_like(core), me])
    output, grad_h1, *grad_mixed, kept, sent = middle(place, tokens, cotangent, mixed, packed_weights)
    grad_heads = [grad_mixed[0]] + [by_sp(grad_mixed[r], r) for r in range(1, 4)]

    if not direct:
        halves = jnp.stack([kept, sent], 2).reshape(pieces, kept.shape[2], model)
        halves = repack(halves, ratio, devices).reshape(groups, shards // 2, 2, -1, model)
        kept = lax.dynamic_index_in_dim(halves, core[0], 2, keepdims=False)
        sent = lax.dynamic_index_in_dim(halves, 1 - core[0], 2, keepdims=False)
    partner = by_fsdp(sent, 1)
    total = (kept.astype(f32) + partner.astype(f32)).astype(bf16)
    total, grad_heads = lax.optimization_barrier((total, grad_heads))
    total = lax.psum_scatter(total.reshape(-1, model), "sp", scatter_dimension=0, tiled=True)
    *parts, turned = attend_backward(
        queries,
        keys,
        values,
        grad_heads,
        attended,
        logsum,
        backward_start,
        backward_number,
        me,
        weights,
        grad_h1,
        heads_local,
    )
    kept, sent = weight_gradient(order, turned, blocks, pieces)
    cores = [[2 * i + c for i in range(shards // 2)] for c in range(2)]
    reduced = lax.psum_scatter(
        total, "fsdp", scatter_dimension=0, tiled=True, axis_index_groups=cores
    )
    grad_input = scatter_rows(*parts)
    if direct:
        total = (kept.astype(f32) + by_fsdp(sent, 1).astype(f32)).astype(bf16)
        moved = [by_fsdp(total[z], 2 * z).astype(f32) for z in range(1, shards // 2)]
        total = sum(moved, total[0].astype(f32))
        by_head = [total[0]] + [by_sp(total[r], r) for r in range(1, groups)]
        weights = finish(order, by_head, reduced, ratio)
        vectors = [item.reshape(-1) for item in weights[4:]]
        owned_qkv, owned_down, owned_up, owned_out = weights[:4]
    else:
        cut = model // pieces
        halves = jnp.stack([kept, sent], 2).transpose(1, 0, 2, 3, 4).reshape(pieces, cut, model)
        biases = halves[:8, :2, model - 128 : model - 128 + cut]
        biases = biases.transpose(1, 0, 2).reshape(2, shards, own).transpose(1, 0, 2)
        biases = jnp.pad(biases, ((0, 0), (0, 6), (0, 3 * width - own)))
        halves = halves[:, :, : 3 * width].reshape(devices, own, 3 * width)
        halves = jnp.concatenate([halves, jnp.tile(biases, (groups, 1, 1))], 1)
        halves = lax.all_to_all(halves, both, split_axis=0, concat_axis=0, tiled=True)
        halves = jnp.sum(halves.reshape(groups, shards, own + 8, 3 * width).astype(f32), 1)
        bias_sums = lax.dynamic_slice(halves, (me[0], own, 0), (1, 2, own))[0]
        by_head = halves[:, :own].reshape(groups, own, 3, width).transpose(1, 2, 0, 3)
        owned_qkv = by_head.reshape(own, 3 * model)
        at = ratio * own
        reduced = reduced.astype(f32)
        owned_up = reduced[at : 2 * at].reshape(ratio, own, model).transpose(1, 0, 2)
        owned_up = owned_up.reshape(own, hidden)
        owned_down, owned_out = reduced[:at], reduced[2 * at : 2 * at + own]
        tail = reduced[2 * at + own :]
        vectors = [tail[i, :own] for i in range(6)] + [tail[6, :at], bias_sums[0], bias_sums[1]]
    return (
        output,
        grad_input,
        owned_qkv,
        vectors[7],
        vectors[8],
        owned_out,
        *vectors[:3],
        owned_up,
        vectors[6],
        owned_down,
        *vectors[3:6],
    )


def solution(mesh):
    in_specs = (
        P(("fsdp", "sp"), None),
        P("fsdp", None),
        P(("fsdp", "sp"), None),
        P(("sp", "fsdp"), None),
        P(("sp", "fsdp")),
        P(("sp", "fsdp")),
        P(("sp", "fsdp"), None),
        P(("sp", "fsdp")),
        P(("sp", "fsdp")),
        P(("sp", "fsdp")),
        P(("sp", "fsdp"), None),
        P(("sp", "fsdp")),
        P(("sp", "fsdp"), None),
        P(("sp", "fsdp")),
        P(("sp", "fsdp")),
        P(("sp", "fsdp")),
    )
    out_specs = (
        P(("fsdp", "sp"), None),
        P(("fsdp", "sp"), None),
        P(("sp", "fsdp"), None),
        P(("sp", "fsdp")),
        P(("sp", "fsdp")),
        P(("sp", "fsdp"), None),
        P(("sp", "fsdp")),
        P(("sp", "fsdp")),
        P(("sp", "fsdp")),
        P(("sp", "fsdp"), None),
        P(("sp", "fsdp")),
        P(("sp", "fsdp"), None),
        P(("sp", "fsdp")),
        P(("sp", "fsdp")),
        P(("sp", "fsdp")),
    )
    return jax.shard_map(body, mesh=mesh, in_specs=in_specs, out_specs=out_specs, check_vma=False)
```
